32 devices in a mesh: dp: 16 (over z, y, x), tensor: 2 (over core).
Axes of the slice: x: 2, y: 2, z: 4, core: 2. Of those that a mesh axis runs over, the one named last changes fastest.
Arguments:
- tokens_in: bfloat16 [16384, 768], P('dp'), may hold values from -6 to 6
- cotangent: bfloat16 [16384, 768], P('dp'), may hold values from -6 to 6
- seq_lengths: int32 [16, 4], P('dp'), may hold values from 1 to 512, 1024 in all within a row
- q_weight: bfloat16 [768, 768], P(None, 'tensor'), may hold values from -0.4375 to 0.4375
- k_weight: bfloat16 [768, 768], P(None, 'tensor'), may hold values from -0.21875 to 0.21875
- v_weight: bfloat16 [768, 768], P(None, 'tensor'), may hold values from -0.21875 to 0.21875
- q_bias: float32 [768], P('tensor'), may hold values from -3 to 3
- v_bias: float32 [768], P('tensor'), may hold values from -3 to 3
- out_weight: bfloat16 [768, 768], P('tensor'), may hold values from -1 to 1
- out_bias: float32 [768], replicated, may hold values from -3 to 3
- first_gain: float32 [768], replicated, may hold values from 0.5 to 1.5
- first_shift: float32 [768], replicated, may hold values from -2 to 2
- up_weight: bfloat16 [768, 3072], P(None, 'tensor'), may hold values from -0.21875 to 0.21875
- up_bias: float32 [3072], P('tensor'), may hold values from -3 to 3
- down_weight: bfloat16 [3072, 768], P('tensor'), may hold values from -0.15625 to 0.15625
- down_bias: float32 [768], replicated, may hold values from -3 to 3
- second_gain: float32 [768], replicated, may hold values from 0.5 to 1.5
- second_shift: float32 [768], replicated, may hold values from -2 to 2
Outputs:
- layer_out: bfloat16 [16384, 768], P('dp')
- grad_input: bfloat16 [16384, 768], P('dp')
- grad_q_weight: float32 [768, 768], P(None, 'tensor')
- grad_k_weight: float32 [768, 768], P(None, 'tensor')
- grad_v_weight: float32 [768, 768], P(None, 'tensor')
- grad_q_bias: float32 [768], P('tensor')
- grad_v_bias: float32 [768], P('tensor')
- grad_out_weight: float32 [768, 768], P('tensor')
- grad_out_bias: float32 [768], replicated
- grad_first_gain: float32 [768], replicated
- grad_first_shift: float32 [768], replicated
- grad_up_weight: float32 [768, 3072], P(None, 'tensor')
- grad_up_bias: float32 [3072], P('tensor')
- grad_down_weight: float32 [3072, 768], P('tensor')
- grad_down_bias: float32 [768], replicated
- grad_second_gain: float32 [768], replicated
- grad_second_shift: float32 [768], replicated
The draws below stay inside these ranges and needn't reach their ends.
Inputs may be any that keep to these rules, and one draw needn't show every extreme that they name: Each row of seq_lengths sums to 1024; in every row the longest sequence has exactly 512 tokens.
All inputs are finite; a program needn't handle non-finite values.
Results may differ from the reference program's by a relative error of at most 0.014.
The reference program's roundings to bfloat16 on the way count: a program that leaves them out, or rounds other values in their place, can miss the bound.
Values sent between devices are 32-bit elements; how exact they have to be, the bound alone decides.
No kernel may reach another device: no remote copies, remote signals or barrier semaphores. Data moves between devices by JAX's collectives and lax.ppermute only.
A program may use at most 192 MiB of HBM per device.

```python
import math
import jax
import jax.numpy as jnp
import numpy as np
from jax import lax

D = 768
H = 12
DH = 64
FF = 3072
SLOT = 1024
SEQS = 4
SLOTS = 16
ROWS = 16384


def shard_levels(stream_key, dims, shards, least, largest):
    def one(axis_at, shards_of):
        draws = jax.random.uniform(jax.random.fold_in(jax.random.fold_in(stream_key, 6), axis_at), (shards_of,), jnp.float32, least / len(shards), largest / len(shards))
        return jnp.repeat(jnp.exp(draws), dims[axis_at] // shards_of).reshape((-1,) + (1,) * (len(dims) - axis_at - 1))

    level = one(*shards[0])
    for cut in shards[1:]:
        level = level * one(*cut)
    return level


def split_up(number_of, total, limit, slope):
    weights = [(1 << 20) // math.isqrt(rank ** slope) + 1 for rank in range(2, number_of + 1)]
    rest, holding = total - limit - (number_of - 1), [1] * (number_of - 1)
    while rest > 0:
        movable = [i for i in range(number_of - 1) if holding[i] < limit]
        pool, left = sum([weights[i] for i in movable]), rest
        for i in movable:
            addition = min(limit - holding[i], max(1, left * weights[i] // pool), rest)
            holding[i] = holding[i] + addition
            rest = rest - addition
    return np.array([limit] + holding)


def ragged_sizes(stream_key, amount, total, bound, slope):
    if amount == 2:
        one = jax.random.randint(stream_key, (), max(1, total - bound), min(bound, total - 1) + 1)
        return jnp.stack([one, total - one])
    sizes = jnp.asarray(split_up(amount, total, bound, slope), jnp.int32)
    couples = (amount - 1) // 2
    donor, taker = sizes[1:1 + 2 * couples:2], sizes[2:2 + 2 * couples:2]
    room = jnp.minimum(donor - 1, bound - taker)
    shifted = jax.random.randint(jax.random.fold_in(stream_key, 1), (couples,), 0, 1 << 20) % (room + 1)
    sizes = sizes.at[1:1 + 2 * couples:2].set(donor - shifted).at[2:2 + 2 * couples:2].set(taker + shifted)
    return sizes[jax.random.permutation(jax.random.fold_in(stream_key, 2), amount)]


def gaussian(rng, extent, deviation, most, cuts=(), kind=jnp.bfloat16):
    array = deviation * jax.random.normal(rng, extent, jnp.float32)
    if cuts:
        array = array * shard_levels(rng, extent, cuts, -0.22, 0.18)
    return jnp.clip(array, -most, most).astype(kind)


def setup_inputs(seed: int = 0) -> dict:
    key_of = jax.random.split(jax.random.key(seed), 19)
    tokens_in = gaussian(key_of[0], (ROWS, D), 1.0, 6.0, ((0, 16),))
    cotangent = gaussian(key_of[1], (ROWS, D), 1.0, 6.0, ((0, 16),))
    seq_lengths = jax.vmap(lambda own: ragged_sizes(own, SEQS, SLOT, SLOT // 2, 2))(jax.random.split(key_of[2], SLOTS)).reshape((SLOTS, SEQS)).astype(jnp.int32)
    q_weight = gaussian(key_of[3], (D, H * DH), (D // 4) ** -0.5, 0.4375, ((1, 2),))
    k_weight = gaussian(key_of[4], (D, H * DH), D ** -0.5, 0.21875, ((1, 2),))
    v_weight = gaussian(key_of[5], (D, H * DH), D ** -0.5, 0.21875, ((1, 2),))
    q_bias = gaussian(key_of[6], (H * DH,), 0.5, 3.0, ((0, 2),), jnp.float32)
    v_bias = gaussian(key_of[7], (H * DH,), 0.5, 3.0, ((0, 2),), jnp.float32)
    out_weight = gaussian(key_of[8], (H * DH, D), (max(H * DH // 24, 2)) ** -0.5, 1.0, ((0, 2),))
    out_bias = gaussian(key_of[9], (D,), 0.5, 3.0, (), jnp.float32)
    first_gain = jnp.clip(1.0 + 0.1 * jax.random.normal(key_of[10], (D,), jnp.float32), 0.5, 1.5)
    first_shift = gaussian(key_of[11], (D,), 0.3, 2.0, (), jnp.float32)
    up_weight = gaussian(key_of[12], (D, FF), D ** -0.5, 0.21875, ((1, 2),))
    up_bias = gaussian(key_of[13], (FF,), 0.5, 3.0, ((0, 2),), jnp.float32)
    down_weight = gaussian(key_of[14], (FF, D), (FF // 2) ** -0.5, 0.15625, ((0, 2),))
    down_bias = gaussian(key_of[15], (D,), 0.5, 3.0, (), jnp.float32)
    second_gain = jnp.clip(1.0 + 0.1 * jax.random.normal(key_of[16], (D,), jnp.float32), 0.5, 1.5)
    second_shift = gaussian(key_of[17], (D,), 0.3, 2.0, (), jnp.float32)
    return dict(tokens_in=tokens_in, cotangent=cotangent, seq_lengths=seq_lengths, q_weight=q_weight, k_weight=k_weight, v_weight=v_weight, q_bias=q_bias, v_bias=v_bias, out_weight=out_weight, out_bias=out_bias, first_gain=first_gain, first_shift=first_shift, up_weight=up_weight, up_bias=up_bias, down_weight=down_weight, down_bias=down_bias, second_gain=second_gain, second_shift=second_shift)


@jax.custom_vjp
def low(v):
    return lax.optimization_barrier(v.astype(jnp.bfloat16)).astype(jnp.float32)

@jax.custom_vjp
def low_back(v):
    return v

def low_keep(v):
    return (low(v), None)

def low_pass(kept, grad):
    return (grad,)

def back_keep(v):
    return (v, None)

def back_low(kept, grad):
    return (low(grad),)
low.defvjp(low_keep, low_pass)
low_back.defvjp(back_keep, back_low)
score_scale = 0.125
norm_eps = 1e-05
far_negative = -1e+30

def matmul(left_side, right_side):
    return jnp.dot(left_side, right_side, precision=lax.Precision.HIGHEST)

def normalize(values, norm_gain, norm_shift):
    centre = values - lax.optimization_barrier(jnp.mean(values, axis=-1, keepdims=True))
    spread = lax.optimization_barrier(jnp.mean(centre * centre, axis=-1, keepdims=True))
    return centre * lax.rsqrt(spread + norm_eps) * norm_gain + norm_shift

def same_sequence(lengths_row, row_count):
    seq_ends = jnp.cumsum(lengths_row)
    positions = jnp.arange(row_count, dtype=jnp.int32)
    seq_labels = lax.optimization_barrier(jnp.sum((positions[:, None] >= seq_ends[None, :]).astype(jnp.int32), axis=1))
    return seq_labels[:, None] == seq_labels[None, :]

def attend(pieces):
    queries, key_rows, value_rows, lengths_row = pieces
    same_seq = same_sequence(lengths_row, queries.shape[0])
    raw_scores = low_back(jnp.einsum('qhd,khd->hqk', queries, key_rows, precision=lax.Precision.HIGHEST))
    scores = jnp.where(same_seq[None], raw_scores * score_scale, far_negative)
    attn_probs = low(jax.nn.softmax(scores, axis=-1))
    return jnp.einsum('hqk,khd->qhd', attn_probs, value_rows, precision=lax.Precision.HIGHEST)

def layer(tokens_in, q_weight, k_weight, v_weight, q_bias, v_bias, out_weight, out_bias, first_gain, first_shift, up_weight, up_bias, down_weight, down_bias, second_gain, second_shift, seq_lengths):
    queries = low_back(low(matmul(tokens_in, q_weight) + q_bias)).reshape(SLOTS, SLOT, H, DH)
    key_rows = low_back(low(matmul(tokens_in, k_weight))).reshape(SLOTS, SLOT, H, DH)
    value_rows = low_back(low(matmul(tokens_in, v_weight) + v_bias)).reshape(SLOTS, SLOT, H, DH)
    context = lax.map(jax.checkpoint(attend), (queries, key_rows, value_rows, seq_lengths))
    context = low_back(low(context.reshape(ROWS, H * DH)))
    attn_out = low_back(matmul(context, out_weight)) + out_bias
    first_norm = normalize(tokens_in + attn_out, first_gain, first_shift)
    ffn_inner = low_back(matmul(low(first_norm), up_weight) + up_bias)
    ffn_active = low(jax.nn.gelu(ffn_inner, approximate=False))
    down_out = low_back(matmul(ffn_active, down_weight)) + down_bias
    return normalize(first_norm + down_out, second_gain, second_shift)

def reference(tokens_in, cotangent, seq_lengths, q_weight, k_weight, v_weight, q_bias, v_bias, out_weight, out_bias, first_gain, first_shift, up_weight, up_bias, down_weight, down_bias, second_gain, second_shift):
    floats = [member.astype(jnp.float32) for member in (tokens_in, q_weight, k_weight, v_weight, q_bias, v_bias, out_weight, out_bias, first_gain, first_shift, up_weight, up_bias, down_weight, down_bias, second_gain, second_shift)]

    def layer_of(*params):
        return layer(*params, seq_lengths)
    result, pullback = jax.vjp(layer_of, *floats)
    grads = pullback(cotangent.astype(jnp.float32))
    return (result.astype(jnp.bfloat16), grads[0].astype(jnp.bfloat16), grads[1], grads[2], grads[3], grads[4], grads[5], grads[6], grads[7], grads[8], grads[9], grads[10], grads[11], grads[12], grads[13], grads[14], grads[15])
```

```python
import jax
import jax.numpy as jnp
from jax import lax
from jax.sharding import PartitionSpec as P

DH = 64


score_scale = 0.125
norm_eps = 1e-05
far_negative = -1e30


def normalize(values, norm_gain, norm_shift):
    centre = values - jnp.mean(values, axis=-1, keepdims=True)
    spread = jnp.mean(centre * centre, axis=-1, keepdims=True)
    return centre * lax.rsqrt(spread + norm_eps) * norm_gain + norm_shift


def gelu_exact(values):
    return jax.nn.gelu(values, approximate=False)


def contract_rows(left_side, right_side):
    return lax.dot_general(
        left_side, right_side, (((0,), (0,)), ((), ())), preferred_element_type=jnp.float32
    )


def times_transposed(left_side, right_side):
    return lax.dot_general(
        left_side, right_side, (((1,), (1,)), ((), ())), preferred_element_type=jnp.float32
    )


def same_sequence(lengths_row, row_count):
    positions = jnp.arange(row_count, dtype=jnp.int32)
    seq_labels = jnp.zeros((row_count,), jnp.int32)
    seq_end = jnp.int32(0)
    for at in range(lengths_row.shape[0]):
        seq_end = seq_end + lengths_row[at]
        seq_labels = seq_labels + (positions >= seq_end).astype(jnp.int32)
    return seq_labels[:, None] == seq_labels[None, :]


def masked_scores(queries, key_rows, same_seq):
    scores = (
        jnp.einsum("qhd,khd->hqk", queries, key_rows, preferred_element_type=jnp.float32)
        * score_scale
    )
    return jnp.where(same_seq[None], scores, far_negative)


def pair_sum(value, tensor_count):
    if tensor_count == 1:
        return value
    if tensor_count != 2:
        return lax.psum(value, "tensor")
    return value + lax.ppermute(value, "tensor", [(0, 1), (1, 0)])


def swap_bit(value, bit, count):
    return lax.ppermute(value, "dp", [(i, i ^ (1 << bit)) for i in range(count)])


def halve(value, bit, count, place):
    rows = value.shape[0] // 2
    mine = (place >> bit) & 1
    sent = lax.dynamic_slice_in_dim(value, (1 - mine) * rows, rows, 0)
    kept = lax.dynamic_slice_in_dim(value, mine * rows, rows, 0)
    return kept + swap_bit(sent, bit, count)


def join(value, bit, count, place):
    other = swap_bit(value, bit, count)
    mine = (place >> bit) & 1
    first = jnp.where(mine == 0, value, other)
    second = jnp.where(mine == 0, other, value)
    return jnp.concatenate([first, second], axis=0)


def line_sum(value, count, place):
    stride = count // 4
    inward = []
    across = []
    outward = []
    for low in range(stride):
        ring = [low + stride * at for at in range(4)]
        inward += [(ring[0], ring[1]), (ring[3], ring[2])]
        across += [(ring[1], ring[2]), (ring[2], ring[1])]
        outward += [(ring[1], ring[0]), (ring[2], ring[3])]
    at_line = place // stride
    value = value + lax.ppermute(value, "dp", inward)
    value = value + lax.ppermute(value, "dp", across)
    ended = lax.ppermute(value, "dp", outward)
    return jnp.where((at_line == 1) | (at_line == 2), value, ended)


def all_sum(value, first_bit, count, place):
    second_bit = 1 - first_bit
    value = halve(value, first_bit, count, place)
    value = halve(value, second_bit, count, place)
    low_bits = (count // 4).bit_length() - 1
    for bit in range(2, low_bits):
        value = value + swap_bit(value, bit, count)
    value = line_sum(value, count, place)
    value = join(value, second_bit, count, place)
    return join(value, first_bit, count, place)


def local(
    dp_count,
    tensor_count,
    tokens_in,
    cotangent,
    seq_lengths,
    q_weight,
    k_weight,
    v_weight,
    q_bias,
    v_bias,
    out_weight,
    out_bias,
    first_gain,
    first_shift,
    up_weight,
    up_bias,
    down_weight,
    down_bias,
    second_gain,
    second_shift,
):
    place = lax.axis_index("dp")
    row_count = tokens_in.shape[0]
    width = q_weight.shape[1]
    model = q_weight.shape[0]
    hidden = up_weight.shape[1]
    heads_here = width // DH
    same_seq = same_sequence(seq_lengths[0], row_count)
    queries = (jnp.dot(tokens_in, q_weight, preferred_element_type=jnp.float32) + q_bias).astype(
        jnp.bfloat16
    )
    key_rows = jnp.dot(tokens_in, k_weight, preferred_element_type=jnp.float32).astype(jnp.bfloat16)
    value_rows = (jnp.dot(tokens_in, v_weight, preferred_element_type=jnp.float32) + v_bias).astype(
        jnp.bfloat16
    )
    queries = queries.reshape(row_count, heads_here, DH)
    key_rows = key_rows.reshape(row_count, heads_here, DH)
    value_rows = value_rows.reshape(row_count, heads_here, DH)
    scores = masked_scores(queries, key_rows, same_seq)
    row_peak = jnp.max(scores, axis=-1, keepdims=True)
    exponents = jnp.exp(scores - row_peak)
    row_total = jnp.sum(exponents, axis=-1, keepdims=True)
    log_total = row_peak + jnp.log(row_total)
    probs_low = (exponents / row_total).astype(jnp.bfloat16)
    context = jnp.einsum("hqk,khd->qhd", probs_low, value_rows, preferred_element_type=jnp.float32)
    context = context.astype(jnp.bfloat16).reshape(row_count, heads_here * DH)
    attn_out = pair_sum(
        jnp.dot(context, out_weight, preferred_element_type=jnp.float32), tensor_count
    )
    first_sum = tokens_in.astype(jnp.float32) + attn_out + out_bias
    first_norm = normalize(first_sum, first_gain, first_shift)
    first_low = first_norm.astype(jnp.bfloat16)
    ffn_inner = jnp.dot(first_low, up_weight, preferred_element_type=jnp.float32) + up_bias
    ffn_active = gelu_exact(ffn_inner).astype(jnp.bfloat16)
    down_out = pair_sum(
        jnp.dot(ffn_active, down_weight, preferred_element_type=jnp.float32), tensor_count
    )
    second_sum = first_norm + down_out + down_bias
    layer_out = normalize(second_sum, second_gain, second_shift).astype(jnp.bfloat16)
    unused, pull_second = jax.vjp(normalize, second_sum, second_gain, second_shift)
    back_second, grad_second_gain, grad_second_shift = pull_second(cotangent.astype(jnp.float32))
    back_down = back_second.astype(jnp.bfloat16)
    grad_down_bias = jnp.sum(back_second, axis=0)
    half = hidden // 2
    down_sums = [
        all_sum(contract_rows(ffn_active[:, at : at + half], back_down), bit, dp_count, place)
        for bit, at in enumerate((0, half))
    ]
    back_active = times_transposed(back_down, down_weight)
    unused_inner, pull_gelu = jax.vjp(gelu_exact, ffn_inner)
    back_inner = pull_gelu(back_active)[0].astype(jnp.bfloat16)
    grad_up_bias = jnp.sum(back_inner.astype(jnp.float32), axis=0)
    up_sums = [
        all_sum(contract_rows(first_low, back_inner[:, at : at + half]), bit, dp_count, place)
        for bit, at in enumerate((0, half))
    ]
    back_first = pair_sum(times_transposed(back_inner, up_weight), tensor_count) + back_second
    unused_first, pull_first = jax.vjp(normalize, first_sum, first_gain, first_shift)
    back_first_sum, grad_first_gain, grad_first_shift = pull_first(back_first)
    back_attn = back_first_sum.astype(jnp.bfloat16)
    grad_out_bias = jnp.sum(back_first_sum, axis=0)
    grad_out_turned = contract_rows(back_attn, context)
    back_context = (
        times_transposed(back_attn, out_weight)
        .astype(jnp.bfloat16)
        .reshape(row_count, heads_here, DH)
    )
    probs_exact = jnp.exp(masked_scores(queries, key_rows, same_seq) - log_total)
    probs_again = probs_exact.astype(jnp.bfloat16)
    back_values = jnp.einsum(
        "hqk,qhd->khd", probs_again, back_context, preferred_element_type=jnp.float32
    )
    back_probs = jnp.einsum(
        "qhd,khd->hqk", back_context, value_rows, preferred_element_type=jnp.float32
    )
    row_inner = jnp.sum(back_probs * probs_exact, axis=-1, keepdims=True)
    back_scores = (probs_exact * (back_probs - row_inner) * score_scale).astype(jnp.bfloat16)
    back_queries = jnp.einsum(
        "hqk,khd->qhd", back_scores, key_rows, preferred_element_type=jnp.float32
    )
    back_keys = jnp.einsum("hqk,qhd->khd", back_scores, queries, preferred_element_type=jnp.float32)
    back_queries = back_queries.astype(jnp.bfloat16).reshape(row_count, heads_here * DH)
    back_keys = back_keys.astype(jnp.bfloat16).reshape(row_count, heads_here * DH)
    back_values = back_values.astype(jnp.bfloat16).reshape(row_count, heads_here * DH)
    grad_q_bias = jnp.sum(back_queries.astype(jnp.float32), axis=0)
    grad_v_bias = jnp.sum(back_values.astype(jnp.float32), axis=0)
    small = [
        grad_q_bias,
        grad_v_bias,
        grad_up_bias,
        grad_out_bias,
        grad_first_gain,
        grad_first_shift,
        grad_down_bias,
        grad_second_gain,
        grad_second_shift,
    ]
    sizes = [member.shape[0] for member in small]
    small_rows = -(-sum(sizes) // (32 * model)) * 32
    packed = jnp.concatenate(small + [jnp.zeros((small_rows * model - sum(sizes),), jnp.float32)])
    first_pack = jnp.concatenate(
        [contract_rows(tokens_in, back_queries), contract_rows(tokens_in, back_keys)], axis=1
    )
    second_pack = jnp.concatenate(
        [contract_rows(tokens_in, back_values), grad_out_turned], axis=1
    )
    second_pack = jnp.concatenate(
        [second_pack, packed.reshape(small_rows, model)], axis=0
    )
    first_pack = all_sum(first_pack, 0, dp_count, place)
    second_pack = all_sum(second_pack, 1, dp_count, place)
    partial_input = (
        times_transposed(back_queries, q_weight)
        + times_transposed(back_keys, k_weight)
        + times_transposed(back_values, v_weight)
    )
    grad_input = (pair_sum(partial_input, tensor_count) + back_first_sum).astype(jnp.bfloat16)
    flat = second_pack[model:].reshape(-1)
    sums = []
    start = 0
    for size in sizes:
        sums.append(flat[start : start + size])
        start += size
    return (
        layer_out,
        grad_input,
        first_pack[:, :width],
        first_pack[:, width:],
        second_pack[:model, :width],
        sums[0],
        sums[1],
        second_pack[:model, width:].T,
        sums[3],
        sums[4],
        sums[5],
        jnp.concatenate(up_sums, axis=1),
        sums[2],
        jnp.concatenate(down_sums, axis=0),
        sums[6],
        sums[7],
        sums[8],
    )


def solution(mesh):
    placed = (
        P("dp", None),
        P("dp", None),
        P("dp", None),
        P(None, "tensor"),
        P(None, "tensor"),
        P(None, "tensor"),
        P("tensor"),
        P("tensor"),
        P("tensor", None),
        P(),
        P(),
        P(),
        P(None, "tensor"),
        P("tensor"),
        P("tensor", None),
        P(),
        P(),
        P(),
    )
    counts = (mesh.shape["dp"], mesh.shape["tensor"])

    def on_device(*args):
        return local(*counts, *args)

    return jax.shard_map(
        on_device,
        mesh=mesh,
        in_specs=placed,
        out_specs=(
            P("dp", None),
            P("dp", None),
            P(None, "tensor"),
            P(None, "tensor"),
            P(None, "tensor"),
            P("tensor"),
            P("tensor"),
            P("tensor", None),
            P(),
            P(),
            P(),
            P(None, "tensor"),
            P("tensor"),
            P("tensor", None),
            P(),
            P(),
            P(),
        ),
        check_vma=False,
    )
```

```python
import functools

import jax
import jax.numpy as jnp
from jax import lax
from jax.experimental import pallas as pl
from jax.experimental.pallas import tpu as pltpu
from jax.sharding import PartitionSpec as P

DH = 64
LANES = 128
ROW_BLOCK = 256
MIB = 1 << 20

score_scale = 0.125
norm_eps = 1e-05
far_negative = -1e30
log2_e = 1.4426950408889634


def contract(left_side, right_side, left_dim, right_dim):
    return lax.dot_general(
        left_side,
        right_side,
        (((left_dim,), (right_dim,)), ((), ())),
        preferred_element_type=jnp.float32,
    )


def sequence_ends(lengths_ref, count):
    ends = []
    total = jnp.int32(0)
    for at in range(count):
        total = total + lengths_ref[0, at]
        ends.append(total)
    return ends


def key_window(ends, first_row, rows):
    last_row = first_row + LANES - 1
    start = jnp.int32(0)
    stop = jnp.int32(rows)
    for end in ends:
        start = jnp.where(end <= first_row, jnp.maximum(start, end), start)
        stop = jnp.where(end > last_row, jnp.minimum(stop, end), stop)
    start = (start // LANES) * LANES
    stop = ((stop + LANES - 1) // LANES) * LANES
    return start, stop


def window_bias(ends, first_row, key_start, width):
    query_at = lax.broadcasted_iota(jnp.int32, (1, LANES), 1) + first_row
    seq_start = jnp.zeros((1, LANES), jnp.int32)
    seq_stop = jnp.full((1, LANES), 1 << 30, jnp.int32)
    for end in ends:
        seq_start = jnp.where(query_at >= end, jnp.maximum(seq_start, end), seq_start)
        seq_stop = jnp.where(query_at < end, jnp.minimum(seq_stop, end), seq_stop)
    key_at = lax.broadcasted_iota(jnp.int32, (width, LANES), 0) + key_start
    seen = (key_at >= seq_start) & (key_at < seq_stop)
    bias = jnp.where(seen, 0.0, far_negative).astype(jnp.float32)
    return jnp.concatenate([bias, bias], axis=1)


def split_heads(block):
    lane = lax.broadcasted_iota(jnp.int32, block.shape, 1)
    wide = block.astype(jnp.float32)
    return jnp.concatenate(
        [jnp.where(lane < DH, wide, 0.0), jnp.where(lane < DH, 0.0, wide)], axis=0
    ).astype(jnp.bfloat16)


def merge_heads(turned):
    return jnp.concatenate([turned[:DH, :LANES], turned[DH:, LANES:]], axis=0).T


def over_query_blocks(ends, rows, widths, body):
    @pl.loop(0, rows // LANES)
    def _(block):
        first_row = pl.multiple_of(block * LANES, LANES)
        start, stop = key_window(ends, first_row, rows)
        span = stop - start
        lower = 0
        for width in widths:
            chosen = (span > lower) & (span <= width)
            key_start = pl.multiple_of(jnp.minimum(start, rows - width), LANES)
            pl.when(chosen)(functools.partial(body, block, first_row, key_start, width))
            lower = width


def attend_kernel(
    widths,
    seqs,
    lengths_ref,
    tokens_ref,
    q_weight_ref,
    k_weight_ref,
    v_weight_ref,
    q_bias_ref,
    v_bias_ref,
    out_weight_ref,
    queries_ref,
    keys_ref,
    values_ref,
    context_ref,
    total_ref,
    attn_out_ref,
    turned_ref,
):
    rows = tokens_ref.shape[0]
    pairs = q_weight_ref.shape[1] // LANES
    tokens = tokens_ref[...]
    queries_ref[...] = (contract(tokens, q_weight_ref[...], 1, 0) + q_bias_ref[...]).astype(
        jnp.bfloat16
    )
    keys_ref[...] = contract(tokens, k_weight_ref[...], 1, 0).astype(jnp.bfloat16)
    values = contract(tokens, v_weight_ref[...], 1, 0) + v_bias_ref[...]
    values_ref[...] = values.astype(jnp.bfloat16)
    turned_ref[...] = values.T.astype(jnp.bfloat16)
    ends = sequence_ends(lengths_ref, seqs)

    def body(block, first_row, key_start, width):
        bias = window_bias(ends, first_row, key_start, width)
        for pair in range(pairs):
            lanes = slice(pair * LANES, (pair + 1) * LANES)
            both = split_heads(queries_ref[pl.ds(first_row, LANES), lanes])
            keys = keys_ref[pl.ds(key_start, width), lanes]
            scores = contract(keys, both, 1, 1) * (score_scale * log2_e) + bias
            peak = jnp.max(scores, axis=0, keepdims=True)
            exponents = jnp.exp2(scores - peak)
            total = jnp.sum(exponents, axis=0, keepdims=True)
            total_ref[pl.ds(block * pairs + pair, 1), :] = peak + jnp.log2(total)
            probs = (exponents * (1.0 / total)).astype(jnp.bfloat16)
            turned = contract(turned_ref[lanes, pl.ds(key_start, width)], probs, 1, 0)
            context_ref[pl.ds(first_row, LANES), lanes] = merge_heads(turned).astype(jnp.bfloat16)

    over_query_blocks(ends, rows, widths, body)
    attn_out_ref[...] = contract(context_ref[...], out_weight_ref[...], 1, 0)


def attend_back_kernel(
    widths,
    seqs,
    lengths_ref,
    back_attn_ref,
    out_weight_ref,
    queries_ref,
    keys_ref,
    values_ref,
    total_ref,
    tokens_ref,
    context_ref,
    q_weight_ref,
    k_weight_ref,
    v_weight_ref,
    small_ref,
    first_pack_ref,
    second_pack_ref,
    partial_ref,
    back_context_ref,
    turned_ref,
    back_queries_ref,
    back_keys_ref,
    back_values_ref,
):
    rows = tokens_ref.shape[0]
    width_here = q_weight_ref.shape[1]
    pairs = width_here // LANES
    back_context_ref[...] = contract(back_attn_ref[...], out_weight_ref[...], 1, 1).astype(
        jnp.bfloat16
    )
    turned_ref[...] = keys_ref[...].astype(jnp.float32).T.astype(jnp.bfloat16)
    back_keys_ref[...] = jnp.zeros_like(back_keys_ref)
    back_values_ref[...] = jnp.zeros_like(back_values_ref)
    ends = sequence_ends(lengths_ref, seqs)

    def body(block, first_row, key_start, width):
        bias = window_bias(ends, first_row, key_start, width)
        for pair in range(pairs):
            lanes = slice(pair * LANES, (pair + 1) * LANES)
            both = split_heads(queries_ref[pl.ds(first_row, LANES), lanes])
            back_both = split_heads(back_context_ref[pl.ds(first_row, LANES), lanes])
            keys = keys_ref[pl.ds(key_start, width), lanes]
            values = values_ref[pl.ds(key_start, width), lanes]
            scores = contract(keys, both, 1, 1) * (score_scale * log2_e) + bias
            probs = jnp.exp2(scores - total_ref[pl.ds(block * pairs + pair, 1), :])
            back_probs = contract(values, back_both, 1, 1)
            inner = jnp.sum(back_probs * probs, axis=0, keepdims=True)
            back_scores = (probs * (back_probs - inner) * score_scale).astype(jnp.bfloat16)
            back_values_ref[pl.ds(key_start, width), lanes] += contract(
                probs.astype(jnp.bfloat16), back_both, 1, 0
            )
            back_keys_ref[pl.ds(key_start, width), lanes] += contract(back_scores, both, 1, 0)
            turned = contract(turned_ref[lanes, pl.ds(key_start, width)], back_scores, 1, 0)
            back_queries_ref[pl.ds(first_row, LANES), lanes] = merge_heads(turned).astype(
                jnp.bfloat16
            )

    over_query_blocks(ends, rows, widths, body)
    model = tokens_ref.shape[1]
    tokens = tokens_ref[...]
    back_queries = back_queries_ref[...]
    back_keys = back_keys_ref[...].astype(jnp.bfloat16)
    back_values = back_values_ref[...].astype(jnp.bfloat16)
    first_pack_ref[:, :width_here] = contract(tokens, back_queries, 0, 0)
    first_pack_ref[:, width_here:] = contract(tokens, back_keys, 0, 0)
    grad_values = contract(tokens, back_values, 0, 0)
    second_pack_ref[:width_here, :] = contract(context_ref[...], back_attn_ref[...], 0, 0)
    half = model // 2
    second_pack_ref[width_here : width_here + half, :width_here] = grad_values[:half]
    second_pack_ref[width_here : width_here + half, width_here:] = grad_values[half:]
    second_pack_ref[width_here + half :, :] = small_ref[...]
    top = width_here + half
    second_pack_ref[top : top + 1, :width_here] = jnp.sum(
        back_queries.astype(jnp.float32), axis=0, keepdims=True
    )
    second_pack_ref[top : top + 1, width_here:] = jnp.sum(
        back_values.astype(jnp.float32), axis=0, keepdims=True
    )
    partial_ref[...] = (
        contract(back_queries, q_weight_ref[...], 1, 1)
        + contract(back_keys, k_weight_ref[...], 1, 1)
        + contract(back_values, v_weight_ref[...], 1, 1)
    )


def row_mean(values):
    return jnp.mean(values, axis=-1, keepdims=True)


def standardize(values):
    centre = values - row_mean(values)
    rate = lax.rsqrt(row_mean(centre * centre) + norm_eps)
    return centre * rate, rate


def norm_back(upstream, unit, rate, gain):
    scaled = upstream * gain
    return rate * (scaled - row_mean(scaled) - unit * row_mean(scaled * unit))


def add_sums(sums_ref, members):
    @pl.when(pl.program_id(0) == 0)
    def _():
        sums_ref[...] = jnp.zeros_like(sums_ref)

    for at, member in enumerate(members):
        sums_ref[at : at + 1, :] += jnp.sum(member, axis=0, keepdims=True)


def feed_kernel(
    tokens_ref,
    own_ref,
    other_ref,
    out_bias_ref,
    gain_ref,
    shift_ref,
    up_weight_ref,
    up_bias_ref,
    down_weight_ref,
    first_sum_ref,
    first_low_ref,
    inner_ref,
    active_ref,
    partial_ref,
):
    first_sum = (
        tokens_ref[...].astype(jnp.float32) + (own_ref[...] + other_ref[...]) + out_bias_ref[...]
    )
    first_sum_ref[...] = first_sum
    unit, unused = standardize(first_sum)
    first_low = (unit * gain_ref[...] + shift_ref[...]).astype(jnp.bfloat16)
    first_low_ref[...] = first_low
    inner = contract(first_low, up_weight_ref[...], 1, 0) + up_bias_ref[...]
    inner_ref[...] = inner
    active = (inner * (0.5 * (1.0 + lax.erf(inner * 0.7071067811865476)))).astype(jnp.bfloat16)
    active_ref[...] = active
    partial_ref[...] = contract(active, down_weight_ref[...], 1, 0)


def second_norm_kernel(
    first_sum_ref,
    own_ref,
    other_ref,
    cotangent_ref,
    active_ref,
    first_gain_ref,
    first_shift_ref,
    down_bias_ref,
    gain_ref,
    shift_ref,
    layer_out_ref,
    back_second_ref,
    back_down_ref,
    grad_low_ref,
    grad_high_ref,
    sums_ref,
):
    unit, unused = standardize(first_sum_ref[...])
    first = unit * first_gain_ref[...] + first_shift_ref[...]
    second_sum = first + (own_ref[...] + other_ref[...]) + down_bias_ref[...]
    unit, rate = standardize(second_sum)
    layer_out_ref[...] = (unit * gain_ref[...] + shift_ref[...]).astype(jnp.bfloat16)
    upstream = cotangent_ref[...].astype(jnp.float32)
    back_second = norm_back(upstream, unit, rate, gain_ref[...])
    back_second_ref[...] = back_second
    back_down = back_second.astype(jnp.bfloat16)
    back_down_ref[...] = back_down
    half = grad_low_ref.shape[0]

    @pl.when(pl.program_id(0) == 0)
    def _():
        grad_low_ref[...] = jnp.zeros_like(grad_low_ref)
        grad_high_ref[...] = jnp.zeros_like(grad_high_ref)

    grad_low_ref[...] += contract(active_ref[:, :half], back_down, 0, 0)
    grad_high_ref[...] += contract(active_ref[:, half:], back_down, 0, 0)
    add_sums(sums_ref, (back_second, upstream * unit, upstream))


def feed_back_kernel(
    back_down_ref,
    inner_ref,
    first_low_ref,
    down_weight_ref,
    up_weight_ref,
    partial_ref,
    grad_low_ref,
    grad_high_ref,
    sums_ref,
):
    inner = inner_ref[...]
    slope = 0.5 * (1.0 + lax.erf(inner * 0.7071067811865476)) + inner * (
        0.3989422804014327 * jnp.exp(-0.5 * inner * inner)
    )
    back_active = contract(back_down_ref[...], down_weight_ref[...], 1, 1)
    back_inner = (back_active * slope).astype(jnp.bfloat16)
    partial_ref[...] = contract(back_inner, up_weight_ref[...], 1, 1)
    half = grad_low_ref.shape[1]

    @pl.when(pl.program_id(0) == 0)
    def _():
        grad_low_ref[...] = jnp.zeros_like(grad_low_ref)
        grad_high_ref[...] = jnp.zeros_like(grad_high_ref)

    first_low = first_low_ref[...]
    grad_low_ref[...] += contract(first_low, back_inner[:, :half], 0, 0)
    grad_high_ref[...] += contract(first_low, back_inner[:, half:], 0, 0)
    add_sums(sums_ref, (back_inner.astype(jnp.float32),))


def first_norm_kernel(
    first_sum_ref,
    own_ref,
    other_ref,
    back_second_ref,
    gain_ref,
    back_first_sum_ref,
    back_attn_ref,
    sums_ref,
):
    unit, rate = standardize(first_sum_ref[...])
    upstream = (own_ref[...] + other_ref[...]) + back_second_ref[...]
    back_first_sum = norm_back(upstream, unit, rate, gain_ref[...])
    back_first_sum_ref[...] = back_first_sum
    back_attn_ref[...] = back_first_sum.astype(jnp.bfloat16)
    add_sums(sums_ref, (back_first_sum, upstream * unit, upstream))


def struct(shape, dtype):
    return jax.ShapeDtypeStruct(shape, dtype)


def by_rows(columns):
    return pl.BlockSpec((ROW_BLOCK, columns), lambda step: (step, 0))


def whole(shape):
    return pl.BlockSpec(shape, lambda *step: (0, 0))


def held(shape):
    return pl.BlockSpec(shape, lambda *step: (0, 0), pipeline_mode=pl.Buffered(1))


def in_smem():
    return pl.BlockSpec(memory_space=pltpu.SMEM)


def in_vmem():
    return pl.BlockSpec(memory_space=pltpu.VMEM)


def params(mebibytes):
    return pltpu.CompilerParams(vmem_limit_bytes=mebibytes * MIB)


def key_widths(rows):
    return tuple(width for width in (640,) if width < rows) + (rows,)


def attend(lengths, tokens, q_weight, k_weight, v_weight, q_bias, v_bias, out_weight):
    rows, model = tokens.shape
    width = q_weight.shape[1]
    totals = rows // LANES * (width // LANES)
    low = struct((rows, width), jnp.bfloat16)
    return pl.pallas_call(
        functools.partial(attend_kernel, key_widths(rows), lengths.shape[1]),
        out_shape=(
            low,
            low,
            low,
            low,
            struct((totals, 2 * LANES), jnp.float32),
            struct((rows, model), jnp.float32),
        ),
        in_specs=[in_smem()] + [in_vmem()] * 7,
        out_specs=(in_vmem(),) * 6,
        scratch_shapes=[pltpu.VMEM((width, rows), jnp.bfloat16)],
        compiler_params=params(40),
        name="attend",
    )(lengths, tokens, q_weight, k_weight, v_weight, q_bias, v_bias, out_weight)


def attend_back(
    lengths,
    back_attn,
    out_weight,
    queries,
    keys,
    values,
    totals,
    tokens,
    context,
    q_weight,
    k_weight,
    v_weight,
    small,
):
    rows, model = tokens.shape
    width = q_weight.shape[1]
    pack_rows = width + model // 2 + small.shape[0]
    return pl.pallas_call(
        functools.partial(attend_back_kernel, key_widths(rows), lengths.shape[1]),
        out_shape=(
            struct((model, 2 * width), jnp.float32),
            struct((pack_rows, model), jnp.float32),
            struct((rows, model), jnp.float32),
        ),
        in_specs=[in_smem()] + [in_vmem()] * 12,
        out_specs=(in_vmem(),) * 3,
        scratch_shapes=[
            pltpu.VMEM((rows, width), jnp.bfloat16),
            pltpu.VMEM((width, rows), jnp.bfloat16),
            pltpu.VMEM((rows, width), jnp.bfloat16),
            pltpu.VMEM((rows, width), jnp.float32),
            pltpu.VMEM((rows, width), jnp.float32),
        ],
        compiler_params=params(44),
        name="attend_back",
    )(
        lengths,
        back_attn,
        out_weight,
        queries,
        keys,
        values,
        totals,
        tokens,
        context,
        q_weight,
        k_weight,
        v_weight,
        small,
    )


def feed(tokens, own, other, out_bias, gain, shift, up_weight, up_bias, down_weight):
    rows, model = tokens.shape
    hidden = up_weight.shape[1]
    return pl.pallas_call(
        feed_kernel,
        grid=(rows // ROW_BLOCK,),
        out_shape=(
            struct((rows, model), jnp.float32),
            struct((rows, model), jnp.bfloat16),
            struct((rows, hidden), jnp.float32),
            struct((rows, hidden), jnp.bfloat16),
            struct((rows, model), jnp.float32),
        ),
        in_specs=[by_rows(model)] * 3
        + [held((1, model))] * 3
        + [held((model, hidden)), held((1, hidden)), held((hidden, model))],
        out_specs=(
            by_rows(model),
            by_rows(model),
            by_rows(hidden),
            by_rows(hidden),
            by_rows(model),
        ),
        compiler_params=params(40),
        name="feed",
    )(tokens, own, other, out_bias, gain, shift, up_weight, up_bias, down_weight)


def second_norm(
    first_sum, own, other, cotangent, active, first_gain, first_shift, down_bias, gain, shift
):
    rows, model = first_sum.shape
    hidden = active.shape[1]
    return pl.pallas_call(
        second_norm_kernel,
        grid=(rows // ROW_BLOCK,),
        out_shape=(
            struct((rows, model), jnp.bfloat16),
            struct((rows, model), jnp.float32),
            struct((rows, model), jnp.bfloat16),
            struct((hidden // 2, model), jnp.float32),
            struct((hidden // 2, model), jnp.float32),
            struct((8, model), jnp.float32),
        ),
        in_specs=[by_rows(model)] * 4 + [by_rows(hidden)] + [held((1, model))] * 5,
        out_specs=(
            by_rows(model),
            by_rows(model),
            by_rows(model),
            whole((hidden // 2, model)),
            whole((hidden // 2, model)),
            whole((8, model)),
        ),
        compiler_params=params(40),
        name="second_norm",
    )(first_sum, own, other, cotangent, active, first_gain, first_shift, down_bias, gain, shift)


def feed_back(back_down, inner, first_low, down_weight, up_weight):
    rows, model = back_down.shape
    hidden = inner.shape[1]
    return pl.pallas_call(
        feed_back_kernel,
        grid=(rows // ROW_BLOCK,),
        out_shape=(
            struct((rows, model), jnp.float32),
            struct((model, hidden // 2), jnp.float32),
            struct((model, hidden // 2), jnp.float32),
            struct((8, hidden), jnp.float32),
        ),
        in_specs=[
            by_rows(model),
            by_rows(hidden),
            by_rows(model),
            held((hidden, model)),
            held((model, hidden)),
        ],
        out_specs=(
            by_rows(model),
            whole((model, hidden // 2)),
            whole((model, hidden // 2)),
            whole((8, hidden)),
        ),
        compiler_params=params(40),
        name="feed_back",
    )(back_down, inner, first_low, down_weight, up_weight)


def first_norm_back(first_sum, own, other, back_second, gain):
    rows, model = first_sum.shape
    return pl.pallas_call(
        first_norm_kernel,
        grid=(rows // ROW_BLOCK,),
        out_shape=(
            struct((rows, model), jnp.float32),
            struct((rows, model), jnp.bfloat16),
            struct((8, model), jnp.float32),
        ),
        in_specs=[by_rows(model)] * 4 + [held((1, model))],
        out_specs=(by_rows(model), by_rows(model), whole((8, model))),
        compiler_params=params(32),
        name="first_norm_back",
    )(first_sum, own, other, back_second, gain)


def swap_cores(value, tensor_count):
    return lax.ppermute(value, "tensor", [(i, i ^ 1) for i in range(tensor_count)])


def swap_bit(value, bit, count):
    return lax.ppermute(value, "dp", [(i, i ^ (1 << bit)) for i in range(count)])


def halve(value, bit, count, place):
    rows = value.shape[0] // 2
    mine = (place >> bit) & 1
    sent = lax.dynamic_slice_in_dim(value, (1 - mine) * rows, rows, 0)
    kept = lax.dynamic_slice_in_dim(value, mine * rows, rows, 0)
    return kept + swap_bit(sent, bit, count)


def join(value, bit, count, place):
    other = swap_bit(value, bit, count)
    mine = (place >> bit) & 1
    first = jnp.where(mine == 0, value, other)
    second = jnp.where(mine == 0, other, value)
    return jnp.concatenate([first, second], axis=0)


def line_sum(value, count, place):
    stride = count // 4
    inward = []
    across = []
    outward = []
    for low in range(stride):
        ring = [low + stride * at for at in range(4)]
        inward += [(ring[0], ring[1]), (ring[3], ring[2])]
        across += [(ring[1], ring[2]), (ring[2], ring[1])]
        outward += [(ring[1], ring[0]), (ring[2], ring[3])]
    at_line = place // stride
    value = value + lax.ppermute(value, "dp", inward)
    value = value + lax.ppermute(value, "dp", across)
    ended = lax.ppermute(value, "dp", outward)
    return jnp.where((at_line == 1) | (at_line == 2), value, ended)


def all_sum(value, first_bit, count, place):
    second_bit = 1 - first_bit
    value = halve(value, first_bit, count, place)
    value = halve(value, second_bit, count, place)
    low_bits = (count // 4).bit_length() - 1
    for bit in range(2, low_bits):
        value = value + swap_bit(value, bit, count)
    value = line_sum(value, count, place)
    value = join(value, second_bit, count, place)
    return join(value, first_bit, count, place)


def local(
    dp_count,
    tensor_count,
    tokens_in,
    cotangent,
    seq_lengths,
    q_weight,
    k_weight,
    v_weight,
    q_bias,
    v_bias,
    out_weight,
    out_bias,
    first_gain,
    first_shift,
    up_weight,
    up_bias,
    down_weight,
    down_bias,
    second_gain,
    second_shift,
):
    place = lax.axis_index("dp")
    model = q_weight.shape[0]
    width = q_weight.shape[1]
    hidden = up_weight.shape[1]
    row = lambda vector: vector.reshape(1, -1)
    queries, keys, values, context, totals, attn_part = attend(
        seq_lengths, tokens_in, q_weight, k_weight, v_weight, row(q_bias), row(v_bias), out_weight
    )
    first_sum, first_low, inner, active, down_part = feed(
        tokens_in,
        attn_part,
        swap_cores(attn_part, tensor_count),
        row(out_bias),
        row(first_gain),
        row(first_shift),
        up_weight,
        row(up_bias),
        down_weight,
    )
    layer_out, back_second, back_down, down_low, down_high, second_sums = second_norm(
        first_sum,
        down_part,
        swap_cores(down_part, tensor_count),
        cotangent,
        active,
        row(first_gain),
        row(first_shift),
        row(down_bias),
        row(second_gain),
        row(second_shift),
    )
    down_low = all_sum(down_low, 0, dp_count, place)
    down_high = all_sum(down_high, 1, dp_count, place)
    back_part, up_low, up_high, up_sums = feed_back(
        back_down, inner, first_low, down_weight, up_weight
    )
    up_low = all_sum(up_low, 0, dp_count, place)
    up_high = all_sum(up_high, 1, dp_count, place)
    back_first_sum, back_attn, first_sums = first_norm_back(
        first_sum, back_part, swap_cores(back_part, tensor_count), back_second, row(first_gain)
    )
    small = jnp.concatenate(
        [
            jnp.zeros((1, model), jnp.float32),
            up_sums[0].reshape(-1, model),
            first_sums[:3],
            second_sums[:3],
        ]
    )
    small = jnp.pad(small, ((0, -small.shape[0] % 32), (0, 0)))
    first_pack, second_pack, input_part = attend_back(
        seq_lengths,
        back_attn,
        out_weight,
        queries,
        keys,
        values,
        totals,
        tokens_in,
        context,
        q_weight,
        k_weight,
        v_weight,
        small,
    )
    first_pack = all_sum(first_pack, 0, dp_count, place)
    second_pack = all_sum(second_pack, 1, dp_count, place)
    grad_input = (
        (input_part + swap_cores(input_part, tensor_count)) + back_first_sum
    ).astype(jnp.bfloat16)
    turned = second_pack[width : width + model // 2]
    tail = second_pack[width + model // 2 :]
    up_rows = hidden // model
    return (
        layer_out,
        grad_input,
        first_pack[:, :width],
        first_pack[:, width:],
        jnp.concatenate([turned[:, :width], turned[:, width:]], axis=0),
        tail[0, :width],
        tail[0, width:],
        second_pack[:width],
        tail[up_rows + 1],
        tail[up_rows + 2],
        tail[up_rows + 3],
        jnp.concatenate([up_low, up_high], axis=1),
        tail[1 : up_rows + 1].reshape(-1),
        jnp.concatenate([down_low, down_high], axis=0),
        tail[up_rows + 4],
        tail[up_rows + 5],
        tail[up_rows + 6],
    )


def solution(mesh):
    placed = (
        P("dp", None),
        P("dp", None),
        P("dp", None),
        P(None, "tensor"),
        P(None, "tensor"),
        P(None, "tensor"),
        P("tensor"),
        P("tensor"),
        P("tensor", None),
        P(),
        P(),
        P(),
        P(None, "tensor"),
        P("tensor"),
        P("tensor", None),
        P(),
        P(),
        P(),
    )
    counts = (mesh.shape["dp"], mesh.shape["tensor"])

    def on_device(*args):
        return local(*counts, *args)

    return jax.shard_map(
        on_device,
        mesh=mesh,
        in_specs=placed,
        out_specs=(
            P("dp", None),
            P("dp", None),
            P(None, "tensor"),
            P(None, "tensor"),
            P(None, "tensor"),
            P("tensor"),
            P("tensor"),
            P("tensor", None),
            P(),
            P(),
            P(),
            P(None, "tensor"),
            P("tensor"),
            P("tensor", None),
            P(),
            P(),
            P(),
        ),
        check_vma=False,
    )
```

```python
import functools

import jax
import jax.numpy as jnp
from jax import lax
from jax.experimental import pallas as pl
from jax.experimental.pallas import tpu as pltpu
from jax.sharding import PartitionSpec as P

DH = 64
LANES = 128
ROW_BLOCK = 256
MIB = 1 << 20

score_scale = 0.125
norm_eps = 1e-05
far_negative = -1e30
log2_e = 1.4426950408889634


def contract(left_side, right_side, left_dim, right_dim):
    return lax.dot_general(
        left_side,
        right_side,
        (((left_dim,), (right_dim,)), ((), ())),
        preferred_element_type=jnp.float32,
    )


def sequence_ends(lengths_ref, count):
    ends = []
    total = jnp.int32(0)
    for at in range(count):
        total = total + lengths_ref[0, at]
        ends.append(total)
    return ends


def key_window(ends, first_row, rows):
    last_row = first_row + LANES - 1
    start = jnp.int32(0)
    stop = jnp.int32(rows)
    for end in ends:
        start = jnp.where(end <= first_row, jnp.maximum(start, end), start)
        stop = jnp.where(end > last_row, jnp.minimum(stop, end), stop)
    start = (start // LANES) * LANES
    stop = ((stop + LANES - 1) // LANES) * LANES
    return start, stop


def window_bias(ends, first_row, key_start, width):
    query_at = lax.broadcasted_iota(jnp.int32, (1, LANES), 1) + first_row
    seq_start = jnp.zeros((1, LANES), jnp.int32)
    seq_stop = jnp.full((1, LANES), 1 << 30, jnp.int32)
    for end in ends:
        seq_start = jnp.where(query_at >= end, jnp.maximum(seq_start, end), seq_start)
        seq_stop = jnp.where(query_at < end, jnp.minimum(seq_stop, end), seq_stop)
    key_at = lax.broadcasted_iota(jnp.int32, (width, LANES), 0) + key_start
    seen = (key_at >= seq_start) & (key_at < seq_stop)
    bias = jnp.where(seen, 0.0, far_negative).astype(jnp.float32)
    return jnp.concatenate([bias, bias], axis=1)


def split_heads(block):
    lane = lax.broadcasted_iota(jnp.int32, block.shape, 1)
    wide = block.astype(jnp.float32)
    return jnp.concatenate(
        [jnp.where(lane < DH, wide, 0.0), jnp.where(lane < DH, 0.0, wide)], axis=0
    ).astype(jnp.bfloat16)


def merge_heads(turned):
    return jnp.concatenate([turned[:DH, :LANES], turned[DH:, LANES:]], axis=0).T


def put_halves(sent_ref, kept_ref, sums, mine):
    rows = sent_ref.shape[0]
    sent_ref[...] = sums[pl.ds(pl.multiple_of((1 - mine) * rows, 8), rows), :]
    kept_ref[...] = sums[pl.ds(pl.multiple_of(mine * rows, 8), rows), :]


def over_query_blocks(ends, rows, widths, body):
    @pl.loop(0, rows // LANES)
    def _(block):
        first_row = pl.multiple_of(block * LANES, LANES)
        start, stop = key_window(ends, first_row, rows)
        span = stop - start
        lower = 0
        for width in widths:
            chosen = (span > lower) & (span <= width)
            key_start = pl.multiple_of(jnp.minimum(start, rows - width), LANES)
            pl.when(chosen)(functools.partial(body, block, first_row, key_start, width))
            lower = width


def attend_kernel(
    widths,
    seqs,
    lengths_ref,
    tokens_ref,
    q_weight_ref,
    k_weight_ref,
    v_weight_ref,
    q_bias_ref,
    v_bias_ref,
    out_weight_ref,
    queries_ref,
    keys_ref,
    values_ref,
    context_ref,
    total_ref,
    attn_out_ref,
    turned_ref,
):
    rows = tokens_ref.shape[0]
    pairs = q_weight_ref.shape[1] // LANES
    tokens = tokens_ref[...]
    queries_ref[...] = (contract(tokens, q_weight_ref[...], 1, 0) + q_bias_ref[...]).astype(
        jnp.bfloat16
    )
    keys_ref[...] = contract(tokens, k_weight_ref[...], 1, 0).astype(jnp.bfloat16)
    values = contract(tokens, v_weight_ref[...], 1, 0) + v_bias_ref[...]
    values_ref[...] = values.astype(jnp.bfloat16)
    turned_ref[...] = values.T.astype(jnp.bfloat16)
    ends = sequence_ends(lengths_ref, seqs)

    def body(block, first_row, key_start, width):
        bias = window_bias(ends, first_row, key_start, width)
        for pair in range(pairs):
            lanes = slice(pair * LANES, (pair + 1) * LANES)
            both = split_heads(queries_ref[pl.ds(first_row, LANES), lanes])
            keys = keys_ref[pl.ds(key_start, width), lanes]
            scores = contract(keys, both, 1, 1) * (score_scale * log2_e) + bias
            peak = jnp.max(scores, axis=0, keepdims=True)
            exponents = jnp.exp2(scores - peak)
            total = jnp.sum(exponents, axis=0, keepdims=True)
            total_ref[pl.ds(block * pairs + pair, 1), :] = peak + jnp.log2(total)
            probs = (exponents * (1.0 / total)).astype(jnp.bfloat16)
            turned = contract(turned_ref[lanes, pl.ds(key_start, width)], probs, 1, 0)
            context_ref[pl.ds(first_row, LANES), lanes] = merge_heads(turned).astype(jnp.bfloat16)

    over_query_blocks(ends, rows, widths, body)
    attn_out_ref[...] = contract(context_ref[...], out_weight_ref[...], 1, 0)


def attend_back_kernel(
    widths,
    seqs,
    lengths_ref,
    bits_ref,
    back_attn_ref,
    out_weight_ref,
    queries_ref,
    keys_ref,
    values_ref,
    total_ref,
    tokens_ref,
    context_ref,
    q_weight_ref,
    k_weight_ref,
    v_weight_ref,
    small_ref,
    first_sent_ref,
    first_kept_ref,
    second_sent_ref,
    second_kept_ref,
    partial_ref,
    first_pack_ref,
    second_pack_ref,
    back_context_ref,
    turned_ref,
    back_queries_ref,
    back_keys_ref,
    back_values_ref,
):
    rows = tokens_ref.shape[0]
    width_here = q_weight_ref.shape[1]
    pairs = width_here // LANES
    back_context_ref[...] = contract(back_attn_ref[...], out_weight_ref[...], 1, 1).astype(
        jnp.bfloat16
    )
    turned_ref[...] = keys_ref[...].astype(jnp.float32).T.astype(jnp.bfloat16)
    back_keys_ref[...] = jnp.zeros_like(back_keys_ref)
    back_values_ref[...] = jnp.zeros_like(back_values_ref)
    ends = sequence_ends(lengths_ref, seqs)

    def body(block, first_row, key_start, width):
        bias = window_bias(ends, first_row, key_start, width)
        for pair in range(pairs):
            lanes = slice(pair * LANES, (pair + 1) * LANES)
            both = split_heads(queries_ref[pl.ds(first_row, LANES), lanes])
            back_both = split_heads(back_context_ref[pl.ds(first_row, LANES), lanes])
            keys = keys_ref[pl.ds(key_start, width), lanes]
            values = values_ref[pl.ds(key_start, width), lanes]
            scores = contract(keys, both, 1, 1) * (score_scale * log2_e) + bias
            probs = jnp.exp2(scores - total_ref[pl.ds(block * pairs + pair, 1), :])
            back_probs = contract(values, back_both, 1, 1)
            inner = jnp.sum(back_probs * probs, axis=0, keepdims=True)
            back_scores = (probs * (back_probs - inner) * score_scale).astype(jnp.bfloat16)
            back_values_ref[pl.ds(key_start, width), lanes] += contract(
                probs.astype(jnp.bfloat16), back_both, 1, 0
            )
            back_keys_ref[pl.ds(key_start, width), lanes] += contract(back_scores, both, 1, 0)
            turned = contract(turned_ref[lanes, pl.ds(key_start, width)], back_scores, 1, 0)
            back_queries_ref[pl.ds(first_row, LANES), lanes] = merge_heads(turned).astype(
                jnp.bfloat16
            )

    over_query_blocks(ends, rows, widths, body)
    model = tokens_ref.shape[1]
    tokens = tokens_ref[...]
    back_queries = back_queries_ref[...]
    back_keys = back_keys_ref[...].astype(jnp.bfloat16)
    back_values = back_values_ref[...].astype(jnp.bfloat16)
    first_pack_ref[:, :width_here] = contract(tokens, back_queries, 0, 0)
    first_pack_ref[:, width_here:] = contract(tokens, back_keys, 0, 0)
    put_halves(first_sent_ref, first_kept_ref, first_pack_ref, bits_ref[0, 0])
    grad_values = contract(tokens, back_values, 0, 0)
    grad_out = contract(context_ref[...], back_attn_ref[...], 0, 0)
    out_half, value_half, small_half = width_here // 2, model // 4, small_ref.shape[0] // 2
    top = 0
    for at in range(2):
        second_pack_ref[top : top + out_half, :] = grad_out[at * out_half : (at + 1) * out_half]
        top += out_half
        for side in range(2):
            start = side * (model // 2) + at * value_half
            second_pack_ref[
                top : top + value_half, side * width_here : (side + 1) * width_here
            ] = grad_values[start : start + value_half]
        top += value_half
        second_pack_ref[top : top + small_half, :] = small_ref[
            at * small_half : (at + 1) * small_half
        ]
        if at == 0:
            second_pack_ref[top : top + 1, :width_here] = jnp.sum(
                back_queries.astype(jnp.float32), axis=0, keepdims=True
            )
            second_pack_ref[top : top + 1, width_here:] = jnp.sum(
                back_values.astype(jnp.float32), axis=0, keepdims=True
            )
        top += small_half
    put_halves(second_sent_ref, second_kept_ref, second_pack_ref, bits_ref[0, 1])
    partial_ref[...] = (
        contract(back_queries, q_weight_ref[...], 1, 1)
        + contract(back_keys, k_weight_ref[...], 1, 1)
        + contract(back_values, v_weight_ref[...], 1, 1)
    )


def row_mean(values):
    return jnp.mean(values, axis=-1, keepdims=True)


def standardize(values):
    centre = values - row_mean(values)
    rate = lax.rsqrt(row_mean(centre * centre) + norm_eps)
    return centre * rate, rate


def norm_back(upstream, unit, rate, gain):
    scaled = upstream * gain
    return rate * (scaled - row_mean(scaled) - unit * row_mean(scaled * unit))


def add_sums(sums_ref, members):
    @pl.when(pl.program_id(0) == 0)
    def _():
        sums_ref[...] = jnp.zeros_like(sums_ref)

    for at, member in enumerate(members):
        sums_ref[at : at + 1, :] += jnp.sum(member, axis=0, keepdims=True)


def feed_kernel(
    tokens_ref,
    own_ref,
    other_ref,
    out_bias_ref,
    gain_ref,
    shift_ref,
    up_weight_ref,
    up_bias_ref,
    down_weight_ref,
    first_sum_ref,
    first_low_ref,
    inner_ref,
    active_ref,
    partial_ref,
):
    first_sum = (
        tokens_ref[...].astype(jnp.float32) + (own_ref[...] + other_ref[...]) + out_bias_ref[...]
    )
    first_sum_ref[...] = first_sum
    unit, unused = standardize(first_sum)
    first_low = (unit * gain_ref[...] + shift_ref[...]).astype(jnp.bfloat16)
    first_low_ref[...] = first_low
    inner = contract(first_low, up_weight_ref[...], 1, 0) + up_bias_ref[...]
    inner_ref[...] = inner
    active = (inner * (0.5 * (1.0 + lax.erf(inner * 0.7071067811865476)))).astype(jnp.bfloat16)
    active_ref[...] = active
    partial_ref[...] = contract(active, down_weight_ref[...], 1, 0)


def second_norm_kernel(
    bits_ref,
    first_sum_ref,
    own_ref,
    other_ref,
    cotangent_ref,
    active_ref,
    first_gain_ref,
    first_shift_ref,
    down_bias_ref,
    gain_ref,
    shift_ref,
    layer_out_ref,
    back_second_ref,
    back_down_ref,
    low_sent_ref,
    low_kept_ref,
    high_sent_ref,
    high_kept_ref,
    sums_ref,
    grad_low_ref,
    grad_high_ref,
):
    unit, unused = standardize(first_sum_ref[...])
    first = unit * first_gain_ref[...] + first_shift_ref[...]
    second_sum = first + (own_ref[...] + other_ref[...]) + down_bias_ref[...]
    unit, rate = standardize(second_sum)
    layer_out_ref[...] = (unit * gain_ref[...] + shift_ref[...]).astype(jnp.bfloat16)
    upstream = cotangent_ref[...].astype(jnp.float32)
    back_second = norm_back(upstream, unit, rate, gain_ref[...])
    back_second_ref[...] = back_second
    back_down = back_second.astype(jnp.bfloat16)
    back_down_ref[...] = back_down
    half = grad_low_ref.shape[0]

    @pl.when(pl.program_id(0) == 0)
    def _():
        grad_low_ref[...] = jnp.zeros_like(grad_low_ref)
        grad_high_ref[...] = jnp.zeros_like(grad_high_ref)

    grad_low_ref[...] += contract(active_ref[:, :half], back_down, 0, 0)
    grad_high_ref[...] += contract(active_ref[:, half:], back_down, 0, 0)
    add_sums(sums_ref, (back_second, upstream * unit, upstream))

    @pl.when(pl.program_id(0) == pl.num_programs(0) - 1)
    def _():
        put_halves(low_sent_ref, low_kept_ref, grad_low_ref, bits_ref[0, 0])
        put_halves(high_sent_ref, high_kept_ref, grad_high_ref, bits_ref[0, 1])


def feed_back_kernel(
    bits_ref,
    back_down_ref,
    inner_ref,
    first_low_ref,
    down_weight_ref,
    up_weight_ref,
    partial_ref,
    low_sent_ref,
    low_kept_ref,
    high_sent_ref,
    high_kept_ref,
    sums_ref,
    grad_low_ref,
    grad_high_ref,
):
    inner = inner_ref[...]
    slope = 0.5 * (1.0 + lax.erf(inner * 0.7071067811865476)) + inner * (
        0.3989422804014327 * jnp.exp(-0.5 * inner * inner)
    )
    back_active = contract(back_down_ref[...], down_weight_ref[...], 1, 1)
    back_inner = (back_active * slope).astype(jnp.bfloat16)
    partial_ref[...] = contract(back_inner, up_weight_ref[...], 1, 1)
    half = grad_low_ref.shape[1]

    @pl.when(pl.program_id(0) == 0)
    def _():
        grad_low_ref[...] = jnp.zeros_like(grad_low_ref)
        grad_high_ref[...] = jnp.zeros_like(grad_high_ref)

    first_low = first_low_ref[...]
    grad_low_ref[...] += contract(first_low, back_inner[:, :half], 0, 0)
    grad_high_ref[...] += contract(first_low, back_inner[:, half:], 0, 0)
    add_sums(sums_ref, (back_inner.astype(jnp.float32),))

    @pl.when(pl.program_id(0) == pl.num_programs(0) - 1)
    def _():
        put_halves(low_sent_ref, low_kept_ref, grad_low_ref, bits_ref[0, 0])
        put_halves(high_sent_ref, high_kept_ref, grad_high_ref, bits_ref[0, 1])


def first_norm_kernel(
    first_sum_ref,
    own_ref,
    other_ref,
    back_second_ref,
    gain_ref,
    back_first_sum_ref,
    back_attn_ref,
    sums_ref,
):
    unit, rate = standardize(first_sum_ref[...])
    upstream = (own_ref[...] + other_ref[...]) + back_second_ref[...]
    back_first_sum = norm_back(upstream, unit, rate, gain_ref[...])
    back_first_sum_ref[...] = back_first_sum
    back_attn_ref[...] = back_first_sum.astype(jnp.bfloat16)
    add_sums(sums_ref, (back_first_sum, upstream * unit, upstream))


def struct(shape, dtype):
    return jax.ShapeDtypeStruct(shape, dtype)


def by_rows(columns):
    return pl.BlockSpec((ROW_BLOCK, columns), lambda step: (step, 0))


def held(shape):
    return pl.BlockSpec(shape, lambda *step: (0, 0), pipeline_mode=pl.Buffered(1))


def in_smem():
    return pl.BlockSpec(memory_space=pltpu.SMEM)


def in_vmem():
    return pl.BlockSpec(memory_space=pltpu.VMEM)


def params(mebibytes):
    return pltpu.CompilerParams(vmem_limit_bytes=mebibytes * MIB)


def lasting(microseconds):
    return pl.CostEstimate(
        flops=int(microseconds * 1.1e9),
        transcendentals=0,
        bytes_accessed=int(microseconds * 1e6),
    )


def key_widths(rows):
    return tuple(width for width in (640,) if width < rows) + (rows,)


def attend(lengths, tokens, q_weight, k_weight, v_weight, q_bias, v_bias, out_weight):
    rows, model = tokens.shape
    width = q_weight.shape[1]
    totals = rows // LANES * (width // LANES)
    low = struct((rows, width), jnp.bfloat16)
    return pl.pallas_call(
        functools.partial(attend_kernel, key_widths(rows), lengths.shape[1]),
        out_shape=(
            low,
            low,
            low,
            low,
            struct((totals, 2 * LANES), jnp.float32),
            struct((rows, model), jnp.float32),
        ),
        in_specs=[in_smem()] + [in_vmem()] * 7,
        out_specs=(in_vmem(),) * 6,
        scratch_shapes=[pltpu.VMEM((width, rows), jnp.bfloat16)],
        compiler_params=params(60),
        cost_estimate=lasting(20),
        name="attend",
    )(lengths, tokens, q_weight, k_weight, v_weight, q_bias, v_bias, out_weight)


def attend_back(
    lengths,
    bits,
    back_attn,
    out_weight,
    queries,
    keys,
    values,
    totals,
    tokens,
    context,
    q_weight,
    k_weight,
    v_weight,
    small,
):
    rows, model = tokens.shape
    width = q_weight.shape[1]
    pack_rows = width + model // 2 + small.shape[0]
    return pl.pallas_call(
        functools.partial(attend_back_kernel, key_widths(rows), lengths.shape[1]),
        out_shape=(
            struct((model // 2, 2 * width), jnp.float32),
            struct((model // 2, 2 * width), jnp.float32),
            struct((pack_rows // 2, model), jnp.float32),
            struct((pack_rows // 2, model), jnp.float32),
            struct((rows, model), jnp.float32),
        ),
        in_specs=[in_smem()] * 2 + [in_vmem()] * 12,
        out_specs=(in_vmem(),) * 5,
        scratch_shapes=[
            pltpu.VMEM((model, 2 * width), jnp.float32),
            pltpu.VMEM((pack_rows, model), jnp.float32),
            pltpu.VMEM((rows, width), jnp.bfloat16),
            pltpu.VMEM((width, rows), jnp.bfloat16),
            pltpu.VMEM((rows, width), jnp.bfloat16),
            pltpu.VMEM((rows, width), jnp.float32),
            pltpu.VMEM((rows, width), jnp.float32),
        ],
        compiler_params=params(60),
        cost_estimate=lasting(27),
        name="attend_back",
    )(
        lengths,
        bits,
        back_attn,
        out_weight,
        queries,
        keys,
        values,
        totals,
        tokens,
        context,
        q_weight,
        k_weight,
        v_weight,
        small,
    )


def feed(tokens, own, other, out_bias, gain, shift, up_weight, up_bias, down_weight):
    rows, model = tokens.shape
    hidden = up_weight.shape[1]
    return pl.pallas_call(
        feed_kernel,
        grid=(rows // ROW_BLOCK,),
        out_shape=(
            struct((rows, model), jnp.float32),
            struct((rows, model), jnp.bfloat16),
            struct((rows, hidden), jnp.float32),
            struct((rows, hidden), jnp.bfloat16),
            struct((rows, model), jnp.float32),
        ),
        in_specs=[by_rows(model)] * 3
        + [held((1, model))] * 3
        + [held((model, hidden)), held((1, hidden)), held((hidden, model))],
        out_specs=(
            by_rows(model),
            by_rows(model),
            by_rows(hidden),
            by_rows(hidden),
            by_rows(model),
        ),
        compiler_params=params(60),
        cost_estimate=lasting(10),
        name="feed",
    )(tokens, own, other, out_bias, gain, shift, up_weight, up_bias, down_weight)


def second_norm(
    bits, first_sum, own, other, cotangent, active, first_gain, first_shift, down_bias, gain, shift
):
    rows, model = first_sum.shape
    hidden = active.shape[1]
    return pl.pallas_call(
        second_norm_kernel,
        grid=(rows // ROW_BLOCK,),
        out_shape=(
            struct((rows, model), jnp.bfloat16),
            struct((rows, model), jnp.float32),
            struct((rows, model), jnp.bfloat16),
            struct((hidden // 4, model), jnp.float32),
            struct((hidden // 4, model), jnp.float32),
            struct((hidden // 4, model), jnp.float32),
            struct((hidden // 4, model), jnp.float32),
            struct((8, model), jnp.float32),
        ),
        in_specs=[in_smem()] + [by_rows(model)] * 4 + [by_rows(hidden)] + [held((1, model))] * 5,
        out_specs=(
            by_rows(model),
            by_rows(model),
            by_rows(model),
            held((hidden // 4, model)),
            held((hidden // 4, model)),
            held((hidden // 4, model)),
            held((hidden // 4, model)),
            held((8, model)),
        ),
        scratch_shapes=[pltpu.VMEM((hidden // 2, model), jnp.float32)] * 2,
        cost_estimate=lasting(10),
        compiler_params=params(60),
        name="second_norm",
    )(bits, first_sum, own, other, cotangent, active, first_gain, first_shift, down_bias, gain, shift)


def feed_back(bits, back_down, inner, first_low, down_weight, up_weight):
    rows, model = back_down.shape
    hidden = inner.shape[1]
    return pl.pallas_call(
        feed_back_kernel,
        grid=(rows // ROW_BLOCK,),
        out_shape=(
            struct((rows, model), jnp.float32),
            struct((model // 2, hidden // 2), jnp.float32),
            struct((model // 2, hidden // 2), jnp.float32),
            struct((model // 2, hidden // 2), jnp.float32),
            struct((model // 2, hidden // 2), jnp.float32),
            struct((8, hidden), jnp.float32),
        ),
        in_specs=[
            in_smem(),
            by_rows(model),
            by_rows(hidden),
            by_rows(model),
            held((hidden, model)),
            held((model, hidden)),
        ],
        out_specs=(
            by_rows(model),
            held((model // 2, hidden // 2)),
            held((model // 2, hidden // 2)),
            held((model // 2, hidden // 2)),
            held((model // 2, hidden // 2)),
            held((8, hidden)),
        ),
        scratch_shapes=[pltpu.VMEM((model, hidden // 2), jnp.float32)] * 2,
        cost_estimate=lasting(13),
        compiler_params=params(60),
        name="feed_back",
    )(bits, back_down, inner, first_low, down_weight, up_weight)


def first_norm_back(first_sum, own, other, back_second, gain):
    rows, model = first_sum.shape
    return pl.pallas_call(
        first_norm_kernel,
        grid=(rows // ROW_BLOCK,),
        out_shape=(
            struct((rows, model), jnp.float32),
            struct((rows, model), jnp.bfloat16),
            struct((8, model), jnp.float32),
        ),
        in_specs=[by_rows(model)] * 4 + [held((1, model))],
        out_specs=(by_rows(model), by_rows(model), held((8, model))),
        cost_estimate=lasting(5),
        compiler_params=params(60),
        name="first_norm_back",
    )(first_sum, own, other, back_second, gain)


def place_kernel(moves, starts_ref, *refs):
    copies = []
    inputs = 1 + max(source for source, *unused in moves)
    for at, (source, rows, columns, target, row_start, column_start) in enumerate(moves):
        start = row_start(starts_ref) if callable(row_start) else row_start
        size = rows[1] - rows[0]
        copies.append(
            pltpu.make_async_copy(
                refs[source].at[pl.ds(rows[0], size), pl.ds(columns[0], columns[1] - columns[0])],
                refs[inputs + target].at[
                    pl.ds(pl.multiple_of(start, 8), size),
                    pl.ds(column_start, columns[1] - columns[0]),
                ],
                refs[-1].at[at],
            )
        )
    for copy in copies:
        copy.start()
    for copy in copies:
        copy.wait()


def place_blocks(starts, operands, shapes, moves, name):
    anywhere = pl.BlockSpec(memory_space=pl.ANY)
    return pl.pallas_call(
        functools.partial(place_kernel, moves),
        out_shape=tuple(struct(shape, jnp.float32) for shape in shapes),
        in_specs=[in_smem()] + [anywhere] * len(operands),
        out_specs=(anywhere,) * len(shapes),
        scratch_shapes=[pltpu.SemaphoreType.DMA((len(moves),))],
        cost_estimate=lasting(2),
        name=name,
    )(starts, *operands)


def at_bit(rows, bit, same):
    def first(bits_ref):
        return (bits_ref[0, bit] if same else 1 - bits_ref[0, bit]) * rows

    return first


def swap_cores(value, tensor_count):
    return lax.ppermute(value, "tensor", [(i, i ^ 1) for i in range(tensor_count)])


class Ring:
    def __init__(self, count, place):
        self.count = count
        self.place = place
        stride = count // 4
        self.low_bits = stride.bit_length() - 1
        self.inward, self.across, self.outward = [], [], []
        for low in range(stride):
            line = [low + stride * at for at in range(4)]
            self.inward += [(line[0], line[1]), (line[3], line[2])]
            self.across += [(line[1], line[2]), (line[2], line[1])]
            self.outward += [(line[1], line[0]), (line[2], line[3])]
        self.is_middle = (place // stride == 1) | (place // stride == 2)

    def swap(self, value, bit):
        return lax.ppermute(value, "dp", [(i, i ^ (1 << bit)) for i in range(self.count)])

    def mine(self, bit):
        return (self.place >> bit) & 1

    def half(self, value, bit, same):
        rows = value.shape[0] // 2
        mine = self.mine(bit)
        return lax.dynamic_slice_in_dim(value, (mine if same else 1 - mine) * rows, rows, 0)


class Chunk:
    def __init__(self, ring, bits, first_bit, sent, kept):
        self.ring = ring
        self.bits = bits
        self.first_bit = first_bit
        self.second_bit = 1 - first_bit
        self.held = (kept,)
        self.arriving = None
        self.sent = sent
        self.step = 0

    def inputs(self):
        return self.held + (() if self.arriving is None else (self.arriving,))

    def join(self, value, arriving, bit):
        rows, columns = value.shape
        [joined] = place_blocks(
            self.bits,
            (value, arriving),
            ((2 * rows, columns),),
            (
                (0, (0, rows), (0, columns), 0, at_bit(rows, bit, True), 0),
                (1, (0, rows), (0, columns), 0, at_bit(rows, bit, False), 0),
            ),
            "join",
        )
        return joined

    def advance(self, inputs):
        ring = self.ring
        step = self.step
        self.step += 1
        if step == 0:
            self.arriving = ring.swap(self.sent, self.first_bit)
            return None
        if step == 1:
            kept, arrived = inputs
            bit = self.second_bit
            sent = ring.half(kept, bit, False) + ring.half(arrived, bit, False)
            self.held = (ring.half(kept, bit, True), ring.half(arrived, bit, True))
            self.arriving = ring.swap(sent, bit)
            return sent
        if step == 2:
            value = (inputs[0] + inputs[1]) + inputs[2]
            for bit in range(2, ring.low_bits):
                value = value + ring.swap(value, bit)
            self.held = (value,)
            self.arriving = lax.ppermute(value, "dp", ring.inward)
            return value
        value, arrived = inputs
        if step == 3:
            value = value + arrived
            self.arriving = lax.ppermute(value, "dp", ring.across)
        elif step == 4:
            value = value + arrived
            self.arriving = lax.ppermute(value, "dp", ring.outward)
        elif step == 5:
            value = jnp.where(ring.is_middle, value, arrived)
            self.arriving = ring.swap(value, self.second_bit)
        else:
            value = self.join(value, arrived, self.second_bit)
            self.arriving = ring.swap(value, self.first_bit)
        self.held = (value,)
        return value


class Sequence:
    def __init__(self):
        self.last = None

    def after(self, values):
        if self.last is None:
            return tuple(values)
        held = lax.optimization_barrier((*values, self.last))
        return held[:-1]

    def ran(self, result):
        if result is not None:
            self.last = result


def local(
    dp_count,
    tensor_count,
    tokens_in,
    cotangent,
    seq_lengths,
    q_weight,
    k_weight,
    v_weight,
    q_bias,
    v_bias,
    out_weight,
    out_bias,
    first_gain,
    first_shift,
    up_weight,
    up_bias,
    down_weight,
    down_bias,
    second_gain,
    second_shift,
):
    place = lax.axis_index("dp")
    ring = Ring(dp_count, place)
    bits = jnp.stack([ring.mine(0), ring.mine(1)]).reshape(1, 2)
    model = q_weight.shape[0]
    width = q_weight.shape[1]
    hidden = up_weight.shape[1]
    row = lambda vector: vector.reshape(1, -1)
    queries, keys, values, context, totals, attn_part = attend(
        seq_lengths, tokens_in, q_weight, k_weight, v_weight, row(q_bias), row(v_bias), out_weight
    )
    first_sum, first_low, inner, active, down_part = feed(
        tokens_in,
        attn_part,
        swap_cores(attn_part, tensor_count),
        row(out_bias),
        row(first_gain),
        row(first_shift),
        up_weight,
        row(up_bias),
        down_weight,
    )
    layer_out, back_second, back_down, *down_halves, second_sums = second_norm(
        bits,
        first_sum,
        down_part,
        swap_cores(down_part, tensor_count),
        cotangent,
        active,
        row(first_gain),
        row(first_shift),
        row(down_bias),
        row(second_gain),
        row(second_shift),
    )
    order = Sequence()
    order.ran(back_down)
    chunks = {}

    def begin(name, halves):
        chunks[name + "0"] = Chunk(ring, bits, 0, *halves[:2])
        chunks[name + "1"] = Chunk(ring, bits, 1, *halves[2:])

    def run(*names):
        for name in names:
            chunk = chunks[name]
            inputs = chunk.inputs()
            order.ran(chunk.advance(order.after(inputs) if chunk.step else inputs))

    begin("D", down_halves)
    run("D1", "D0")
    [back_down] = order.after((back_down,))
    back_part, *up_halves, up_sums = feed_back(
        bits, back_down, inner, first_low, down_weight, up_weight
    )
    order.ran(back_part)
    begin("U", up_halves)
    run("U1", "U0")
    back_first_sum, back_attn, first_sums = first_norm_back(
        first_sum, back_part, swap_cores(back_part, tensor_count), back_second, row(first_gain)
    )
    order.ran(back_attn)
    run("D1", "D0")
    small = jnp.concatenate(
        [
            jnp.zeros((1, model), jnp.float32),
            up_sums[0].reshape(-1, model),
            first_sums[:3],
            second_sums[:3],
        ]
    )
    small = jnp.pad(small, ((0, -small.shape[0] % 32), (0, 0)))
    [back_attn] = order.after((back_attn,))
    *attn_halves, input_part = attend_back(
        seq_lengths,
        bits,
        back_attn,
        out_weight,
        queries,
        keys,
        values,
        totals,
        tokens_in,
        context,
        q_weight,
        k_weight,
        v_weight,
        small,
    )
    order.ran(input_part)
    begin("A", attn_halves)
    run("A1", "U1", "D0", "D1", "U0", "A0")
    input_part, input_other = order.after((input_part, swap_cores(input_part, tensor_count)))
    grad_input = ((input_part + input_other) + back_first_sum).astype(jnp.bfloat16)
    order.ran(grad_input)
    run("U1", "D0", "A1", "D1", "D0", "U0", "A0", "U1", "D1", "D0", "A1", "U0", "A0", "U1", "D1")
    run("A1", "D0", "U0", "U1", "D1", "A0", "A1", "U0", "A0", "A1")

    def finish(name, shapes, moves):
        operands = ()
        for chunk in (chunks[name + "0"], chunks[name + "1"]):
            operands += order.after(chunk.inputs())
        results = place_blocks(bits, operands, shapes, moves, "place")
        order.ran(results[0])
        return results

    def halves_at(source, rows, columns, target, row_offset, column, bit, height):
        moves = []
        for same in (True, False):
            first = at_bit(height, bit, same)
            moves.append(
                (
                    source + (0 if same else 1),
                    rows,
                    columns,
                    target,
                    lambda ref, first=first: row_offset + first(ref),
                    column,
                )
            )
        return moves

    half = hidden // 2
    quarter = half // 2
    [grad_down] = finish(
        "D",
        ((hidden, model),),
        halves_at(0, (0, quarter), (0, model), 0, 0, 0, 0, quarter)
        + halves_at(2, (0, quarter), (0, model), 0, half, 0, 1, quarter),
    )
    run("A0", "U1", "U0", "A1", "A0")
    rows = model // 2
    [grad_up] = finish(
        "U",
        ((model, hidden),),
        halves_at(0, (0, rows), (0, half), 0, 0, 0, 0, rows)
        + halves_at(2, (0, rows), (0, half), 0, 0, half, 1, rows),
    )
    out_half, value_half = width // 2, model // 4
    tail_start = out_half + value_half
    small_half = small.shape[0] // 2
    square = (model, width)
    grad_q, grad_k, grad_v, grad_out, tail = finish(
        "A",
        (square, square, square, (width, model), (2 * small_half, model)),
        halves_at(0, (0, rows), (0, width), 0, 0, 0, 0, rows)
        + halves_at(0, (0, rows), (width, 2 * width), 1, 0, 0, 0, rows)
        + halves_at(2, (out_half, tail_start), (0, width), 2, 0, 0, 1, value_half)
        + halves_at(2, (out_half, tail_start), (width, 2 * width), 2, rows, 0, 1, value_half)
        + halves_at(2, (0, out_half), (0, model), 3, 0, 0, 1, out_half)
        + halves_at(2, (tail_start, tail_start + small_half), (0, model), 4, 0, 0, 1, small_half),
    )
    up_rows = hidden // model
    return (
        layer_out,
        grad_input,
        grad_q,
        grad_k,
        grad_v,
        tail[0, :width],
        tail[0, width:],
        grad_out,
        tail[up_rows + 1],
        tail[up_rows + 2],
        tail[up_rows + 3],
        grad_up,
        tail[1 : up_rows + 1].reshape(-1),
        grad_down,
        tail[up_rows + 4],
        tail[up_rows + 5],
        tail[up_rows + 6],
    )


def solution(mesh):
    placed = (
        P("dp", None),
        P("dp", None),
        P("dp", None),
        P(None, "tensor"),
        P(None, "tensor"),
        P(None, "tensor"),
        P("tensor"),
        P("tensor"),
        P("tensor", None),
        P(),
        P(),
        P(),
        P(None, "tensor"),
        P("tensor"),
        P("tensor", None),
        P(),
        P(),
        P(),
    )
    counts = (mesh.shape["dp"], mesh.shape["tensor"])

    def on_device(*args):
        return local(*counts, *args)

    return jax.shard_map(
        on_device,
        mesh=mesh,
        in_specs=placed,
        out_specs=(
            P("dp", None),
            P("dp", None),
            P(None, "tensor"),
            P(None, "tensor"),
            P(None, "tensor"),
            P("tensor"),
            P("tensor"),
            P("tensor", None),
            P(),
            P(),
            P(),
            P(None, "tensor"),
            P("tensor"),
            P("tensor", None),
            P(),
            P(),
            P(),
        ),
        check_vma=False,
    )
```

```python
import functools

import jax
import jax.numpy as jnp
from jax import lax
from jax.experimental import pallas as pl
from jax.experimental.pallas import tpu as pltpu
from jax.sharding import PartitionSpec as P

DH = 64
LANES = 128
ROW_BLOCK = 256
MIB = 1 << 20

score_scale = 0.125
norm_eps = 1e-05
far_negative = -1e30
log2_e = 1.4426950408889634


def contract(left_side, right_side, left_dim, right_dim):
    return lax.dot_general(
        left_side,
        right_side,
        (((left_dim,), (right_dim,)), ((), ())),
        preferred_element_type=jnp.float32,
    )


def sequence_ends(lengths_ref, count):
    ends = []
    total = jnp.int32(0)
    for at in range(count):
        total = total + lengths_ref[0, at]
        ends.append(total)
    return ends


def key_window(ends, first_row, rows):
    last_row = first_row + LANES - 1
    start = jnp.int32(0)
    stop = jnp.int32(rows)
    for end in ends:
        start = jnp.where(end <= first_row, jnp.maximum(start, end), start)
        stop = jnp.where(end > last_row, jnp.minimum(stop, end), stop)
    start = (start // LANES) * LANES
    stop = ((stop + LANES - 1) // LANES) * LANES
    return start, stop


def window_bias(ends, first_row, key_start, width):
    query_at = lax.broadcasted_iota(jnp.int32, (1, LANES), 1) + first_row
    seq_start = jnp.zeros((1, LANES), jnp.int32)
    seq_stop = jnp.full((1, LANES), 1 << 30, jnp.int32)
    for end in ends:
        seq_start = jnp.where(query_at >= end, jnp.maximum(seq_start, end), seq_start)
        seq_stop = jnp.where(query_at < end, jnp.minimum(seq_stop, end), seq_stop)
    key_at = lax.broadcasted_iota(jnp.int32, (width, LANES), 0) + key_start
    seen = (key_at >= seq_start) & (key_at < seq_stop)
    bias = jnp.where(seen, 0.0, far_negative).astype(jnp.float32)
    return jnp.concatenate([bias, bias], axis=1)


def split_heads(block):
    lane = lax.broadcasted_iota(jnp.int32, block.shape, 1)
    wide = block.astype(jnp.float32)
    return jnp.concatenate(
        [jnp.where(lane < DH, wide, 0.0), jnp.where(lane < DH, 0.0, wide)], axis=0
    ).astype(jnp.bfloat16)


def merge_heads(turned):
    return jnp.concatenate([turned[:DH, :LANES], turned[DH:, LANES:]], axis=0).T


def put_halves(sent_ref, kept_ref, sums, mine):
    rows = sent_ref.shape[0]
    sent_ref[...] = sums[pl.ds(pl.multiple_of((1 - mine) * rows, 8), rows), :]
    kept_ref[...] = sums[pl.ds(pl.multiple_of(mine * rows, 8), rows), :]


def over_query_blocks(ends, rows, widths, body):
    @pl.loop(0, rows // LANES)
    def _(block):
        first_row = pl.multiple_of(block * LANES, LANES)
        start, stop = key_window(ends, first_row, rows)
        span = stop - start
        lower = 0
        for width in widths:
            chosen = (span > lower) & (span <= width)
            key_start = pl.multiple_of(jnp.minimum(start, rows - width), LANES)
            pl.when(chosen)(functools.partial(body, block, first_row, key_start, width))
            lower = width


def attend_kernel(
    widths,
    seqs,
    lengths_ref,
    tokens_ref,
    q_weight_ref,
    k_weight_ref,
    v_weight_ref,
    q_bias_ref,
    v_bias_ref,
    out_weight_ref,
    queries_ref,
    keys_ref,
    values_ref,
    context_ref,
    total_ref,
    attn_low_ref,
    attn_high_ref,
    turned_ref,
):
    rows = tokens_ref.shape[0]
    pairs = q_weight_ref.shape[1] // LANES
    tokens = tokens_ref[...]
    queries_ref[...] = (contract(tokens, q_weight_ref[...], 1, 0) + q_bias_ref[...]).astype(
        jnp.bfloat16
    )
    keys_ref[...] = contract(tokens, k_weight_ref[...], 1, 0).astype(jnp.bfloat16)
    values = contract(tokens, v_weight_ref[...], 1, 0) + v_bias_ref[...]
    values_ref[...] = values.astype(jnp.bfloat16)
    turned_ref[...] = values.T.astype(jnp.bfloat16)
    ends = sequence_ends(lengths_ref, seqs)

    def body(block, first_row, key_start, width):
        bias = window_bias(ends, first_row, key_start, width)
        for pair in range(pairs):
            lanes = slice(pair * LANES, (pair + 1) * LANES)
            both = split_heads(queries_ref[pl.ds(first_row, LANES), lanes])
            keys = keys_ref[pl.ds(key_start, width), lanes]
            scores = contract(keys, both, 1, 1) * (score_scale * log2_e) + bias
            peak = jnp.max(scores, axis=0, keepdims=True)
            exponents = jnp.exp2(scores - peak)
            total = jnp.sum(exponents, axis=0, keepdims=True)
            total_ref[pl.ds(block * pairs + pair, 1), :] = peak + jnp.log2(total)
            probs = (exponents * (1.0 / total)).astype(jnp.bfloat16)
            turned = contract(turned_ref[lanes, pl.ds(key_start, width)], probs, 1, 0)
            context_ref[pl.ds(first_row, LANES), lanes] = merge_heads(turned).astype(jnp.bfloat16)

    over_query_blocks(ends, rows, widths, body)
    half = rows // 2
    attn_low_ref[...] = contract(context_ref[:half], out_weight_ref[...], 1, 0)
    attn_high_ref[...] = contract(context_ref[half:], out_weight_ref[...], 1, 0)


def attend_back_kernel(
    widths,
    seqs,
    lengths_ref,
    bits_ref,
    back_low_ref,
    back_high_ref,
    out_weight_ref,
    queries_ref,
    keys_ref,
    values_ref,
    total_ref,
    tokens_ref,
    context_ref,
    q_weight_ref,
    k_weight_ref,
    v_weight_ref,
    small_ref,
    first_sent_ref,
    first_kept_ref,
    second_sent_ref,
    second_kept_ref,
    partial_low_ref,
    partial_high_ref,
    first_pack_ref,
    second_pack_ref,
    back_context_ref,
    turned_ref,
    back_queries_ref,
    back_keys_ref,
    back_values_ref,
):
    rows = tokens_ref.shape[0]
    width_here = q_weight_ref.shape[1]
    pairs = width_here // LANES
    half_rows = rows // 2
    for at, back_ref in enumerate((back_low_ref, back_high_ref)):
        back_context_ref[at * half_rows : (at + 1) * half_rows] = contract(
            back_ref[...], out_weight_ref[...], 1, 1
        ).astype(jnp.bfloat16)
    turned_ref[...] = keys_ref[...].astype(jnp.float32).T.astype(jnp.bfloat16)
    back_keys_ref[...] = jnp.zeros_like(back_keys_ref)
    back_values_ref[...] = jnp.zeros_like(back_values_ref)
    ends = sequence_ends(lengths_ref, seqs)

    def body(block, first_row, key_start, width):
        bias = window_bias(ends, first_row, key_start, width)
        for pair in range(pairs):
            lanes = slice(pair * LANES, (pair + 1) * LANES)
            both = split_heads(queries_ref[pl.ds(first_row, LANES), lanes])
            back_both = split_heads(back_context_ref[pl.ds(first_row, LANES), lanes])
            keys = keys_ref[pl.ds(key_start, width), lanes]
            values = values_ref[pl.ds(key_start, width), lanes]
            scores = contract(keys, both, 1, 1) * (score_scale * log2_e) + bias
            probs = jnp.exp2(scores - total_ref[pl.ds(block * pairs + pair, 1), :])
            back_probs = contract(values, back_both, 1, 1)
            inner = jnp.sum(back_probs * probs, axis=0, keepdims=True)
            back_scores = (probs * (back_probs - inner) * score_scale).astype(jnp.bfloat16)
            back_values_ref[pl.ds(key_start, width), lanes] += contract(
                probs.astype(jnp.bfloat16), back_both, 1, 0
            )
            back_keys_ref[pl.ds(key_start, width), lanes] += contract(back_scores, both, 1, 0)
            turned = contract(turned_ref[lanes, pl.ds(key_start, width)], back_scores, 1, 0)
            back_queries_ref[pl.ds(first_row, LANES), lanes] = merge_heads(turned).astype(
                jnp.bfloat16
            )

    over_query_blocks(ends, rows, widths, body)
    model = tokens_ref.shape[1]
    tokens = tokens_ref[...]
    back_queries = back_queries_ref[...]
    back_keys = back_keys_ref[...].astype(jnp.bfloat16)
    back_values = back_values_ref[...].astype(jnp.bfloat16)
    first_pack_ref[:, :width_here] = contract(tokens, back_queries, 0, 0)
    first_pack_ref[:, width_here:] = contract(tokens, back_keys, 0, 0)
    put_halves(first_sent_ref, first_kept_ref, first_pack_ref, bits_ref[0, 0])
    grad_values = contract(tokens, back_values, 0, 0)
    grad_out = contract(context_ref[:half_rows], back_low_ref[...], 0, 0) + contract(
        context_ref[half_rows:], back_high_ref[...], 0, 0
    )
    out_half, value_half, small_half = width_here // 2, model // 4, small_ref.shape[0] // 2
    top = 0
    for at in range(2):
        second_pack_ref[top : top + out_half, :] = grad_out[at * out_half : (at + 1) * out_half]
        top += out_half
        for side in range(2):
            start = side * (model // 2) + at * value_half
            second_pack_ref[
                top : top + value_half, side * width_here : (side + 1) * width_here
            ] = grad_values[start : start + value_half]
        top += value_half
        second_pack_ref[top : top + small_half, :] = small_ref[
            at * small_half : (at + 1) * small_half
        ]
        if at == 0:
            second_pack_ref[top : top + 1, :width_here] = jnp.sum(
                back_queries.astype(jnp.float32), axis=0, keepdims=True
            )
            second_pack_ref[top : top + 1, width_here:] = jnp.sum(
                back_values.astype(jnp.float32), axis=0, keepdims=True
            )
        top += small_half
    put_halves(second_sent_ref, second_kept_ref, second_pack_ref, bits_ref[0, 1])
    for at, out_ref in enumerate((partial_low_ref, partial_high_ref)):
        part = slice(at * half_rows, (at + 1) * half_rows)
        out_ref[...] = (
            contract(back_queries[part], q_weight_ref[...], 1, 1)
            + contract(back_keys[part], k_weight_ref[...], 1, 1)
            + contract(back_values[part], v_weight_ref[...], 1, 1)
        )


def row_mean(values):
    return jnp.mean(values, axis=-1, keepdims=True)


def standardize(values):
    centre = values - row_mean(values)
    rate = lax.rsqrt(row_mean(centre * centre) + norm_eps)
    return centre * rate, rate


def norm_back(upstream, unit, rate, gain):
    scaled = upstream * gain
    return rate * (scaled - row_mean(scaled) - unit * row_mean(scaled * unit))


def column_sum(member):
    return jnp.sum(member, axis=0, keepdims=True)


def row_blocks(rows):
    return [slice(at, at + ROW_BLOCK) for at in range(0, rows, ROW_BLOCK)]


def feed_kernel(first_row, *refs):
    (
        tokens_ref,
        own_ref,
        *other_refs,
        out_bias_ref,
        gain_ref,
        shift_ref,
        up_weight_ref,
        up_bias_ref,
        down_weight_ref,
        first_sum_ref,
        first_low_ref,
        active_ref,
        partial_ref,
    ) = refs
    for at, other_ref in zip(row_blocks(own_ref.shape[0]), other_refs, strict=True):
        tokens = tokens_ref[first_row + at.start : first_row + at.stop]
        first_sum = (
            tokens.astype(jnp.float32) + (own_ref[at] + other_ref[...]) + out_bias_ref[...]
        )
        first_sum_ref[at] = first_sum
        unit, unused = standardize(first_sum)
        first_low = (unit * gain_ref[...] + shift_ref[...]).astype(jnp.bfloat16)
        first_low_ref[at] = first_low
        inner = contract(first_low, up_weight_ref[...], 1, 0) + up_bias_ref[...]
        active = (inner * (0.5 * (1.0 + lax.erf(inner * 0.7071067811865476)))).astype(
            jnp.bfloat16
        )
        active_ref[at] = active
        partial_ref[at] = contract(active, down_weight_ref[...], 1, 0)


def second_norm_kernel(first_row, *refs):
    (
        first_sum_ref,
        own_ref,
        *other_refs,
        cotangent_ref,
        first_gain_ref,
        first_shift_ref,
        down_bias_ref,
        gain_ref,
        shift_ref,
        layer_out_ref,
        back_second_ref,
        back_down_ref,
        sums_ref,
    ) = refs
    bias_sum, gain_sum, shift_sum = 0.0, 0.0, 0.0
    for at, other_ref in zip(row_blocks(own_ref.shape[0]), other_refs, strict=True):
        unit, unused = standardize(first_sum_ref[at])
        first = unit * first_gain_ref[...] + first_shift_ref[...]
        second_sum = first + (own_ref[at] + other_ref[...]) + down_bias_ref[...]
        unit, rate = standardize(second_sum)
        layer_out_ref[at] = (unit * gain_ref[...] + shift_ref[...]).astype(jnp.bfloat16)
        upstream = cotangent_ref[first_row + at.start : first_row + at.stop].astype(jnp.float32)
        back_second = norm_back(upstream, unit, rate, gain_ref[...])
        back_second_ref[at] = back_second
        back_down_ref[at] = back_second.astype(jnp.bfloat16)
        bias_sum += column_sum(back_second)
        gain_sum += column_sum(upstream * unit)
        shift_sum += column_sum(upstream)
    sums_ref[...] = jnp.zeros_like(sums_ref)
    sums_ref[0:1, :] = bias_sum
    sums_ref[1:2, :] = gain_sum
    sums_ref[2:3, :] = shift_sum


def grad_down_kernel(
    bits_ref,
    active_low_ref,
    active_high_ref,
    back_low_ref,
    back_high_ref,
    low_sent_ref,
    low_kept_ref,
    high_sent_ref,
    high_kept_ref,
):
    rows = low_sent_ref.shape[0]
    for at, (sent_ref, kept_ref) in enumerate(
        ((low_sent_ref, low_kept_ref), (high_sent_ref, high_kept_ref))
    ):
        mine = bits_ref[0, at]
        for out_ref, place in ((sent_ref, 1 - mine), (kept_ref, mine)):
            units = pl.ds(pl.multiple_of((2 * at + place) * rows, LANES), rows)
            out_ref[...] = contract(active_low_ref[:, units], back_low_ref[...], 0, 0) + contract(
                active_high_ref[:, units], back_high_ref[...], 0, 0
            )


def feed_back_kernel(
    back_down_ref,
    first_low_ref,
    up_weight_ref,
    up_bias_ref,
    down_weight_ref,
    partial_ref,
    back_inner_ref,
    sums_ref,
):
    total = 0.0
    for at in row_blocks(back_down_ref.shape[0]):
        inner = contract(first_low_ref[at], up_weight_ref[...], 1, 0) + up_bias_ref[...]
        slope = 0.5 * (1.0 + lax.erf(inner * 0.7071067811865476)) + inner * (
            0.3989422804014327 * jnp.exp(-0.5 * inner * inner)
        )
        back_active = contract(back_down_ref[at], down_weight_ref[...], 1, 1)
        back_inner = (back_active * slope).astype(jnp.bfloat16)
        back_inner_ref[at] = back_inner
        partial_ref[at] = contract(back_inner, up_weight_ref[...], 1, 1)
        total += column_sum(back_inner.astype(jnp.float32))
    sums_ref[...] = jnp.zeros_like(sums_ref)
    sums_ref[0:1, :] = total


def grad_up_kernel(
    bits_ref,
    first_low_ref,
    first_high_ref,
    back_low_ref,
    back_high_ref,
    low_sent_ref,
    low_kept_ref,
    high_sent_ref,
    high_kept_ref,
):
    rows, columns = low_sent_ref.shape
    for at, (sent_ref, kept_ref) in enumerate(
        ((low_sent_ref, low_kept_ref), (high_sent_ref, high_kept_ref))
    ):
        mine = bits_ref[0, at]
        units = slice(at * columns, (at + 1) * columns)
        for out_ref, place in ((sent_ref, 1 - mine), (kept_ref, mine)):
            features = pl.ds(pl.multiple_of(place * rows, LANES), rows)
            out_ref[...] = contract(
                first_low_ref[:, features], back_low_ref[:, units], 0, 0
            ) + contract(first_high_ref[:, features], back_high_ref[:, units], 0, 0)


def first_norm_kernel(*refs):
    (
        first_sum_ref,
        own_ref,
        *other_refs,
        back_second_ref,
        gain_ref,
        back_first_sum_ref,
        back_attn_ref,
        sums_ref,
    ) = refs
    bias_sum, gain_sum, shift_sum = 0.0, 0.0, 0.0
    for at, other_ref in zip(row_blocks(own_ref.shape[0]), other_refs, strict=True):
        unit, rate = standardize(first_sum_ref[at])
        upstream = (own_ref[at] + other_ref[...]) + back_second_ref[at]
        back_first_sum = norm_back(upstream, unit, rate, gain_ref[...])
        back_first_sum_ref[at] = back_first_sum
        back_attn_ref[at] = back_first_sum.astype(jnp.bfloat16)
        bias_sum += column_sum(back_first_sum)
        gain_sum += column_sum(upstream * unit)
        shift_sum += column_sum(upstream)
    sums_ref[...] = jnp.zeros_like(sums_ref)
    sums_ref[0:1, :] = bias_sum
    sums_ref[1:2, :] = gain_sum
    sums_ref[2:3, :] = shift_sum


def input_kernel(*refs):
    *sources, grad_ref = refs
    rows = grad_ref.shape[0] // 2
    blocks = row_blocks(rows)
    for half in range(2):
        own_ref, *other_refs, first_ref = sources[half * len(sources) // 2 :][: len(sources) // 2]
        for at, other_ref in zip(blocks, other_refs, strict=True):
            grad_ref[half * rows + at.start : half * rows + at.stop] = (
                (own_ref[at] + other_ref[...]) + first_ref[at]
            ).astype(jnp.bfloat16)


def joined_kernel(low_ref, high_ref, out_ref):
    rows = low_ref.shape[0]
    out_ref[:rows] = low_ref[...]
    out_ref[rows:] = high_ref[...]


def struct(shape, dtype):
    return jax.ShapeDtypeStruct(shape, dtype)


def in_smem():
    return pl.BlockSpec(memory_space=pltpu.SMEM)


def in_vmem():
    return pl.BlockSpec(memory_space=pltpu.VMEM)


def key_widths(rows):
    return tuple(width for width in (640,) if width < rows) + (rows,)


def call(body, outs, scalars, operands, name, mebibytes=16, scratch=()):
    return pl.pallas_call(
        body,
        out_shape=tuple(struct(*out) for out in outs),
        in_specs=[in_smem()] * len(scalars) + [in_vmem()] * len(operands),
        out_specs=(in_vmem(),) * len(outs),
        scratch_shapes=[pltpu.VMEM(*shape) for shape in scratch],
        compiler_params=pltpu.CompilerParams(vmem_limit_bytes=mebibytes * MIB),
        name=name,
    )(*scalars, *operands)


low, exact = jnp.bfloat16, jnp.float32


def attend(lengths, tokens, *others):
    rows, model = tokens.shape
    width = others[0].shape[1]
    totals = rows // LANES * (width // LANES)
    half = (rows // 2, model)
    return call(
        functools.partial(attend_kernel, key_widths(rows), lengths.shape[1]),
        [((rows, width), low)] * 4
        + [((totals, 2 * LANES), exact), (half, exact), (half, exact)],
        (lengths,),
        (tokens, *others),
        "attend",
        20,
        [((width, rows), low)],
    )


def attend_back(lengths, bits, operands, rows, model, width, small_rows):
    pack_rows = width + model // 2 + small_rows
    half = (rows // 2, model)
    return call(
        functools.partial(attend_back_kernel, key_widths(rows), lengths.shape[1]),
        [((model // 2, 2 * width), exact)] * 2
        + [((pack_rows // 2, model), exact)] * 2
        + [(half, exact)] * 2,
        (lengths, bits),
        operands,
        "attend_back",
        28,
        [
            ((model, 2 * width), exact),
            ((pack_rows, model), exact),
            ((rows, width), low),
            ((width, rows), low),
            ((rows, width), low),
            ((rows, width), exact),
            ((rows, width), exact),
        ],
    )


def place_kernel(moves, starts_ref, *refs):
    copies = []
    inputs = 1 + max(source for source, *unused in moves)
    for at, (source, rows, columns, target, row_start, column_start) in enumerate(moves):
        start = row_start(starts_ref) if callable(row_start) else row_start
        size = rows[1] - rows[0]
        copies.append(
            pltpu.make_async_copy(
                refs[source].at[pl.ds(rows[0], size), pl.ds(columns[0], columns[1] - columns[0])],
                refs[inputs + target].at[
                    pl.ds(pl.multiple_of(start, 8), size),
                    pl.ds(column_start, columns[1] - columns[0]),
                ],
                refs[-1].at[at],
            )
        )
    for copy in copies:
        copy.start()
    for copy in copies:
        copy.wait()


def place_blocks(starts, operands, shapes, moves, name):
    anywhere = pl.BlockSpec(memory_space=pl.ANY)
    return pl.pallas_call(
        functools.partial(place_kernel, moves),
        out_shape=tuple(struct(shape, jnp.float32) for shape in shapes),
        in_specs=[in_smem()] + [in_vmem()] * len(operands),
        out_specs=(anywhere,) * len(shapes),
        scratch_shapes=[pltpu.SemaphoreType.DMA((len(moves),))],
        compiler_params=pltpu.CompilerParams(vmem_limit_bytes=8 * MIB),
        name=name,
    )(starts, *operands)


def at_bit(rows, bit, same):
    def first(bits_ref):
        return (bits_ref[0, bit] if same else 1 - bits_ref[0, bit]) * rows

    return first


def swap_cores(value, tensor_count):
    return lax.ppermute(value, "tensor", [(i, i ^ 1) for i in range(tensor_count)])


class Ring:
    def __init__(self, count, place):
        self.count = count
        self.place = place
        stride = count // 4
        self.low_bits = stride.bit_length() - 1
        self.inward, self.across, self.outward = [], [], []
        for low in range(stride):
            line = [low + stride * at for at in range(4)]
            self.inward += [(line[0], line[1]), (line[3], line[2])]
            self.across += [(line[1], line[2]), (line[2], line[1])]
            self.outward += [(line[1], line[0]), (line[2], line[3])]
        self.is_middle = (place // stride == 1) | (place // stride == 2)

    def swap(self, value, bit):
        return lax.ppermute(value, "dp", [(i, i ^ (1 << bit)) for i in range(self.count)])

    def mine(self, bit):
        return (self.place >> bit) & 1

    def half(self, value, bit, same):
        rows = value.shape[0] // 2
        mine = self.mine(bit)
        return lax.dynamic_slice_in_dim(value, (mine if same else 1 - mine) * rows, rows, 0)


class Chunk:
    def __init__(self, ring, bits, first_bit, sent, kept):
        self.ring = ring
        self.bits = bits
        self.first_bit = first_bit
        self.second_bit = 1 - first_bit
        self.held = (kept,)
        self.arriving = None
        self.sent = sent
        self.step = 0

    def inputs(self):
        return self.held + (() if self.arriving is None else (self.arriving,))

    def join(self, value, arriving, bit):
        rows, columns = value.shape
        [joined] = place_blocks(
            self.bits,
            (value, arriving),
            ((2 * rows, columns),),
            (
                (0, (0, rows), (0, columns), 0, at_bit(rows, bit, True), 0),
                (1, (0, rows), (0, columns), 0, at_bit(rows, bit, False), 0),
            ),
            "join",
        )
        return joined

    def advance(self, inputs):
        ring = self.ring
        step = self.step
        self.step += 1
        if step == 0:
            self.arriving = ring.swap(self.sent, self.first_bit)
            return None
        if step == 1:
            kept, arrived = inputs
            bit = self.second_bit
            sent = ring.half(kept, bit, False) + ring.half(arrived, bit, False)
            self.held = (ring.half(kept, bit, True), ring.half(arrived, bit, True))
            self.arriving = ring.swap(sent, bit)
            return sent
        if step == 2:
            value = (inputs[0] + inputs[1]) + inputs[2]
            for bit in range(2, ring.low_bits):
                value = value + ring.swap(value, bit)
            self.held = (value,)
            self.arriving = lax.ppermute(value, "dp", ring.inward)
            return value
        value, arrived = inputs
        if step == 3:
            value = value + arrived
            self.arriving = lax.ppermute(value, "dp", ring.across)
        elif step == 4:
            value = value + arrived
            self.arriving = lax.ppermute(value, "dp", ring.outward)
        elif step == 5:
            value = jnp.where(ring.is_middle, value, arrived)
            self.arriving = ring.swap(value, self.second_bit)
        else:
            value = self.join(value, arrived, self.second_bit)
            self.arriving = ring.swap(value, self.first_bit)
        self.held = (value,)
        return value


class Sequence:
    def __init__(self):
        self.last = None

    def after(self, values):
        if self.last is None:
            return tuple(values)
        held = lax.optimization_barrier((*values, self.last))
        return held[:-1]

    def ran(self, result):
        if result is not None:
            self.last = result


def local(
    dp_count,
    tensor_count,
    tokens_in,
    cotangent,
    seq_lengths,
    q_weight,
    k_weight,
    v_weight,
    q_bias,
    v_bias,
    out_weight,
    out_bias,
    first_gain,
    first_shift,
    up_weight,
    up_bias,
    down_weight,
    down_bias,
    second_gain,
    second_shift,
):
    place = lax.axis_index("dp")
    ring = Ring(dp_count, place)
    bits = jnp.stack([ring.mine(0), ring.mine(1)]).reshape(1, 2)
    model = q_weight.shape[0]
    width = q_weight.shape[1]
    hidden = up_weight.shape[1]
    row = lambda vector: vector.reshape(1, -1)
    rows = tokens_in.shape[0]
    half_rows = rows // 2
    half_shape = (half_rows, model)
    queries, keys, values, context, totals, *attn_parts = attend(
        seq_lengths, tokens_in, q_weight, k_weight, v_weight, row(q_bias), row(v_bias), out_weight
    )
    first_vectors = (row(out_bias), row(first_gain), row(first_shift))
    order = Sequence()

    def exchanged(parts):
        return [
            (part,)
            + tuple(swap_cores(part[at], tensor_count) for at in row_blocks(part.shape[0]))
            for part in parts
        ]

    fed = []
    for at, pair in enumerate(exchanged(attn_parts)):
        fed.append(
            call(
                functools.partial(feed_kernel, at * half_rows),
                [(half_shape, exact), (half_shape, low), ((half_rows, hidden), low), (half_shape, exact)],
                (),
                (tokens_in, *pair, *first_vectors, up_weight, row(up_bias), down_weight),
                "feed",
            )
        )
    first_sums, first_lows, actives, down_parts = zip(*fed, strict=True)
    second_vectors = [row(member) for member in (first_gain, first_shift, down_bias, second_gain, second_shift)]
    normed = []
    for at, pair in enumerate(exchanged(down_parts)):
        normed.append(
            call(
                functools.partial(second_norm_kernel, at * half_rows),
                [(half_shape, low), (half_shape, exact), (half_shape, low), ((8, model), exact)],
                (),
                (first_sums[at], *pair, cotangent, *second_vectors),
                "second_norm",
            )
        )
    outs, back_seconds, back_downs, second_sums = zip(*normed, strict=True)
    chunks = {}

    def begin(name, halves):
        chunks[name + "0"] = Chunk(ring, bits, 0, *halves[:2])
        chunks[name + "1"] = Chunk(ring, bits, 1, *halves[2:])

    def run(*names):
        for name in names:
            chunk = chunks[name]
            inputs = chunk.inputs()
            order.ran(chunk.advance(order.after(inputs) if chunk.step else inputs))

    down_halves = call(
        grad_down_kernel,
        [((hidden // 4, model), exact)] * 4,
        (bits,),
        (*actives, *back_downs),
        "grad_down",
    )
    order.ran(down_halves[0])
    begin("D", down_halves)
    run("D1", "D0")
    fed_back = []
    for at in range(2):
        [back_down] = order.after((back_downs[at],))
        fed_back.append(
            call(
                feed_back_kernel,
                [(half_shape, exact), ((half_rows, hidden), low), ((8, hidden), exact)],
                (),
                (back_down, first_lows[at], up_weight, row(up_bias), down_weight),
                "feed_back",
            )
        )
        order.ran(fed_back[-1][1])
    back_parts, back_inners, up_sums = zip(*fed_back, strict=True)
    back_inner = order.after((back_inners[0],))
    up_halves = call(
        grad_up_kernel,
        [((model // 2, hidden // 2), exact)] * 4,
        (bits,),
        (*first_lows, *back_inner, back_inners[1]),
        "grad_up",
    )
    order.ran(up_halves[0])
    begin("U", up_halves)
    run("U1", "U0")
    normed_back = []
    for at, pair in enumerate(exchanged(back_parts)):
        pair = order.after(pair)
        normed_back.append(
            call(
                first_norm_kernel,
                [(half_shape, exact), (half_shape, low), ((8, model), exact)],
                (),
                (first_sums[at], *pair, back_seconds[at], row(first_gain)),
                "first_norm_back",
            )
        )
        order.ran(normed_back[-1][1])
        if at == 0:
            run("D1", "D0")
    back_first_sums, back_attns, norm_sums = zip(*normed_back, strict=True)
    small = jnp.concatenate(
        [
            jnp.zeros((1, model), jnp.float32),
            (up_sums[0] + up_sums[1])[0].reshape(-1, model),
            (norm_sums[0] + norm_sums[1])[:3],
            (second_sums[0] + second_sums[1])[:3],
        ]
    )
    small = jnp.pad(small, ((0, -small.shape[0] % 32), (0, 0)))
    back_attn = order.after(back_attns)
    *attn_halves, low_part, high_part = attend_back(
        seq_lengths,
        bits,
        (*back_attn, out_weight, queries, keys, values, totals, tokens_in, context)
        + (q_weight, k_weight, v_weight, small),
        rows,
        model,
        width,
        small.shape[0],
    )
    order.ran(low_part)
    begin("A", attn_halves)
    run("A1", "U1", "D0", "D1", "U0", "A0")
    pairs = exchanged((low_part, high_part))
    first = order.after(pairs[0])
    [grad_input] = call(
        input_kernel,
        [((rows, model), low)],
        (),
        (*first, back_first_sums[0], *pairs[1], back_first_sums[1]),
        "grad_input",
    )
    order.ran(grad_input)
    [layer_out] = call(joined_kernel, [((rows, model), low)], (), outs, "layer_out")
    run("U1", "D0", "A1", "D1", "D0", "U0", "A0", "U1", "D1", "D0", "A1", "U0", "A0", "U1", "D1")
    run("A1", "D0", "U0", "U1", "D1", "A0", "A1", "U0", "A0", "A1")

    def finish(name, shapes, moves):
        operands = ()
        for chunk in (chunks[name + "0"], chunks[name + "1"]):
            operands += order.after(chunk.inputs())
        results = place_blocks(bits, operands, shapes, moves, "place")
        order.ran(results[0])
        return results

    def halves_at(source, rows, columns, target, row_offset, column, bit, height):
        moves = []
        for same in (True, False):
            first = at_bit(height, bit, same)
            moves.append(
                (
                    source + (0 if same else 1),
                    rows,
                    columns,
                    target,
                    lambda ref, first=first: row_offset + first(ref),
                    column,
                )
            )
        return moves

    half = hidden // 2
    quarter = half // 2
    [grad_down] = finish(
        "D",
        ((hidden, model),),
        halves_at(0, (0, quarter), (0, model), 0, 0, 0, 0, quarter)
        + halves_at(2, (0, quarter), (0, model), 0, half, 0, 1, quarter),
    )
    run("A0", "U1", "U0", "A1", "A0")
    rows = model // 2
    [grad_up] = finish(
        "U",
        ((model, hidden),),
        halves_at(0, (0, rows), (0, half), 0, 0, 0, 0, rows)
        + halves_at(2, (0, rows), (0, half), 0, 0, half, 1, rows),
    )
    out_half, value_half = width // 2, model // 4
    tail_start = out_half + value_half
    small_half = small.shape[0] // 2
    square = (model, width)
    grad_q, grad_k, grad_v, grad_out, tail = finish(
        "A",
        (square, square, square, (width, model), (2 * small_half, model)),
        halves_at(0, (0, rows), (0, width), 0, 0, 0, 0, rows)
        + halves_at(0, (0, rows), (width, 2 * width), 1, 0, 0, 0, rows)
        + halves_at(2, (out_half, tail_start), (0, width), 2, 0, 0, 1, value_half)
        + halves_at(2, (out_half, tail_start), (width, 2 * width), 2, rows, 0, 1, value_half)
        + halves_at(2, (0, out_half), (0, model), 3, 0, 0, 1, out_half)
        + halves_at(2, (tail_start, tail_start + small_half), (0, model), 4, 0, 0, 1, small_half),
    )
    up_rows = hidden // model
    return (
        layer_out,
        grad_input,
        grad_q,
        grad_k,
        grad_v,
        tail[0, :width],
        tail[0, width:],
        grad_out,
        tail[up_rows + 1],
        tail[up_rows + 2],
        tail[up_rows + 3],
        grad_up,
        tail[1 : up_rows + 1].reshape(-1),
        grad_down,
        tail[up_rows + 4],
        tail[up_rows + 5],
        tail[up_rows + 6],
    )


def solution(mesh):
    placed = (
        P("dp", None),
        P("dp", None),
        P("dp", None),
        P(None, "tensor"),
        P(None, "tensor"),
        P(None, "tensor"),
        P("tensor"),
        P("tensor"),
        P("tensor", None),
        P(),
        P(),
        P(),
        P(None, "tensor"),
        P("tensor"),
        P("tensor", None),
        P(),
        P(),
        P(),
    )
    counts = (mesh.shape["dp"], mesh.shape["tensor"])

    def on_device(*args):
        return local(*counts, *args)

    return jax.shard_map(
        on_device,
        mesh=mesh,
        in_specs=placed,
        out_specs=(
            P("dp", None),
            P("dp", None),
            P(None, "tensor"),
            P(None, "tensor"),
            P(None, "tensor"),
            P("tensor"),
            P("tensor"),
            P("tensor", None),
            P(),
            P(),
            P(),
            P(None, "tensor"),
            P("tensor"),
            P("tensor", None),
            P(),
            P(),
            P(),
        ),
        check_vma=False,
    )
```

```python
import functools

import jax
import jax.numpy as jnp
from jax import lax
from jax.experimental import pallas as pl
from jax.experimental.pallas import tpu as pltpu
from jax.sharding import PartitionSpec as P

DH = 64
LANES = 128
QUERY_BLOCK = 256
ROW_BLOCK = 256
MIB = 1 << 20

score_scale = 0.125
norm_eps = 1e-05
far_negative = -1e30
log2_e = 1.4426950408889634


def contract(left_side, right_side, left_dim, right_dim):
    return lax.dot_general(
        left_side,
        right_side,
        (((left_dim,), (right_dim,)), ((), ())),
        preferred_element_type=jnp.float32,
    )


def sequence_ends(lengths_ref, count):
    ends = []
    total = jnp.int32(0)
    for at in range(count):
        total = total + lengths_ref[0, at]
        ends.append(total)
    return ends


def key_window(ends, first_row, rows):
    last_row = first_row + QUERY_BLOCK - 1
    start = jnp.int32(0)
    stop = jnp.int32(rows)
    for end in ends:
        start = jnp.where(end <= first_row, jnp.maximum(start, end), start)
        stop = jnp.where(end > last_row, jnp.minimum(stop, end), stop)
    start = (start // LANES) * LANES
    stop = ((stop + LANES - 1) // LANES) * LANES
    return start, stop


def window_bias(ends, first_row, key_start, width, key_axis):
    line = (1, QUERY_BLOCK) if key_axis == 0 else (QUERY_BLOCK, 1)
    whole = (width, QUERY_BLOCK) if key_axis == 0 else (QUERY_BLOCK, width)
    query_at = lax.broadcasted_iota(jnp.int32, line, 1 - key_axis) + first_row
    seq_start = jnp.zeros(line, jnp.int32)
    seq_stop = jnp.full(line, 1 << 30, jnp.int32)
    for end in ends:
        seq_start = jnp.where(query_at >= end, jnp.maximum(seq_start, end), seq_start)
        seq_stop = jnp.where(query_at < end, jnp.minimum(seq_stop, end), seq_stop)
    key_at = lax.broadcasted_iota(jnp.int32, whole, key_axis) + key_start
    seen = (key_at >= seq_start) & (key_at < seq_stop)
    bias = jnp.where(seen, 0.0, far_negative).astype(jnp.float32)
    return jnp.concatenate([bias, bias], axis=1 - key_axis)


def split_heads(block):
    lane = lax.broadcasted_iota(jnp.int32, block.shape, 1)
    wide = block.astype(jnp.float32)
    return jnp.concatenate(
        [jnp.where(lane < DH, wide, 0.0), jnp.where(lane < DH, 0.0, wide)], axis=0
    ).astype(jnp.bfloat16)


def merge_heads(stacked):
    rows = stacked.shape[0] // 2
    lane = lax.broadcasted_iota(jnp.int32, (rows, LANES), 1)
    return jnp.where(lane < DH, stacked[:rows], stacked[rows:]).astype(jnp.bfloat16)


def put_halves(moves, sent_far, kept_far, sums, mine):
    rows = sent_far.shape[0]
    for far, place in ((sent_far, 1 - mine), (kept_far, mine)):
        moves.out(sums.at[pl.ds(pl.multiple_of(place * rows, 8), rows), :], far)


def over_query_blocks(ends, rows, widths, body):
    @pl.loop(0, rows // QUERY_BLOCK)
    def _(block):
        first_row = pl.multiple_of(block * QUERY_BLOCK, QUERY_BLOCK)
        start, stop = key_window(ends, first_row, rows)
        span = stop - start
        lower = 0
        for width in widths:
            chosen = (span > lower) & (span <= width)
            key_start = pl.multiple_of(jnp.minimum(start, rows - width), LANES)
            pl.when(chosen)(functools.partial(body, block, first_row, key_start, width))
            lower = width


def row_mean(values):
    return jnp.mean(values, axis=-1, keepdims=True)


def standardize(values):
    centre = values - row_mean(values)
    rate = lax.rsqrt(row_mean(centre * centre) + norm_eps)
    return centre * rate, rate


def norm_back(upstream, unit, rate, gain):
    scaled = upstream * gain
    return rate * (scaled - row_mean(scaled) - unit * row_mean(scaled * unit))


def column_sum(member):
    return jnp.sum(member, axis=0, keepdims=True)


def row_blocks(rows):
    return [slice(at, at + ROW_BLOCK) for at in range(0, rows, ROW_BLOCK)]


class Moves:
    def __init__(self, semaphores):
        self.semaphores = semaphores
        self.used = 0
        self.outward = []

    def start(self, source, target):
        copy = pltpu.make_async_copy(source, target, self.semaphores.at[self.used])
        self.used += 1
        copy.start()
        return copy

    def out(self, source, target):
        self.outward.append(self.start(source, target))

    def finish(self):
        for copy in self.outward:
            copy.wait()


def attend_kernel(widths, seqs, *refs):
    (
        lengths_ref,
        tokens_far,
        q_weight_far,
        k_weight_far,
        v_weight_far,
        out_weight_far,
        q_bias_ref,
        v_bias_ref,
        queries_far,
        keys_far,
        values_far,
        context_far,
        totals_far,
        *parts_far,
        tokens_ref,
        q_weight_ref,
        k_weight_ref,
        v_weight_ref,
        out_weight_ref,
        queries_ref,
        keys_ref,
        values_ref,
        context_ref,
        total_ref,
        part_ref,
        semaphores,
    ) = refs
    rows = tokens_ref.shape[0]
    pairs = q_weight_ref.shape[1] // LANES
    moves = Moves(semaphores)
    tokens_in = moves.start(tokens_far, tokens_ref)
    weights_in = [
        moves.start(far, near)
        for far, near in (
            (q_weight_far, q_weight_ref),
            (k_weight_far, k_weight_ref),
            (v_weight_far, v_weight_ref),
            (out_weight_far, out_weight_ref),
        )
    ]
    tokens_in.wait()
    tokens = tokens_ref[...]
    for copy, weight_ref, bias, near, far in (
        (weights_in[0], q_weight_ref, q_bias_ref, queries_ref, queries_far),
        (weights_in[1], k_weight_ref, None, keys_ref, keys_far),
        (weights_in[2], v_weight_ref, v_bias_ref, values_ref, values_far),
    ):
        copy.wait()
        product = contract(tokens, weight_ref[...], 1, 0)
        if bias is not None:
            product = product + bias[...].reshape(1, -1)
        near[...] = product.astype(jnp.bfloat16)
        moves.out(near, far)
    ends = sequence_ends(lengths_ref, seqs)

    def body(block, first_row, key_start, width):
        bias = window_bias(ends, first_row, key_start, width, 1)
        for pair in range(pairs):
            lanes = slice(pair * LANES, (pair + 1) * LANES)
            both = split_heads(queries_ref[pl.ds(first_row, QUERY_BLOCK), lanes])
            keys = keys_ref[pl.ds(key_start, width), lanes]
            scores = contract(both, keys, 1, 1) * (score_scale * log2_e) + bias
            peak = jnp.max(scores, axis=1, keepdims=True)
            exponents = jnp.exp2(scores - peak)
            total = jnp.sum(exponents, axis=1, keepdims=True)
            spread = jnp.broadcast_to(peak + jnp.log2(total), (2 * QUERY_BLOCK, LANES))
            total_ref[pl.ds(block * pairs + pair, 1), :] = spread.T[0:1]
            probs = (exponents * (1.0 / total)).astype(jnp.bfloat16)
            context = contract(probs, values_ref[pl.ds(key_start, width), lanes], 1, 0)
            context_ref[pl.ds(first_row, QUERY_BLOCK), lanes] = merge_heads(context)

    over_query_blocks(ends, rows, widths, body)
    moves.out(context_ref, context_far)
    moves.out(total_ref, totals_far)
    weights_in[3].wait()
    for at, far in zip(row_blocks(rows), parts_far, strict=True):
        part_ref[at] = contract(context_ref[at], out_weight_ref[...], 1, 0)
        moves.out(part_ref.at[at], far)
    moves.finish()


def attend_back_kernel(widths, seqs, *refs):
    (
        lengths_ref,
        bits_ref,
        back_low_far,
        back_high_far,
        out_weight_far,
        queries_far,
        keys_far,
        values_far,
        totals_far,
        tokens_far,
        context_far,
        q_weight_far,
        k_weight_far,
        v_weight_far,
        small_ref,
        first_sent_far,
        first_kept_far,
        second_sent_far,
        second_kept_far,
        *parts_far,
        back_attn_ref,
        out_weight_ref,
        queries_ref,
        keys_ref,
        values_ref,
        total_ref,
        tokens_ref,
        context_ref,
        q_weight_ref,
        k_weight_ref,
        v_weight_ref,
        part_ref,
        first_pack_ref,
        second_pack_ref,
        back_context_ref,
        back_all_ref,
        back_keys_ref,
        back_values_ref,
        semaphores,
    ) = refs
    rows, model = tokens_ref.shape
    width_here = q_weight_ref.shape[1]
    pairs = width_here // LANES
    half_rows = rows // 2
    moves = Moves(semaphores)
    early = [
        moves.start(far, near)
        for far, near in (
            (out_weight_far, out_weight_ref),
            (back_low_far, back_attn_ref.at[:half_rows]),
            (back_high_far, back_attn_ref.at[half_rows:]),
            (queries_far, queries_ref),
            (keys_far, keys_ref),
            (values_far, values_ref),
            (totals_far, total_ref),
        )
    ]
    late = [
        moves.start(far, near)
        for far, near in (
            (tokens_far, tokens_ref),
            (context_far, context_ref),
            (q_weight_far, q_weight_ref),
            (k_weight_far, k_weight_ref),
            (v_weight_far, v_weight_ref),
        )
    ]
    back_keys_ref[...] = jnp.zeros_like(back_keys_ref)
    back_values_ref[...] = jnp.zeros_like(back_values_ref)
    for copy in early:
        copy.wait()
    back_context_ref[...] = contract(back_attn_ref[...], out_weight_ref[...], 1, 1).astype(
        jnp.bfloat16
    )
    ends = sequence_ends(lengths_ref, seqs)

    def body(block, first_row, key_start, width):
        bias = window_bias(ends, first_row, key_start, width, 0)
        for pair in range(pairs):
            lanes = slice(pair * LANES, (pair + 1) * LANES)
            both = split_heads(queries_ref[pl.ds(first_row, QUERY_BLOCK), lanes])
            back_both = split_heads(back_context_ref[pl.ds(first_row, QUERY_BLOCK), lanes])
            keys = keys_ref[pl.ds(key_start, width), lanes]
            values = values_ref[pl.ds(key_start, width), lanes]
            scores = contract(keys, both, 1, 1) * (score_scale * log2_e) + bias
            probs = jnp.exp2(scores - total_ref[pl.ds(block * pairs + pair, 1), :])
            back_probs = contract(values, back_both, 1, 1)
            inner = jnp.sum(back_probs * probs, axis=0, keepdims=True)
            back_scores = (probs * (back_probs - inner) * score_scale).astype(jnp.bfloat16)
            back_values_ref[pl.ds(key_start, width), lanes] += contract(
                probs.astype(jnp.bfloat16), back_both, 1, 0
            )
            back_keys_ref[pl.ds(key_start, width), lanes] += contract(back_scores, both, 1, 0)
            back_queries = contract(back_scores, keys, 0, 0)
            back_all_ref[pl.ds(first_row, QUERY_BLOCK), lanes] = merge_heads(back_queries)

    over_query_blocks(ends, rows, widths, body)
    for copy in late:
        copy.wait()
    back_all_ref[:, width_here : 2 * width_here] = back_keys_ref[...].astype(jnp.bfloat16)
    back_all_ref[:, 2 * width_here :] = back_values_ref[...].astype(jnp.bfloat16)
    tokens = tokens_ref[...]
    first_pack_ref[...] = contract(tokens, back_all_ref[:, : 2 * width_here], 0, 0)
    put_halves(moves, first_sent_far, first_kept_far, first_pack_ref, bits_ref[0, 0])
    grad_values = contract(tokens, back_all_ref[:, 2 * width_here :], 0, 0)
    grad_out = contract(context_ref[...], back_attn_ref[...], 0, 0)
    out_half, value_half, small_half = width_here // 2, model // 4, small_ref.shape[0] // 2
    top = 0
    for at in range(2):
        second_pack_ref[top : top + out_half, :] = grad_out[at * out_half : (at + 1) * out_half]
        top += out_half
        for side in range(2):
            start = side * (model // 2) + at * value_half
            second_pack_ref[
                top : top + value_half, side * width_here : (side + 1) * width_here
            ] = grad_values[start : start + value_half]
        top += value_half
        second_pack_ref[top : top + small_half, :] = small_ref[
            at * small_half : (at + 1) * small_half
        ]
        if at == 0:
            for side in range(2):
                member = back_all_ref[:, 2 * side * width_here : (2 * side + 1) * width_here]
                second_pack_ref[top : top + 1, side * width_here : (side + 1) * width_here] = (
                    column_sum(member.astype(jnp.float32))
                )
        top += small_half
    put_halves(moves, second_sent_far, second_kept_far, second_pack_ref, bits_ref[0, 1])
    for at, far in zip(row_blocks(rows), parts_far, strict=True):
        part_ref[at] = (
            contract(back_all_ref[at, :width_here], q_weight_ref[...], 1, 1)
            + contract(back_all_ref[at, width_here : 2 * width_here], k_weight_ref[...], 1, 1)
            + contract(back_all_ref[at, 2 * width_here :], v_weight_ref[...], 1, 1)
        )
        moves.out(part_ref.at[at], far)
    moves.finish()


def feed_kernel(first_row, *refs):
    (
        tokens_far,
        *own_fars,
        out_bias_ref,
        gain_ref,
        shift_ref,
        up_weight_ref,
        up_bias_ref,
        down_weight_ref,
        first_sum_far,
        first_low_far,
        active_far,
        part_low_far,
        part_high_far,
        tokens_ref,
        own_ref,
        first_sum_ref,
        first_low_ref,
        active_ref,
        part_ref,
        semaphores,
    ) = refs
    rows = own_ref.shape[0]
    own_fars, other_refs = own_fars[: len(own_fars) // 2], own_fars[len(own_fars) // 2 :]
    moves = Moves(semaphores)
    arriving = []
    for at, own_far in zip(row_blocks(rows), own_fars, strict=True):
        there = slice(first_row + at.start, first_row + at.stop)
        arriving.append(
            (
                moves.start(own_far, own_ref.at[at]),
                moves.start(tokens_far.at[there], tokens_ref.at[at]),
            )
        )
    for at, copies, other_ref, part_far in zip(
        row_blocks(rows), arriving, other_refs, (part_low_far, part_high_far), strict=True
    ):
        for copy in copies:
            copy.wait()
        first_sum = (
            tokens_ref[at].astype(jnp.float32)
            + (own_ref[at] + other_ref[...])
            + out_bias_ref[...].reshape(1, -1)
        )
        first_sum_ref[at] = first_sum
        moves.out(first_sum_ref.at[at], first_sum_far.at[at])
        unit, unused = standardize(first_sum)
        first_low = (
            unit * gain_ref[...].reshape(1, -1) + shift_ref[...].reshape(1, -1)
        ).astype(jnp.bfloat16)
        first_low_ref[at] = first_low
        moves.out(first_low_ref.at[at], first_low_far.at[at])
        inner = contract(first_low, up_weight_ref[...], 1, 0) + up_bias_ref[...].reshape(1, -1)
        active = (inner * (0.5 * (1.0 + lax.erf(inner * 0.7071067811865476)))).astype(
            jnp.bfloat16
        )
        active_ref[at] = active
        moves.out(active_ref.at[at], active_far.at[at])
        part_ref[at] = contract(active, down_weight_ref[...], 1, 0)
        moves.out(part_ref.at[at], part_far)
    moves.finish()


def second_norm_kernel(first_row, last, *refs):
    refs = list(refs)
    if last:
        bits_ref, active_low_far, active_high_far, back_low_far, layer_before_far = refs[:5]
        del refs[:5]
    (
        first_sum_far,
        own_low_far,
        own_high_far,
        *other_refs,
        cotangent_far,
        first_gain_ref,
        first_shift_ref,
        down_bias_ref,
        gain_ref,
        shift_ref,
    ) = refs[:11]
    layer_far, back_second_far, back_down_far, sums_ref = refs[11:15]
    rest = refs[15:]
    if last:
        grads_far, rest = rest[:4], rest[4:]
    first_sum_ref, own_ref, cotangent_ref, layer_ref, back_second_ref, back_down_ref, *rest = rest
    semaphores = rest[-1]
    rows = own_ref.shape[0]
    moves = Moves(semaphores)
    arriving = []
    for at, own_far in zip(row_blocks(rows), (own_low_far, own_high_far), strict=True):
        there = slice(first_row + at.start, first_row + at.stop)
        arriving.append(
            (
                moves.start(own_far, own_ref.at[at]),
                moves.start(first_sum_far.at[at], first_sum_ref.at[at]),
                moves.start(cotangent_far.at[there], cotangent_ref.at[at]),
            )
        )
    if last:
        active_ref, back_before_ref, grads_ref, unused = rest
        early = [
            moves.start(active_low_far, active_ref.at[:rows]),
            moves.start(back_low_far, back_before_ref),
        ]
        late = moves.start(active_high_far, active_ref.at[rows:])
    bias_sum, gain_sum, shift_sum = 0.0, 0.0, 0.0
    gain = gain_ref[...].reshape(1, -1)
    shift = shift_ref[...].reshape(1, -1)
    for at, copies, other_ref in zip(row_blocks(rows), arriving, other_refs, strict=True):
        for copy in copies:
            copy.wait()
        unit, unused = standardize(first_sum_ref[at])
        first = unit * first_gain_ref[...].reshape(1, -1) + first_shift_ref[...].reshape(1, -1)
        second_sum = first + (own_ref[at] + other_ref[...]) + down_bias_ref[...].reshape(1, -1)
        unit, rate = standardize(second_sum)
        layer_ref[at] = (unit * gain + shift).astype(jnp.bfloat16)
        there = slice(first_row + at.start, first_row + at.stop)
        moves.out(layer_ref.at[at], layer_far.at[there])
        upstream = cotangent_ref[at].astype(jnp.float32)
        back_second = norm_back(upstream, unit, rate, gain)
        back_second_ref[at] = back_second
        moves.out(back_second_ref.at[at], back_second_far.at[at])
        back_down_ref[at] = back_second.astype(jnp.bfloat16)
        moves.out(back_down_ref.at[at], back_down_far.at[at])
        bias_sum += column_sum(back_second)
        gain_sum += column_sum(upstream * unit)
        shift_sum += column_sum(upstream)
    put_sums(sums_ref, bias_sum, gain_sum, shift_sum)
    if last:
        for copy in early:
            copy.wait()
        late.wait()
        height = grads_ref.shape[1]
        for slot, (block, same) in enumerate(((0, False), (1, False), (0, True), (1, True))):
            mine = bits_ref[0, block]
            place = mine if same else 1 - mine
            units = pl.ds(pl.multiple_of((2 * block + place) * height, LANES), height)
            grads_ref[slot] = contract(
                active_ref[:rows, units], back_before_ref[...], 0, 0
            ) + contract(active_ref[rows:, units], back_down_ref[...], 0, 0)
            moves.out(grads_ref.at[slot], grads_far[slot])
    moves.finish()


def put_sums(sums_ref, *members):
    sums_ref[...] = jnp.zeros_like(sums_ref)
    for at, member in enumerate(members):
        sums_ref[at : at + 1, :] = member


def feed_back_kernel(last, *refs):
    refs = list(refs)
    if last:
        bits_ref, first_before_far, inner_before_far = refs[:3]
        del refs[:3]
    (
        back_down_far,
        first_low_far,
        up_weight_ref,
        up_bias_ref,
        down_weight_ref,
        part_low_far,
        part_high_far,
        inner_far,
        sums_ref,
        *rest,
    ) = refs
    if last:
        grads_far, rest = rest[:4], rest[4:]
    back_down_ref, first_low_ref, part_ref, inner_ref, *rest = rest
    semaphores = rest[-1]
    rows = back_down_ref.shape[0]
    moves = Moves(semaphores)
    arriving = [
        (
            moves.start(first_low_far.at[at], first_low_ref.at[at]),
            moves.start(back_down_far.at[at], back_down_ref.at[at]),
        )
        for at in row_blocks(rows)
    ]
    if last:
        first_before_ref, inner_before_ref, grads_ref, unused = rest
        late = [
            moves.start(first_before_far, first_before_ref),
            moves.start(inner_before_far, inner_before_ref),
        ]
    total = 0.0
    for at, copies, part_far in zip(
        row_blocks(rows), arriving, (part_low_far, part_high_far), strict=True
    ):
        for copy in copies:
            copy.wait()
        inner = contract(first_low_ref[at], up_weight_ref[...], 1, 0) + up_bias_ref[...].reshape(
            1, -1
        )
        slope = 0.5 * (1.0 + lax.erf(inner * 0.7071067811865476)) + inner * (
            0.3989422804014327 * jnp.exp(-0.5 * inner * inner)
        )
        back_active = contract(back_down_ref[at], down_weight_ref[...], 1, 1)
        back_inner = (back_active * slope).astype(jnp.bfloat16)
        inner_ref[at] = back_inner
        if not last:
            moves.out(inner_ref.at[at], inner_far.at[at])
        part_ref[at] = contract(back_inner, up_weight_ref[...], 1, 1)
        moves.out(part_ref.at[at], part_far)
        total += column_sum(back_inner.astype(jnp.float32))
    put_sums(sums_ref, total)
    if last:
        moves.out(inner_ref.at[:16], inner_far)
        for copy in late:
            copy.wait()
        height, columns = grads_ref.shape[1:]
        for slot, (block, same) in enumerate(((0, False), (1, False), (0, True), (1, True))):
            mine = bits_ref[0, block]
            place = mine if same else 1 - mine
            features = pl.ds(pl.multiple_of(place * height, LANES), height)
            units = slice(block * columns, (block + 1) * columns)
            grads_ref[slot] = contract(
                first_before_ref[:, features], inner_before_ref[:, units], 0, 0
            ) + contract(first_low_ref[:, features], inner_ref[:, units], 0, 0)
            moves.out(grads_ref.at[slot], grads_far[slot])
    moves.finish()


def first_norm_kernel(*refs):
    (
        first_sum_far,
        own_low_far,
        own_high_far,
        *other_refs,
        back_second_far,
        gain_ref,
        back_first_far,
        back_attn_far,
        sums_ref,
        first_sum_ref,
        own_ref,
        back_second_ref,
        back_first_ref,
        back_attn_ref,
        semaphores,
    ) = refs
    rows = own_ref.shape[0]
    moves = Moves(semaphores)
    arriving = [
        (
            moves.start(own_far, own_ref.at[at]),
            moves.start(first_sum_far.at[at], first_sum_ref.at[at]),
            moves.start(back_second_far.at[at], back_second_ref.at[at]),
        )
        for at, own_far in zip(row_blocks(rows), (own_low_far, own_high_far), strict=True)
    ]
    bias_sum, gain_sum, shift_sum = 0.0, 0.0, 0.0
    gain = gain_ref[...].reshape(1, -1)
    for at, copies, other_ref in zip(row_blocks(rows), arriving, other_refs, strict=True):
        for copy in copies:
            copy.wait()
        unit, rate = standardize(first_sum_ref[at])
        upstream = (own_ref[at] + other_ref[...]) + back_second_ref[at]
        back_first_sum = norm_back(upstream, unit, rate, gain)
        back_first_ref[at] = back_first_sum
        moves.out(back_first_ref.at[at], back_first_far.at[at])
        back_attn_ref[at] = back_first_sum.astype(jnp.bfloat16)
        moves.out(back_attn_ref.at[at], back_attn_far.at[at])
        bias_sum += column_sum(back_first_sum)
        gain_sum += column_sum(upstream * unit)
        shift_sum += column_sum(upstream)
    put_sums(sums_ref, bias_sum, gain_sum, shift_sum)
    moves.finish()


def input_kernel(blocks, *refs):
    own_fars, other_refs = refs[:blocks], refs[blocks : 2 * blocks]
    *first_fars, grad_far, own_ref, first_ref, grad_ref, semaphores = refs[2 * blocks :]
    rows = own_ref.shape[0]
    moves = Moves(semaphores)
    arriving = []
    per = blocks // len(first_fars)
    for block, (at, own_far) in enumerate(zip(row_blocks(rows), own_fars, strict=True)):
        inside = slice(block % per * ROW_BLOCK, (block % per + 1) * ROW_BLOCK)
        arriving.append(
            (
                moves.start(own_far, own_ref.at[at]),
                moves.start(first_fars[block // per].at[inside], first_ref.at[at]),
            )
        )
    for at, copies, other_ref in zip(row_blocks(rows), arriving, other_refs, strict=True):
        for copy in copies:
            copy.wait()
        grad_ref[at] = ((own_ref[at] + other_ref[...]) + first_ref[at]).astype(jnp.bfloat16)
        moves.out(grad_ref.at[at], grad_far.at[at])
    moves.finish()


def struct(shape, dtype):
    return jax.ShapeDtypeStruct(shape, dtype)


def in_smem():
    return pl.BlockSpec(memory_space=pltpu.SMEM)


def in_vmem():
    return pl.BlockSpec(memory_space=pltpu.VMEM)


def in_hbm():
    return pl.BlockSpec(memory_space=pltpu.HBM)


def key_widths(rows):
    return tuple(width for width in (512, 768) if width < rows) + (rows,)


def call(body, name, operands, outs, scratch=(), near=(), near_outs=(), scalars=0, room=4, aliases=None):
    bytes_here = sum(
        jnp.dtype(dtype).itemsize * functools.reduce(lambda a, b: a * b, shape) for shape, dtype in scratch
    )
    specs = [
        in_smem() if at < scalars else in_vmem() if at in near else in_hbm()
        for at in range(len(operands))
    ]
    return pl.pallas_call(
        body,
        out_shape=tuple(struct(*out) for out in outs),
        in_specs=specs,
        out_specs=tuple(in_vmem() if at in near_outs else in_hbm() for at in range(len(outs))),
        scratch_shapes=[pltpu.VMEM(*shape) for shape in scratch]
        + [pltpu.SemaphoreType.DMA((48,))],
        input_output_aliases=aliases or {},
        compiler_params=pltpu.CompilerParams(vmem_limit_bytes=bytes_here + room * MIB),
        name=name,
    )(*operands)


low, exact = jnp.bfloat16, jnp.float32


def place_kernel(moves, starts_ref, *refs):
    copies = []
    inputs = 1 + max(source for source, *unused in moves)
    for at, (source, rows, columns, target, row_start, column_start) in enumerate(moves):
        start = row_start(starts_ref) if callable(row_start) else row_start
        size = rows[1] - rows[0]
        copies.append(
            pltpu.make_async_copy(
                refs[source].at[pl.ds(rows[0], size), pl.ds(columns[0], columns[1] - columns[0])],
                refs[inputs + target].at[
                    pl.ds(pl.multiple_of(start, 8), size),
                    pl.ds(column_start, columns[1] - columns[0]),
                ],
                refs[-1].at[at],
            )
        )
    for copy in copies:
        copy.start()
    for copy in copies:
        copy.wait()


def place_blocks(starts, operands, shapes, moves, name):
    anywhere = pl.BlockSpec(memory_space=pl.ANY)
    return pl.pallas_call(
        functools.partial(place_kernel, moves),
        out_shape=tuple(struct(shape, jnp.float32) for shape in shapes),
        in_specs=[in_smem()] + [in_vmem()] * len(operands),
        out_specs=(anywhere,) * len(shapes),
        scratch_shapes=[pltpu.SemaphoreType.DMA((len(moves),))],
        compiler_params=pltpu.CompilerParams(vmem_limit_bytes=4 * MIB),
        name=name,
    )(starts, *operands)


def at_bit(rows, bit, same):
    def first(bits_ref):
        return (bits_ref[0, bit] if same else 1 - bits_ref[0, bit]) * rows

    return first


def swap_cores(value, tensor_count):
    return lax.ppermute(value, "tensor", [(i, i ^ 1) for i in range(tensor_count)])


class Ring:
    def __init__(self, count, place):
        self.count = count
        self.place = place
        stride = count // 4
        self.low_bits = stride.bit_length() - 1
        self.inward, self.across, self.outward = [], [], []
        for low in range(stride):
            line = [low + stride * at for at in range(4)]
            self.inward += [(line[0], line[1]), (line[3], line[2])]
            self.across += [(line[1], line[2]), (line[2], line[1])]
            self.outward += [(line[1], line[0]), (line[2], line[3])]
        self.is_middle = (place // stride == 1) | (place // stride == 2)

    def swap(self, value, bit):
        return lax.ppermute(value, "dp", [(i, i ^ (1 << bit)) for i in range(self.count)])

    def mine(self, bit):
        return (self.place >> bit) & 1

    def half(self, value, bit, same):
        rows = value.shape[0] // 2
        mine = self.mine(bit)
        return lax.dynamic_slice_in_dim(value, (mine if same else 1 - mine) * rows, rows, 0)


class Chunk:
    def __init__(self, ring, bits, first_bit, sent, kept):
        self.ring = ring
        self.bits = bits
        self.first_bit = first_bit
        self.second_bit = 1 - first_bit
        self.held = (kept,)
        self.arriving = None
        self.sent = sent
        self.step = 0

    def inputs(self):
        return self.held + (() if self.arriving is None else (self.arriving,))

    def join(self, value, arriving, bit):
        rows, columns = value.shape
        [joined] = place_blocks(
            self.bits,
            (value, arriving),
            ((2 * rows, columns),),
            (
                (0, (0, rows), (0, columns), 0, at_bit(rows, bit, True), 0),
                (1, (0, rows), (0, columns), 0, at_bit(rows, bit, False), 0),
            ),
            "join",
        )
        return joined

    def advance(self, inputs):
        ring = self.ring
        step = self.step
        self.step += 1
        if step == 0:
            self.arriving = ring.swap(self.sent, self.first_bit)
            return None
        if step == 1:
            kept, arrived = inputs
            bit = self.second_bit
            sent = ring.half(kept, bit, False) + ring.half(arrived, bit, False)
            self.held = (ring.half(kept, bit, True), ring.half(arrived, bit, True))
            self.arriving = ring.swap(sent, bit)
            return sent
        if step == 2:
            value = (inputs[0] + inputs[1]) + inputs[2]
            for bit in range(2, ring.low_bits):
                value = value + ring.swap(value, bit)
            self.held = (value,)
            self.arriving = lax.ppermute(value, "dp", ring.inward)
            return value
        value, arrived = inputs
        if step == 3:
            value = value + arrived
            self.arriving = lax.ppermute(value, "dp", ring.across)
        elif step == 4:
            value = value + arrived
            self.arriving = lax.ppermute(value, "dp", ring.outward)
        elif step == 5:
            value = jnp.where(ring.is_middle, value, arrived)
            self.arriving = ring.swap(value, self.second_bit)
        else:
            value = self.join(value, arrived, self.second_bit)
            self.arriving = ring.swap(value, self.first_bit)
        self.held = (value,)
        return value


class Sequence:
    def __init__(self):
        self.last = None

    def after(self, values):
        if self.last is None:
            return tuple(values)
        held = lax.optimization_barrier((*values, self.last))
        return held[:-1]

    def ran(self, result):
        if result is not None:
            self.last = result


def local(
    dp_count,
    tensor_count,
    tokens_in,
    cotangent,
    seq_lengths,
    q_weight,
    k_weight,
    v_weight,
    q_bias,
    v_bias,
    out_weight,
    out_bias,
    first_gain,
    first_shift,
    up_weight,
    up_bias,
    down_weight,
    down_bias,
    second_gain,
    second_shift,
):
    place = lax.axis_index("dp")
    ring = Ring(dp_count, place)
    bits = jnp.stack([ring.mine(0), ring.mine(1)]).reshape(1, 2)
    model = q_weight.shape[0]
    width = q_weight.shape[1]
    hidden = up_weight.shape[1]
    rows = tokens_in.shape[0]
    half_rows = rows // 2
    block = (ROW_BLOCK, model)
    blocks = rows // ROW_BLOCK
    half_blocks = blocks // 2
    half_exact = ((half_rows, model), exact)
    half_low = ((half_rows, model), low)
    half_active = ((half_rows, hidden), low)
    rows_width = ((rows, width), low)
    into = ((model, width), low)
    outof = ((width, model), low)
    seqs = seq_lengths.shape[1]
    widths = key_widths(rows)
    totals_shape = ((rows // QUERY_BLOCK * (width // LANES), 2 * QUERY_BLOCK), exact)
    queries, keys, values, context, totals, *attn_parts = call(
        functools.partial(attend_kernel, widths, seqs),
        "attend",
        (seq_lengths, tokens_in, q_weight, k_weight, v_weight, out_weight, q_bias, v_bias),
        [rows_width] * 4 + [totals_shape] + [(block, exact)] * blocks,
        [((rows, model), low), into, into, into, outof]
        + [rows_width] * 4
        + [totals_shape, ((rows, model), exact)],
        near=(6, 7),
        scalars=1,
        room=8,
    )
    order = Sequence()

    def swapped(parts):
        return tuple(swap_cores(part, tensor_count) for part in parts)

    attn_others = swapped(attn_parts)
    fed = []
    for at in range(2):
        mine = slice(at * half_blocks, (at + 1) * half_blocks)
        fed.append(
            call(
                functools.partial(feed_kernel, at * half_rows),
                "feed",
                (tokens_in, *attn_parts[mine], *attn_others[mine])
                + (out_bias, first_gain, first_shift, up_weight, up_bias, down_weight),
                [half_exact, half_low, half_active] + [(block, exact)] * half_blocks,
                [half_low, half_exact, half_exact, half_low, half_active, half_exact],
                near=range(1 + half_blocks, 1 + 2 * half_blocks + 6),
            )
        )
    first_sums, first_lows, actives = zip(*[member[:3] for member in fed], strict=True)
    down_parts = [member[3:] for member in fed]
    down_others = [swapped(parts) for parts in down_parts]
    second_vectors = (first_gain, first_shift, down_bias, second_gain, second_shift)
    sums_shape = ((8, model), exact)

    def second_norm(at, before, scratch, extra_outs):
        lead = len(before)
        return call(
            functools.partial(second_norm_kernel, at * half_rows, at == 1),
            "second_norm",
            (*before, first_sums[at], *down_parts[at], *down_others[at], cotangent)
            + second_vectors,
            [((rows, model), low), half_exact, half_low, sums_shape] + extra_outs,
            [half_exact, half_exact, half_low, half_low, half_exact, half_low] + scratch,
            near=[*range(lead + 1 + half_blocks, lead + 1 + 2 * half_blocks)]
            + [*range(lead + 2 + 2 * half_blocks, lead + 7 + 2 * half_blocks)],
            near_outs=(3,),
            scalars=1 if before else 0,
            room=8,
            aliases={4: 0} if before else None,
        )

    layer_out, back_second, back_down, second_sums = second_norm(0, (), [], [])
    down_piece = (hidden // 4, model)
    layer_out, *rest = second_norm(
        1,
        (bits, *actives, back_down, layer_out),
        [((rows, hidden), low), half_low, ((4, *down_piece), exact)],
        [(down_piece, exact)] * 4,
    )
    back_seconds, back_downs = (back_second, rest[0]), (back_down, rest[1])
    second_sums = second_sums + rest[2]
    down_pieces = rest[3:]
    order.ran(down_pieces[0])
    chunks = {}

    def begin(name, pieces):
        chunks[name + "0"] = Chunk(ring, bits, 0, pieces[0], pieces[2])
        chunks[name + "1"] = Chunk(ring, bits, 1, pieces[1], pieces[3])

    def run(*names):
        for name in names:
            chunk = chunks[name]
            inputs = chunk.inputs()
            order.ran(chunk.advance(order.after(inputs) if chunk.step else inputs))

    begin("D", down_pieces)
    run("D1", "D0")
    up_piece = (model // 2, hidden // 2)

    def feed_back(at, before, inner_rows, scratch, extra_outs):
        [back_down] = order.after((back_downs[at],))
        lead = len(before)
        results = call(
            functools.partial(feed_back_kernel, at == 1),
            "feed_back",
            (*before, back_down, first_lows[at], up_weight, up_bias, down_weight),
            [(block, exact)] * half_blocks
            + [((inner_rows, hidden), low), ((8, hidden), exact)]
            + extra_outs,
            [half_low, half_low, half_exact, half_active] + scratch,
            near=range(lead + 2, lead + 5),
            near_outs=(half_blocks + 1,),
            scalars=1 if before else 0,
            room=6,
        )
        order.ran(results[half_blocks])
        return results

    fed_back = [feed_back(0, (), half_rows, [], [])]
    fed_back.append(
        feed_back(
            1,
            (bits, first_lows[0], fed_back[0][half_blocks]),
            16,
            [half_low, half_active, ((4, *up_piece), exact)],
            [(up_piece, exact)] * 4,
        )
    )
    up_sums = fed_back[0][half_blocks + 1] + fed_back[1][half_blocks + 1]
    begin("U", fed_back[1][half_blocks + 2 :])
    run("U1", "U0")
    normed_back = []
    for at in range(2):
        parts = fed_back[at][:half_blocks]
        others = order.after(swapped(parts))
        normed_back.append(
            call(
                first_norm_kernel,
                "first_norm_back",
                (first_sums[at], *parts, *others, back_seconds[at], first_gain),
                [half_exact, half_low, sums_shape],
                [half_exact, half_exact, half_exact, half_exact, half_low],
                near=[*range(1 + half_blocks, 1 + 2 * half_blocks), 2 + 2 * half_blocks],
                near_outs=(2,),
                room=8,
            )
        )
        order.ran(normed_back[-1][1])
        if at == 0:
            run("D1", "D0")
    back_first_sums, back_attns, norm_sums = zip(*normed_back, strict=True)
    small = jnp.concatenate(
        [
            jnp.zeros((1, model), jnp.float32),
            up_sums[0].reshape(-1, model),
            (norm_sums[0] + norm_sums[1])[:3],
            second_sums[:3],
        ]
    )
    small = jnp.pad(small, ((0, -small.shape[0] % 32), (0, 0)))
    back_attn = order.after(back_attns)
    first_piece = ((model // 2, 2 * width), exact)
    second_rows = (width + model // 2 + small.shape[0]) // 2
    second_piece = ((second_rows, model), exact)
    attn_pieces = call(
        functools.partial(attend_back_kernel, widths, seqs),
        "attend_back",
        (seq_lengths, bits, *back_attn, out_weight, queries, keys, values, totals, tokens_in)
        + (context, q_weight, k_weight, v_weight, small),
        [first_piece, first_piece, second_piece, second_piece] + [(block, exact)] * blocks,
        [((rows, model), low), outof, rows_width, rows_width, rows_width, totals_shape]
        + [((rows, model), low), rows_width, into, into, into, ((rows, model), exact)]
        + [((model, 2 * width), exact), ((2 * second_rows, model), exact), rows_width]
        + [((rows, 3 * width), low), ((rows, width), exact), ((rows, width), exact)],
        near=(14,),
        scalars=2,
        room=12,
    )
    input_parts = attn_pieces[4:]
    order.ran(attn_pieces[0])
    begin("A", [attn_pieces[at] for at in (0, 2, 1, 3)])
    run("A1", "U1", "D0", "D1", "U0", "A0")
    input_others = order.after(swapped(input_parts))
    [grad_input] = call(
        functools.partial(input_kernel, blocks),
        "grad_input",
        (*input_parts, *input_others, *back_first_sums),
        [((rows, model), low)],
        [((rows, model), exact), ((rows, model), exact), ((rows, model), low)],
        near=range(blocks, 2 * blocks),
    )
    order.ran(grad_input)
    run("U1", "D0", "A1", "D1", "D0", "U0", "A0", "U1", "D1", "D0", "A1", "U0", "A0", "U1", "D1")
    run("A1", "D0", "U0", "U1", "D1", "A0", "A1", "U0", "A0", "A1")

    def finish(name, shapes, moves):
        operands = ()
        for chunk in (chunks[name + "0"], chunks[name + "1"]):
            operands += order.after(chunk.inputs())
        results = place_blocks(bits, operands, shapes, moves, "place")
        order.ran(results[0])
        return results

    def halves_at(source, rows, columns, target, row_offset, column, bit, height):
        moves = []
        for same in (True, False):
            first = at_bit(height, bit, same)
            moves.append(
                (
                    source + (0 if same else 1),
                    rows,
                    columns,
                    target,
                    lambda ref, first=first: row_offset + first(ref),
                    column,
                )
            )
        return moves

    half = hidden // 2
    quarter = half // 2
    [grad_down] = finish(
        "D",
        ((hidden, model),),
        halves_at(0, (0, quarter), (0, model), 0, 0, 0, 0, quarter)
        + halves_at(2, (0, quarter), (0, model), 0, half, 0, 1, quarter),
    )
    run("A0", "U1", "U0", "A1", "A0")
    rows = model // 2
    [grad_up] = finish(
        "U",
        ((model, hidden),),
        halves_at(0, (0, rows), (0, half), 0, 0, 0, 0, rows)
        + halves_at(2, (0, rows), (0, half), 0, 0, half, 1, rows),
    )
    out_half, value_half = width // 2, model // 4
    tail_start = out_half + value_half
    small_half = small.shape[0] // 2
    square = (model, width)
    grad_q, grad_k, grad_v, grad_out, tail = finish(
        "A",
        (square, square, square, (width, model), (2 * small_half, model)),
        halves_at(0, (0, rows), (0, width), 0, 0, 0, 0, rows)
        + halves_at(0, (0, rows), (width, 2 * width), 1, 0, 0, 0, rows)
        + halves_at(2, (out_half, tail_start), (0, width), 2, 0, 0, 1, value_half)
        + halves_at(2, (out_half, tail_start), (width, 2 * width), 2, rows, 0, 1, value_half)
        + halves_at(2, (0, out_half), (0, model), 3, 0, 0, 1, out_half)
        + halves_at(2, (tail_start, tail_start + small_half), (0, model), 4, 0, 0, 1, small_half),
    )
    up_rows = hidden // model
    return (
        layer_out,
        grad_input,
        grad_q,
        grad_k,
        grad_v,
        tail[0, :width],
        tail[0, width:],
        grad_out,
        tail[up_rows + 1],
        tail[up_rows + 2],
        tail[up_rows + 3],
        grad_up,
        tail[1 : up_rows + 1].reshape(-1),
        grad_down,
        tail[up_rows + 4],
        tail[up_rows + 5],
        tail[up_rows + 6],
    )


def solution(mesh):
    placed = (
        P("dp", None),
        P("dp", None),
        P("dp", None),
        P(None, "tensor"),
        P(None, "tensor"),
        P(None, "tensor"),
        P("tensor"),
        P("tensor"),
        P("tensor", None),
        P(),
        P(),
        P(),
        P(None, "tensor"),
        P("tensor"),
        P("tensor", None),
        P(),
        P(),
        P(),
    )
    counts = (mesh.shape["dp"], mesh.shape["tensor"])

    def on_device(*args):
        return local(*counts, *args)

    return jax.shard_map(
        on_device,
        mesh=mesh,
        in_specs=placed,
        out_specs=(
            P("dp", None),
            P("dp", None),
            P(None, "tensor"),
            P(None, "tensor"),
            P(None, "tensor"),
            P("tensor"),
            P("tensor"),
            P("tensor", None),
            P(),
            P(),
            P(),
            P(None, "tensor"),
            P("tensor"),
            P("tensor", None),
            P(),
            P(),
            P(),
        ),
        check_vma=False,
    )
```

```python
import functools

import jax
import jax.numpy as jnp
from jax import lax
from jax.experimental import pallas as pl
from jax.experimental.pallas import tpu as pltpu
from jax.sharding import PartitionSpec as P

DH = 64
LANES = 128
QUERY_BLOCK = 256
ROW_BLOCK = 256
MIB = 1 << 20

score_scale = 0.125
norm_eps = 1e-05
far_negative = -1e30
log2_e = 1.4426950408889634


def contract(left_side, right_side, left_dim, right_dim):
    return lax.dot_general(
        left_side,
        right_side,
        (((left_dim,), (right_dim,)), ((), ())),
        preferred_element_type=jnp.float32,
    )


def sequence_ends(lengths_ref, count):
    ends = []
    total = jnp.int32(0)
    for at in range(count):
        total = total + lengths_ref[0, at]
        ends.append(total)
    return ends


def key_window(ends, first_row, rows):
    last_row = first_row + QUERY_BLOCK - 1
    start = jnp.int32(0)
    stop = jnp.int32(rows)
    for end in ends:
        start = jnp.where(end <= first_row, jnp.maximum(start, end), start)
        stop = jnp.where(end > last_row, jnp.minimum(stop, end), stop)
    start = (start // LANES) * LANES
    stop = ((stop + LANES - 1) // LANES) * LANES
    return start, stop


def window_bias(ends, first_row, key_start, width, key_axis):
    line = (1, QUERY_BLOCK) if key_axis == 0 else (QUERY_BLOCK, 1)
    whole = (width, QUERY_BLOCK) if key_axis == 0 else (QUERY_BLOCK, width)
    query_at = lax.broadcasted_iota(jnp.int32, line, 1 - key_axis) + first_row
    seq_start = jnp.zeros(line, jnp.int32)
    seq_stop = jnp.full(line, 1 << 30, jnp.int32)
    for end in ends:
        seq_start = jnp.where(query_at >= end, jnp.maximum(seq_start, end), seq_start)
        seq_stop = jnp.where(query_at < end, jnp.minimum(seq_stop, end), seq_stop)
    key_at = lax.broadcasted_iota(jnp.int32, whole, key_axis) + key_start
    seen = (key_at >= seq_start) & (key_at < seq_stop)
    bias = jnp.where(seen, 0.0, far_negative).astype(jnp.float32)
    return jnp.concatenate([bias, bias], axis=1 - key_axis)


def split_heads(block):
    lane = lax.broadcasted_iota(jnp.int32, block.shape, 1)
    wide = block.astype(jnp.float32)
    return jnp.concatenate(
        [jnp.where(lane < DH, wide, 0.0), jnp.where(lane < DH, 0.0, wide)], axis=0
    ).astype(jnp.bfloat16)


def merge_heads(stacked):
    rows = stacked.shape[0] // 2
    lane = lax.broadcasted_iota(jnp.int32, (rows, LANES), 1)
    return jnp.where(lane < DH, stacked[:rows], stacked[rows:]).astype(jnp.bfloat16)


def put_halves(moves, sent_far, kept_far, sums, mine):
    rows = sent_far.shape[0]
    for far, place in ((sent_far, 1 - mine), (kept_far, mine)):
        moves.out(sums.at[pl.ds(pl.multiple_of(place * rows, 8), rows), :], far)


def over_query_blocks(ends, rows, widths, body):
    @pl.loop(0, rows // QUERY_BLOCK)
    def _(block):
        first_row = pl.multiple_of(block * QUERY_BLOCK, QUERY_BLOCK)
        start, stop = key_window(ends, first_row, rows)
        span = stop - start
        lower = 0
        for width in widths:
            chosen = (span > lower) & (span <= width)
            key_start = pl.multiple_of(jnp.minimum(start, rows - width), LANES)
            pl.when(chosen)(functools.partial(body, block, first_row, key_start, width))
            lower = width


def row_mean(values):
    return jnp.mean(values, axis=-1, keepdims=True)


def standardize(values):
    centre = values - row_mean(values)
    rate = lax.rsqrt(row_mean(centre * centre) + norm_eps)
    return centre * rate, rate


def norm_back(upstream, unit, rate, gain):
    scaled = upstream * gain
    return rate * (scaled - row_mean(scaled) - unit * row_mean(scaled * unit))


def column_sum(member):
    return jnp.sum(member, axis=0, keepdims=True)


def row_blocks(rows):
    return [slice(at, at + ROW_BLOCK) for at in range(0, rows, ROW_BLOCK)]


class Moves:
    def __init__(self, semaphores):
        self.semaphores = semaphores
        self.used = 0
        self.outward = []

    def start(self, source, target):
        copy = pltpu.make_async_copy(source, target, self.semaphores.at[self.used])
        self.used += 1
        copy.start()
        return copy

    def out(self, source, target):
        self.outward.append(self.start(source, target))

    def finish(self):
        for copy in self.outward:
            copy.wait()


def attend_kernel(widths, seqs, *refs):
    (
        lengths_ref,
        tokens_far,
        q_weight_far,
        k_weight_far,
        v_weight_far,
        out_weight_far,
        q_bias_ref,
        v_bias_ref,
        queries_far,
        keys_far,
        values_far,
        context_far,
        totals_far,
        *parts_far,
        tokens_ref,
        q_weight_ref,
        k_weight_ref,
        v_weight_ref,
        out_weight_ref,
        queries_ref,
        keys_ref,
        values_ref,
        context_ref,
        total_ref,
        part_ref,
        semaphores,
    ) = refs
    rows = tokens_ref.shape[0]
    pairs = q_weight_ref.shape[1] // LANES
    moves = Moves(semaphores)
    tokens_in = moves.start(tokens_far, tokens_ref)
    weights_in = [
        moves.start(far, near)
        for far, near in (
            (q_weight_far, q_weight_ref),
            (k_weight_far, k_weight_ref),
            (v_weight_far, v_weight_ref),
            (out_weight_far, out_weight_ref),
        )
    ]
    tokens_in.wait()
    tokens = tokens_ref[...]
    for copy, weight_ref, bias, near, far in (
        (weights_in[0], q_weight_ref, q_bias_ref, queries_ref, queries_far),
        (weights_in[1], k_weight_ref, None, keys_ref, keys_far),
        (weights_in[2], v_weight_ref, v_bias_ref, values_ref, values_far),
    ):
        copy.wait()
        product = contract(tokens, weight_ref[...], 1, 0)
        if bias is not None:
            product = product + bias[...].reshape(1, -1)
        near[...] = product.astype(jnp.bfloat16)
        moves.out(near, far)
    ends = sequence_ends(lengths_ref, seqs)

    def body(block, first_row, key_start, width):
        bias = window_bias(ends, first_row, key_start, width, 1)
        for pair in range(pairs):
            lanes = slice(pair * LANES, (pair + 1) * LANES)
            both = split_heads(queries_ref[pl.ds(first_row, QUERY_BLOCK), lanes])
            keys = keys_ref[pl.ds(key_start, width), lanes]
            scores = contract(both, keys, 1, 1) * (score_scale * log2_e) + bias
            peak = jnp.max(scores, axis=1, keepdims=True)
            exponents = jnp.exp2(scores - peak)
            total = jnp.sum(exponents, axis=1, keepdims=True)
            spread = jnp.broadcast_to(peak + jnp.log2(total), (2 * QUERY_BLOCK, LANES))
            total_ref[pl.ds(block * pairs + pair, 1), :] = spread.T[0:1]
            probs = (exponents * (1.0 / total)).astype(jnp.bfloat16)
            context = contract(probs, values_ref[pl.ds(key_start, width), lanes], 1, 0)
            context_ref[pl.ds(first_row, QUERY_BLOCK), lanes] = merge_heads(context)

    over_query_blocks(ends, rows, widths, body)
    moves.out(context_ref, context_far)
    moves.out(total_ref, totals_far)
    weights_in[3].wait()
    for at, far in zip(row_blocks(rows), parts_far, strict=True):
        part_ref[at] = contract(context_ref[at], out_weight_ref[...], 1, 0)
        moves.out(part_ref.at[at], far)
    moves.finish()


def attend_back_kernel(widths, seqs, *refs):
    (
        lengths_ref,
        back_low_far,
        back_high_far,
        out_weight_far,
        queries_far,
        keys_far,
        values_far,
        totals_far,
        back_all_far,
        back_attn_ref,
        out_weight_ref,
        queries_ref,
        keys_ref,
        values_ref,
        total_ref,
        back_context_ref,
        back_all_ref,
        back_keys_ref,
        back_values_ref,
        semaphores,
    ) = refs
    rows, width_here = queries_ref.shape
    pairs = width_here // LANES
    half_rows = rows // 2
    moves = Moves(semaphores)
    early = [
        moves.start(far, near)
        for far, near in (
            (out_weight_far, out_weight_ref),
            (back_low_far, back_attn_ref.at[:half_rows]),
            (back_high_far, back_attn_ref.at[half_rows:]),
        )
    ]
    late = [
        moves.start(far, near)
        for far, near in (
            (queries_far, queries_ref),
            (keys_far, keys_ref),
            (values_far, values_ref),
            (totals_far, total_ref),
        )
    ]
    back_keys_ref[...] = jnp.zeros_like(back_keys_ref)
    back_values_ref[...] = jnp.zeros_like(back_values_ref)
    for copy in early:
        copy.wait()
    back_context_ref[...] = contract(back_attn_ref[...], out_weight_ref[...], 1, 1).astype(
        jnp.bfloat16
    )
    for copy in late:
        copy.wait()
    ends = sequence_ends(lengths_ref, seqs)

    def body(block, first_row, key_start, width):
        bias = window_bias(ends, first_row, key_start, width, 0)
        for pair in range(pairs):
            lanes = slice(pair * LANES, (pair + 1) * LANES)
            both = split_heads(queries_ref[pl.ds(first_row, QUERY_BLOCK), lanes])
            back_both = split_heads(back_context_ref[pl.ds(first_row, QUERY_BLOCK), lanes])
            keys = keys_ref[pl.ds(key_start, width), lanes]
            values = values_ref[pl.ds(key_start, width), lanes]
            scores = contract(keys, both, 1, 1) * (score_scale * log2_e) + bias
            probs = jnp.exp2(scores - total_ref[pl.ds(block * pairs + pair, 1), :])
            back_probs = contract(values, back_both, 1, 1)
            inner = jnp.sum(back_probs * probs, axis=0, keepdims=True)
            back_scores = (probs * (back_probs - inner) * score_scale).astype(jnp.bfloat16)
            back_values_ref[pl.ds(key_start, width), lanes] += contract(
                probs.astype(jnp.bfloat16), back_both, 1, 0
            )
            back_keys_ref[pl.ds(key_start, width), lanes] += contract(back_scores, both, 1, 0)
            back_queries = contract(back_scores, keys, 0, 0)
            back_all_ref[pl.ds(first_row, QUERY_BLOCK), lanes] = merge_heads(back_queries)

    over_query_blocks(ends, rows, widths, body)
    back_all_ref[:, width_here : 2 * width_here] = back_keys_ref[...].astype(jnp.bfloat16)
    back_all_ref[:, 2 * width_here :] = back_values_ref[...].astype(jnp.bfloat16)
    moves.out(back_all_ref, back_all_far)
    moves.finish()


def grad_attn_kernel(*refs):
    (
        bits_ref,
        tokens_far,
        back_all_far,
        context_far,
        back_low_far,
        back_high_far,
        small_ref,
        first_sent_far,
        first_kept_far,
        second_sent_far,
        second_kept_far,
        tokens_ref,
        back_all_ref,
        context_ref,
        back_attn_ref,
        first_pack_ref,
        second_pack_ref,
        semaphores,
    ) = refs
    rows, model = tokens_ref.shape
    width_here = context_ref.shape[1]
    half_rows = rows // 2
    moves = Moves(semaphores)
    arriving = [
        moves.start(far, near)
        for far, near in (
            (tokens_far, tokens_ref),
            (back_all_far, back_all_ref),
            (context_far, context_ref),
            (back_low_far, back_attn_ref.at[:half_rows]),
            (back_high_far, back_attn_ref.at[half_rows:]),
        )
    ]
    for copy in arriving[:2]:
        copy.wait()
    grads = contract(tokens_ref[...], back_all_ref[...], 0, 0)
    first_pack_ref[...] = grads[:, : 2 * width_here]
    put_halves(moves, first_sent_far, first_kept_far, first_pack_ref, bits_ref[0, 0])
    grad_values = grads[:, 2 * width_here :]
    for copy in arriving[2:]:
        copy.wait()
    grad_out = contract(context_ref[...], back_attn_ref[...], 0, 0)
    out_half, value_half, small_half = width_here // 2, model // 4, small_ref.shape[0] // 2
    top = 0
    for at in range(2):
        second_pack_ref[top : top + out_half, :] = grad_out[at * out_half : (at + 1) * out_half]
        top += out_half
        for side in range(2):
            start = side * (model // 2) + at * value_half
            second_pack_ref[
                top : top + value_half, side * width_here : (side + 1) * width_here
            ] = grad_values[start : start + value_half]
        top += value_half
        second_pack_ref[top : top + small_half, :] = small_ref[
            at * small_half : (at + 1) * small_half
        ]
        if at == 0:
            for side in range(2):
                member = back_all_ref[:, 2 * side * width_here : (2 * side + 1) * width_here]
                second_pack_ref[top : top + 1, side * width_here : (side + 1) * width_here] = (
                    column_sum(member.astype(jnp.float32))
                )
        top += small_half
    put_halves(moves, second_sent_far, second_kept_far, second_pack_ref, bits_ref[0, 1])
    moves.finish()


def input_part_kernel(*refs):
    (
        back_all_far,
        q_weight_far,
        k_weight_far,
        v_weight_far,
        *parts_far,
        back_all_ref,
        weights_ref,
        part_ref,
        semaphores,
    ) = refs
    width_here = q_weight_far.shape[1]
    moves = Moves(semaphores)
    arriving = [
        moves.start(far, weights_ref.at[:, at * width_here : (at + 1) * width_here])
        for at, far in enumerate((q_weight_far, k_weight_far, v_weight_far))
    ]
    blocks = row_blocks(back_all_ref.shape[0])
    arriving += [moves.start(back_all_far.at[at], back_all_ref.at[at]) for at in blocks]
    for copy in arriving:
        copy.wait()
    for at, far in zip(blocks, parts_far, strict=True):
        part_ref[at] = contract(back_all_ref[at], weights_ref[...], 1, 1)
        moves.out(part_ref.at[at], far)
    moves.finish()


def feed_kernel(first_row, *refs):
    (
        tokens_far,
        *own_fars,
        out_bias_ref,
        gain_ref,
        shift_ref,
        up_weight_ref,
        up_bias_ref,
        down_weight_ref,
        first_sum_far,
        first_low_far,
        active_far,
        part_low_far,
        part_high_far,
        tokens_ref,
        own_ref,
        first_sum_ref,
        first_low_ref,
        active_ref,
        part_ref,
        semaphores,
    ) = refs
    rows = own_ref.shape[0]
    own_fars, other_refs = own_fars[: len(own_fars) // 2], own_fars[len(own_fars) // 2 :]
    moves = Moves(semaphores)
    arriving = []
    for at, own_far in zip(row_blocks(rows), own_fars, strict=True):
        there = slice(first_row + at.start, first_row + at.stop)
        arriving.append(
            (
                moves.start(own_far, own_ref.at[at]),
                moves.start(tokens_far.at[there], tokens_ref.at[at]),
            )
        )
    for at, copies, other_ref, part_far in zip(
        row_blocks(rows), arriving, other_refs, (part_low_far, part_high_far), strict=True
    ):
        for copy in copies:
            copy.wait()
        first_sum = (
            tokens_ref[at].astype(jnp.float32)
            + (own_ref[at] + other_ref[...])
            + out_bias_ref[...].reshape(1, -1)
        )
        first_sum_ref[at] = first_sum
        moves.out(first_sum_ref.at[at], first_sum_far.at[at])
        unit, unused = standardize(first_sum)
        first_low = (
            unit * gain_ref[...].reshape(1, -1) + shift_ref[...].reshape(1, -1)
        ).astype(jnp.bfloat16)
        first_low_ref[at] = first_low
        moves.out(first_low_ref.at[at], first_low_far.at[at])
        inner = contract(first_low, up_weight_ref[...], 1, 0) + up_bias_ref[...].reshape(1, -1)
        active = (inner * (0.5 * (1.0 + lax.erf(inner * 0.7071067811865476)))).astype(
            jnp.bfloat16
        )
        active_ref[at] = active
        moves.out(active_ref.at[at], active_far.at[at])
        part_ref[at] = contract(active, down_weight_ref[...], 1, 0)
        moves.out(part_ref.at[at], part_far)
    moves.finish()


def second_norm_kernel(first_row, last, *refs):
    refs = list(refs)
    if last:
        bits_ref, active_low_far, active_high_far, back_low_far, layer_before_far = refs[:5]
        del refs[:5]
    (
        first_sum_far,
        own_low_far,
        own_high_far,
        *other_refs,
        cotangent_far,
        first_gain_ref,
        first_shift_ref,
        down_bias_ref,
        gain_ref,
        shift_ref,
    ) = refs[:11]
    layer_far, back_second_far, back_down_far, sums_ref = refs[11:15]
    rest = refs[15:]
    if last:
        grads_far, rest = rest[:4], rest[4:]
    first_sum_ref, own_ref, cotangent_ref, layer_ref, back_second_ref, back_down_ref, *rest = rest
    semaphores = rest[-1]
    rows = own_ref.shape[0]
    moves = Moves(semaphores)
    arriving = []
    for at, own_far in zip(row_blocks(rows), (own_low_far, own_high_far), strict=True):
        there = slice(first_row + at.start, first_row + at.stop)
        arriving.append(
            (
                moves.start(own_far, own_ref.at[at]),
                moves.start(first_sum_far.at[at], first_sum_ref.at[at]),
                moves.start(cotangent_far.at[there], cotangent_ref.at[at]),
            )
        )
    if last:
        active_ref, back_before_ref, grads_ref, unused = rest
        early = [
            moves.start(active_low_far, active_ref.at[:rows]),
            moves.start(back_low_far, back_before_ref),
        ]
        late = moves.start(active_high_far, active_ref.at[rows:])
    bias_sum, gain_sum, shift_sum = 0.0, 0.0, 0.0
    gain = gain_ref[...].reshape(1, -1)
    shift = shift_ref[...].reshape(1, -1)
    for at, copies, other_ref in zip(row_blocks(rows), arriving, other_refs, strict=True):
        for copy in copies:
            copy.wait()
        unit, unused = standardize(first_sum_ref[at])
        first = unit * first_gain_ref[...].reshape(1, -1) + first_shift_ref[...].reshape(1, -1)
        second_sum = first + (own_ref[at] + other_ref[...]) + down_bias_ref[...].reshape(1, -1)
        unit, rate = standardize(second_sum)
        layer_ref[at] = (unit * gain + shift).astype(jnp.bfloat16)
        there = slice(first_row + at.start, first_row + at.stop)
        moves.out(layer_ref.at[at], layer_far.at[there])
        upstream = cotangent_ref[at].astype(jnp.float32)
        back_second = norm_back(upstream, unit, rate, gain)
        back_second_ref[at] = back_second
        moves.out(back_second_ref.at[at], back_second_far.at[at])
        back_down_ref[at] = back_second.astype(jnp.bfloat16)
        moves.out(back_down_ref.at[at], back_down_far.at[at])
        bias_sum += column_sum(back_second)
        gain_sum += column_sum(upstream * unit)
        shift_sum += column_sum(upstream)
    put_sums(sums_ref, bias_sum, gain_sum, shift_sum)
    if last:
        for copy in early:
            copy.wait()
        late.wait()
        height = grads_ref.shape[1]
        for slot, (block, same) in enumerate(((0, False), (1, False), (0, True), (1, True))):
            mine = bits_ref[0, block]
            place = mine if same else 1 - mine
            units = pl.ds(pl.multiple_of((2 * block + place) * height, LANES), height)
            grads_ref[slot] = contract(
                active_ref[:rows, units], back_before_ref[...], 0, 0
            ) + contract(active_ref[rows:, units], back_down_ref[...], 0, 0)
            moves.out(grads_ref.at[slot], grads_far[slot])
    moves.finish()


def put_sums(sums_ref, *members):
    sums_ref[...] = jnp.zeros_like(sums_ref)
    for at, member in enumerate(members):
        sums_ref[at : at + 1, :] = member


def feed_back_kernel(last, *refs):
    refs = list(refs)
    if last:
        bits_ref, first_before_far, inner_before_far = refs[:3]
        del refs[:3]
    (
        back_down_far,
        first_low_far,
        up_weight_ref,
        up_bias_ref,
        down_weight_ref,
        part_low_far,
        part_high_far,
        inner_far,
        sums_ref,
        *rest,
    ) = refs
    if last:
        grads_far, rest = rest[:4], rest[4:]
    back_down_ref, first_low_ref, part_ref, inner_ref, *rest = rest
    semaphores = rest[-1]
    rows = back_down_ref.shape[0]
    moves = Moves(semaphores)
    arriving = [
        (
            moves.start(first_low_far.at[at], first_low_ref.at[at]),
            moves.start(back_down_far.at[at], back_down_ref.at[at]),
        )
        for at in row_blocks(rows)
    ]
    if last:
        first_before_ref, inner_before_ref, grads_ref, unused = rest
        late = [
            moves.start(first_before_far, first_before_ref),
            moves.start(inner_before_far, inner_before_ref),
        ]
    total = 0.0
    for at, copies, part_far in zip(
        row_blocks(rows), arriving, (part_low_far, part_high_far), strict=True
    ):
        for copy in copies:
            copy.wait()
        inner = contract(first_low_ref[at], up_weight_ref[...], 1, 0) + up_bias_ref[...].reshape(
            1, -1
        )
        slope = 0.5 * (1.0 + lax.erf(inner * 0.7071067811865476)) + inner * (
            0.3989422804014327 * jnp.exp(-0.5 * inner * inner)
        )
        back_active = contract(back_down_ref[at], down_weight_ref[...], 1, 1)
        back_inner = (back_active * slope).astype(jnp.bfloat16)
        inner_ref[at] = back_inner
        if not last:
            moves.out(inner_ref.at[at], inner_far.at[at])
        part_ref[at] = contract(back_inner, up_weight_ref[...], 1, 1)
        moves.out(part_ref.at[at], part_far)
        total += column_sum(back_inner.astype(jnp.float32))
    put_sums(sums_ref, total)
    if last:
        moves.out(inner_ref.at[:16], inner_far)
        for copy in late:
            copy.wait()
        height, columns = grads_ref.shape[1:]
        for slot, (block, same) in enumerate(((0, False), (1, False), (0, True), (1, True))):
            mine = bits_ref[0, block]
            place = mine if same else 1 - mine
            features = pl.ds(pl.multiple_of(place * height, LANES), height)
            units = slice(block * columns, (block + 1) * columns)
            grads_ref[slot] = contract(
                first_before_ref[:, features], inner_before_ref[:, units], 0, 0
            ) + contract(first_low_ref[:, features], inner_ref[:, units], 0, 0)
            moves.out(grads_ref.at[slot], grads_far[slot])
    moves.finish()


def first_norm_kernel(*refs):
    (
        first_sum_far,
        own_low_far,
        own_high_far,
        *other_refs,
        back_second_far,
        gain_ref,
        back_first_far,
        back_attn_far,
        sums_ref,
        first_sum_ref,
        own_ref,
        back_second_ref,
        back_first_ref,
        back_attn_ref,
        semaphores,
    ) = refs
    rows = own_ref.shape[0]
    moves = Moves(semaphores)
    arriving = [
        (
            moves.start(own_far, own_ref.at[at]),
            moves.start(first_sum_far.at[at], first_sum_ref.at[at]),
            moves.start(back_second_far.at[at], back_second_ref.at[at]),
        )
        for at, own_far in zip(row_blocks(rows), (own_low_far, own_high_far), strict=True)
    ]
    bias_sum, gain_sum, shift_sum = 0.0, 0.0, 0.0
    gain = gain_ref[...].reshape(1, -1)
    for at, copies, other_ref in zip(row_blocks(rows), arriving, other_refs, strict=True):
        for copy in copies:
            copy.wait()
        unit, rate = standardize(first_sum_ref[at])
        upstream = (own_ref[at] + other_ref[...]) + back_second_ref[at]
        back_first_sum = norm_back(upstream, unit, rate, gain)
        back_first_ref[at] = back_first_sum
        moves.out(back_first_ref.at[at], back_first_far.at[at])
        back_attn_ref[at] = back_first_sum.astype(jnp.bfloat16)
        moves.out(back_attn_ref.at[at], back_attn_far.at[at])
        bias_sum += column_sum(back_first_sum)
        gain_sum += column_sum(upstream * unit)
        shift_sum += column_sum(upstream)
    put_sums(sums_ref, bias_sum, gain_sum, shift_sum)
    moves.finish()


def input_kernel(blocks, *refs):
    own_fars, other_refs = refs[:blocks], refs[blocks : 2 * blocks]
    *first_fars, grad_far, own_ref, first_ref, grad_ref, semaphores = refs[2 * blocks :]
    rows = own_ref.shape[0]
    moves = Moves(semaphores)
    arriving = []
    per = blocks // len(first_fars)
    for block, (at, own_far) in enumerate(zip(row_blocks(rows), own_fars, strict=True)):
        inside = slice(block % per * ROW_BLOCK, (block % per + 1) * ROW_BLOCK)
        arriving.append(
            (
                moves.start(own_far, own_ref.at[at]),
                moves.start(first_fars[block // per].at[inside], first_ref.at[at]),
            )
        )
    for at, copies, other_ref in zip(row_blocks(rows), arriving, other_refs, strict=True):
        for copy in copies:
            copy.wait()
        grad_ref[at] = ((own_ref[at] + other_ref[...]) + first_ref[at]).astype(jnp.bfloat16)
        moves.out(grad_ref.at[at], grad_far.at[at])
    moves.finish()


def struct(shape, dtype):
    return jax.ShapeDtypeStruct(shape, dtype)


def in_smem():
    return pl.BlockSpec(memory_space=pltpu.SMEM)


def in_vmem():
    return pl.BlockSpec(memory_space=pltpu.VMEM)


def in_hbm():
    return pl.BlockSpec(memory_space=pltpu.HBM)


def key_widths(rows):
    return tuple(width for width in (512, 768) if width < rows) + (rows,)


def call(body, name, operands, outs, scratch=(), near=(), near_outs=(), scalars=0, room=4, aliases=None):
    bytes_here = sum(
        jnp.dtype(dtype).itemsize * functools.reduce(lambda a, b: a * b, shape) for shape, dtype in scratch
    )
    specs = [
        in_smem() if at < scalars else in_vmem() if at in near else in_hbm()
        for at in range(len(operands))
    ]
    return pl.pallas_call(
        body,
        out_shape=tuple(
            struct(*out) if at in near_outs else pltpu.HBM(*out) for at, out in enumerate(outs)
        ),
        in_specs=specs,
        out_specs=tuple(in_vmem() if at in near_outs else in_hbm() for at in range(len(outs))),
        scratch_shapes=[pltpu.VMEM(*shape) for shape in scratch]
        + [pltpu.SemaphoreType.DMA((48,))],
        input_output_aliases=aliases or {},
        compiler_params=pltpu.CompilerParams(vmem_limit_bytes=bytes_here + room * MIB),
        name=name,
    )(
        *(
            operand
            if at < scalars or at in near
            else pltpu.with_memory_space_constraint(operand, pltpu.HBM)
            for at, operand in enumerate(operands)
        )
    )


low, exact = jnp.bfloat16, jnp.float32


def place_kernel(moves, starts_ref, *refs):
    copies = []
    inputs = 1 + max(source for source, *unused in moves)
    for at, (source, rows, columns, target, row_start, column_start) in enumerate(moves):
        start = row_start(starts_ref) if callable(row_start) else row_start
        size = rows[1] - rows[0]
        copies.append(
            pltpu.make_async_copy(
                refs[source].at[pl.ds(rows[0], size), pl.ds(columns[0], columns[1] - columns[0])],
                refs[inputs + target].at[
                    pl.ds(pl.multiple_of(start, 8), size),
                    pl.ds(column_start, columns[1] - columns[0]),
                ],
                refs[-1].at[at],
            )
        )
    for copy in copies:
        copy.start()
    for copy in copies:
        copy.wait()


def place_blocks(starts, operands, shapes, moves, name):
    anywhere = pl.BlockSpec(memory_space=pl.ANY)
    return pl.pallas_call(
        functools.partial(place_kernel, moves),
        out_shape=tuple(struct(shape, jnp.float32) for shape in shapes),
        in_specs=[in_smem()] + [in_vmem()] * len(operands),
        out_specs=(anywhere,) * len(shapes),
        scratch_shapes=[pltpu.SemaphoreType.DMA((len(moves),))],
        compiler_params=pltpu.CompilerParams(vmem_limit_bytes=4 * MIB),
        name=name,
    )(starts, *operands)


def at_bit(rows, bit, same):
    def first(bits_ref):
        return (bits_ref[0, bit] if same else 1 - bits_ref[0, bit]) * rows

    return first


def swap_cores(value, tensor_count):
    return lax.ppermute(value, "tensor", [(i, i ^ 1) for i in range(tensor_count)])


class Ring:
    def __init__(self, count, place):
        self.count = count
        self.place = place
        stride = count // 4
        self.low_bits = stride.bit_length() - 1
        self.inward, self.across, self.outward = [], [], []
        for low in range(stride):
            line = [low + stride * at for at in range(4)]
            self.inward += [(line[0], line[1]), (line[3], line[2])]
            self.across += [(line[1], line[2]), (line[2], line[1])]
            self.outward += [(line[1], line[0]), (line[2], line[3])]
        self.is_middle = (place // stride == 1) | (place // stride == 2)

    def swap(self, value, bit):
        return lax.ppermute(value, "dp", [(i, i ^ (1 << bit)) for i in range(self.count)])

    def mine(self, bit):
        return (self.place >> bit) & 1

    def half(self, value, bit, same):
        rows = value.shape[0] // 2
        mine = self.mine(bit)
        return lax.dynamic_slice_in_dim(value, (mine if same else 1 - mine) * rows, rows, 0)


class Chunk:
    def __init__(self, ring, bits, first_bit, sent, kept):
        self.ring = ring
        self.bits = bits
        self.first_bit = first_bit
        self.second_bit = 1 - first_bit
        self.held = (kept,)
        self.arriving = None
        self.sent = sent
        self.step = 0

    def inputs(self):
        return self.held + (() if self.arriving is None else (self.arriving,))

    def join(self, value, arriving, bit):
        rows, columns = value.shape
        [joined] = place_blocks(
            self.bits,
            (value, arriving),
            ((2 * rows, columns),),
            (
                (0, (0, rows), (0, columns), 0, at_bit(rows, bit, True), 0),
                (1, (0, rows), (0, columns), 0, at_bit(rows, bit, False), 0),
            ),
            "join",
        )
        return joined

    def advance(self, inputs):
        ring = self.ring
        step = self.step
        self.step += 1
        if step == 0:
            self.arriving = ring.swap(self.sent, self.first_bit)
            return None
        if step == 1:
            kept, arrived = inputs
            bit = self.second_bit
            sent = ring.half(kept, bit, False) + ring.half(arrived, bit, False)
            self.held = (ring.half(kept, bit, True), ring.half(arrived, bit, True))
            self.arriving = ring.swap(sent, bit)
            return sent
        if step == 2:
            value = (inputs[0] + inputs[1]) + inputs[2]
            for bit in range(2, ring.low_bits):
                value = value + ring.swap(value, bit)
            self.held = (value,)
            self.arriving = lax.ppermute(value, "dp", ring.inward)
            return value
        value, arrived = inputs
        if step == 3:
            value = value + arrived
            self.arriving = lax.ppermute(value, "dp", ring.across)
        elif step == 4:
            value = value + arrived
            self.arriving = lax.ppermute(value, "dp", ring.outward)
        elif step == 5:
            value = jnp.where(ring.is_middle, value, arrived)
            self.arriving = ring.swap(value, self.second_bit)
        else:
            value = self.join(value, arrived, self.second_bit)
            self.arriving = ring.swap(value, self.first_bit)
        self.held = (value,)
        return value


class Sequence:
    def __init__(self):
        self.last = None

    def after(self, values):
        if self.last is None:
            return tuple(values)
        held = lax.optimization_barrier((*values, self.last))
        return held[:-1]

    def ran(self, result):
        if result is not None:
            self.last = result


plan = (
    "D1", "D0", "FB0", "FB1", "U1", "U0", "LN", "D1", "D0", "LN", "AB", "D0", "GA", "A1", "D1",
    "U0", "A0", "U1", "IP", "GI", "U0", "U1", "D0", "A1", "D1", "D0", "A0", "U1", "D1", "D0", "A1",
    "U0", "A0", "U1", "D1", "A1", "D0", "U0", "U1", "D1", "A0", "A1", "U0", "A0", "A1", "PD", "A0",
    "U1", "U0", "A1", "A0", "PU", "PA",
)


def local(
    dp_count,
    tensor_count,
    tokens_in,
    cotangent,
    seq_lengths,
    q_weight,
    k_weight,
    v_weight,
    q_bias,
    v_bias,
    out_weight,
    out_bias,
    first_gain,
    first_shift,
    up_weight,
    up_bias,
    down_weight,
    down_bias,
    second_gain,
    second_shift,
):
    place = lax.axis_index("dp")
    ring = Ring(dp_count, place)
    bits = jnp.stack([ring.mine(0), ring.mine(1)]).reshape(1, 2)
    model = q_weight.shape[0]
    width = q_weight.shape[1]
    hidden = up_weight.shape[1]
    rows = tokens_in.shape[0]
    half_rows = rows // 2
    block = (ROW_BLOCK, model)
    blocks = rows // ROW_BLOCK
    half_blocks = blocks // 2
    half_exact = ((half_rows, model), exact)
    half_low = ((half_rows, model), low)
    half_active = ((half_rows, hidden), low)
    rows_width = ((rows, width), low)
    into = ((model, width), low)
    outof = ((width, model), low)
    seqs = seq_lengths.shape[1]
    widths = key_widths(rows)
    totals_shape = ((rows // QUERY_BLOCK * (width // LANES), 2 * QUERY_BLOCK), exact)
    queries, keys, values, context, totals, *attn_parts = call(
        functools.partial(attend_kernel, widths, seqs),
        "attend",
        (seq_lengths, tokens_in, q_weight, k_weight, v_weight, out_weight, q_bias, v_bias),
        [rows_width] * 4 + [totals_shape] + [(block, exact)] * blocks,
        [((rows, model), low), into, into, into, outof]
        + [rows_width] * 4
        + [totals_shape, ((rows, model), exact)],
        near=(6, 7),
        scalars=1,
        room=8,
    )
    order = Sequence()

    def swapped(parts):
        return tuple(swap_cores(part, tensor_count) for part in parts)

    attn_others = swapped(attn_parts)
    fed = []
    for at in range(2):
        mine = slice(at * half_blocks, (at + 1) * half_blocks)
        fed.append(
            call(
                functools.partial(feed_kernel, at * half_rows),
                "feed",
                (tokens_in, *attn_parts[mine], *attn_others[mine])
                + (out_bias, first_gain, first_shift, up_weight, up_bias, down_weight),
                [half_exact, half_low, half_active] + [(block, exact)] * half_blocks,
                [half_low, half_exact, half_exact, half_low, half_active, half_exact],
                near=range(1 + half_blocks, 1 + 2 * half_blocks + 6),
            )
        )
    first_sums, first_lows, actives = zip(*[member[:3] for member in fed], strict=True)
    down_parts = [member[3:] for member in fed]
    down_others = [swapped(parts) for parts in down_parts]
    second_vectors = (first_gain, first_shift, down_bias, second_gain, second_shift)
    sums_shape = ((8, model), exact)

    def second_norm(at, before, scratch, extra_outs):
        lead = len(before)
        return call(
            functools.partial(second_norm_kernel, at * half_rows, at == 1),
            "second_norm",
            (*before, first_sums[at], *down_parts[at], *down_others[at], cotangent)
            + second_vectors,
            [((rows, model), low), half_exact, half_low, sums_shape] + extra_outs,
            [half_exact, half_exact, half_low, half_low, half_exact, half_low] + scratch,
            near=[*range(lead + 1 + half_blocks, lead + 1 + 2 * half_blocks)]
            + [*range(lead + 2 + 2 * half_blocks, lead + 7 + 2 * half_blocks)],
            near_outs=(3,),
            scalars=1 if before else 0,
            room=8,
            aliases={4: 0} if before else None,
        )

    layer_out, back_second, back_down, second_sums = second_norm(0, (), [], [])
    down_piece = (hidden // 4, model)
    layer_out, *rest = second_norm(
        1,
        (bits, *actives, back_down, layer_out),
        [((rows, hidden), low), half_low, ((4, *down_piece), exact)],
        [(down_piece, exact)] * 4,
    )
    back_seconds, back_downs = (back_second, rest[0]), (back_down, rest[1])
    second_sums = second_sums + rest[2]
    down_pieces = rest[3:]
    order.ran(down_pieces[0])
    chunks = {}

    def begin(name, pieces):
        chunks[name + "0"] = Chunk(ring, bits, 0, pieces[0], pieces[2])
        chunks[name + "1"] = Chunk(ring, bits, 1, pieces[1], pieces[3])

    def run(*names):
        for name in names:
            chunk = chunks[name]
            inputs = chunk.inputs()
            order.ran(chunk.advance(order.after(inputs) if chunk.step else inputs))

    up_piece = (model // 2, hidden // 2)
    fed_back = []
    normed_back = []
    made = {}

    def feed_back(at, before, inner_rows, scratch, extra_outs):
        [back_down] = order.after((back_downs[at],))
        lead = len(before)
        results = call(
            functools.partial(feed_back_kernel, at == 1),
            "feed_back",
            (*before, back_down, first_lows[at], up_weight, up_bias, down_weight),
            [(block, exact)] * half_blocks
            + [((inner_rows, hidden), low), ((8, hidden), exact)]
            + extra_outs,
            [half_low, half_low, half_exact, half_active] + scratch,
            near=range(lead + 2, lead + 5),
            near_outs=(half_blocks + 1,),
            scalars=1 if before else 0,
            room=6,
        )
        order.ran(results[half_blocks])
        fed_back.append(results)

    def feed_back_first():
        feed_back(0, (), half_rows, [], [])

    def feed_back_last():
        feed_back(
            1,
            (bits, first_lows[0], fed_back[0][half_blocks]),
            16,
            [half_low, half_active, ((4, *up_piece), exact)],
            [(up_piece, exact)] * 4,
        )
        begin("U", fed_back[1][half_blocks + 2 :])

    def first_norm_back():
        at = len(normed_back)
        parts = fed_back[at][:half_blocks]
        others = order.after(swapped(parts))
        normed_back.append(
            call(
                first_norm_kernel,
                "first_norm_back",
                (first_sums[at], *parts, *others, back_seconds[at], first_gain),
                [half_exact, half_low, sums_shape],
                [half_exact, half_exact, half_exact, half_exact, half_low],
                near=[*range(1 + half_blocks, 1 + 2 * half_blocks), 2 + 2 * half_blocks],
                near_outs=(2,),
                room=8,
            )
        )
        order.ran(normed_back[-1][1])

    back_all_shape = ((rows, 3 * width), low)

    def attend_back():
        back_attn = order.after([member[1] for member in normed_back])
        made["attns"] = back_attn
        [made["all"]] = call(
            functools.partial(attend_back_kernel, widths, seqs),
            "attend_back",
            (seq_lengths, *back_attn, out_weight, queries, keys, values, totals),
            [back_all_shape],
            [((rows, model), low), outof, rows_width, rows_width, rows_width, totals_shape]
            + [rows_width, back_all_shape, ((rows, width), exact), ((rows, width), exact)],
            scalars=1,
            room=12,
        )
        order.ran(made["all"])

    def grad_attn():
        norm_sums = [member[2] for member in normed_back]
        up_sums = fed_back[0][half_blocks + 1] + fed_back[1][half_blocks + 1]
        small = jnp.concatenate(
            [
                jnp.zeros((1, model), jnp.float32),
                up_sums[0].reshape(-1, model),
                (norm_sums[0] + norm_sums[1])[:3],
                second_sums[:3],
            ]
        )
        small = jnp.pad(small, ((0, -small.shape[0] % 32), (0, 0)))
        made["small"] = small.shape[0]
        first_piece = ((model // 2, 2 * width), exact)
        second_rows = (width + model // 2 + small.shape[0]) // 2
        second_piece = ((second_rows, model), exact)
        [back_all] = order.after((made["all"],))
        pieces = call(
            grad_attn_kernel,
            "grad_attn",
            (bits, tokens_in, back_all, context, *made["attns"], small),
            [first_piece, first_piece, second_piece, second_piece],
            [((rows, model), low), back_all_shape, rows_width, ((rows, model), low)]
            + [((model, 2 * width), exact), ((2 * second_rows, model), exact)],
            near=(6,),
            scalars=1,
            room=8,
        )
        order.ran(pieces[0])
        begin("A", [pieces[at] for at in (0, 2, 1, 3)])

    def input_part():
        [back_all] = order.after((made["all"],))
        made["parts"] = call(
            input_part_kernel,
            "input_part",
            (back_all, q_weight, k_weight, v_weight),
            [(block, exact)] * blocks,
            [back_all_shape, ((model, 3 * width), low), ((rows, model), exact)],
        )
        order.ran(made["parts"][-1])

    def grad_input():
        parts = made["parts"]
        others = order.after(swapped(parts))
        [result] = call(
            functools.partial(input_kernel, blocks),
            "grad_input",
            (*parts, *others, normed_back[0][0], normed_back[1][0]),
            [((rows, model), low)],
            [((rows, model), exact), ((rows, model), exact), ((rows, model), low)],
            near=range(blocks, 2 * blocks),
        )
        order.ran(result)
        made["input"] = result

    def finish(name, shapes, moves):
        operands = ()
        for chunk in (chunks[name + "0"], chunks[name + "1"]):
            operands += order.after(chunk.inputs())
        results = place_blocks(bits, operands, shapes, moves, "place")
        order.ran(results[0])
        return results

    def halves_at(source, rows, columns, target, row_offset, column, bit, height):
        moves = []
        for same in (True, False):
            first = at_bit(height, bit, same)
            moves.append(
                (
                    source + (0 if same else 1),
                    rows,
                    columns,
                    target,
                    lambda ref, first=first: row_offset + first(ref),
                    column,
                )
            )
        return moves

    half = hidden // 2
    quarter = half // 2
    columns_here = model // 2
    out_half, value_half = width // 2, model // 4
    tail_start = out_half + value_half
    square = (model, width)

    def place_down():
        [made["down"]] = finish(
            "D",
            ((hidden, model),),
            halves_at(0, (0, quarter), (0, model), 0, 0, 0, 0, quarter)
            + halves_at(2, (0, quarter), (0, model), 0, half, 0, 1, quarter),
        )

    def place_up():
        [made["up"]] = finish(
            "U",
            ((model, hidden),),
            halves_at(0, (0, columns_here), (0, half), 0, 0, 0, 0, columns_here)
            + halves_at(2, (0, columns_here), (0, half), 0, 0, half, 1, columns_here),
        )

    def place_attn():
        small_half = made["small"] // 2
        made["attn"] = finish(
            "A",
            (square, square, square, (width, model), (2 * small_half, model)),
            halves_at(0, (0, columns_here), (0, width), 0, 0, 0, 0, columns_here)
            + halves_at(0, (0, columns_here), (width, 2 * width), 1, 0, 0, 0, columns_here)
            + halves_at(2, (out_half, tail_start), (0, width), 2, 0, 0, 1, value_half)
            + halves_at(
                2, (out_half, tail_start), (width, 2 * width), 2, columns_here, 0, 1, value_half
            )
            + halves_at(2, (0, out_half), (0, model), 3, 0, 0, 1, out_half)
            + halves_at(2, (tail_start, tail_start + small_half), (0, model), 4, 0, 0, 1, small_half),
        )

    steps = {
        "FB0": feed_back_first,
        "FB1": feed_back_last,
        "LN": first_norm_back,
        "AB": attend_back,
        "GA": grad_attn,
        "IP": input_part,
        "GI": grad_input,
        "PD": place_down,
        "PU": place_up,
        "PA": place_attn,
    }
    begin("D", down_pieces)
    for name in plan:
        if name in steps:
            steps[name]()
        else:
            run(name)
    grad_q, grad_k, grad_v, grad_out, tail = made["attn"]
    up_rows = hidden // model
    return (
        layer_out,
        made["input"],
        grad_q,
        grad_k,
        grad_v,
        tail[0, :width],
        tail[0, width:],
        grad_out,
        tail[up_rows + 1],
        tail[up_rows + 2],
        tail[up_rows + 3],
        made["up"],
        tail[1 : up_rows + 1].reshape(-1),
        made["down"],
        tail[up_rows + 4],
        tail[up_rows + 5],
        tail[up_rows + 6],
    )


def solution(mesh):
    placed = (
        P("dp", None),
        P("dp", None),
        P("dp", None),
        P(None, "tensor"),
        P(None, "tensor"),
        P(None, "tensor"),
        P("tensor"),
        P("tensor"),
        P("tensor", None),
        P(),
        P(),
        P(),
        P(None, "tensor"),
        P("tensor"),
        P("tensor", None),
        P(),
        P(),
        P(),
    )
    counts = (mesh.shape["dp"], mesh.shape["tensor"])

    def on_device(*args):
        return local(*counts, *args)

    return jax.shard_map(
        on_device,
        mesh=mesh,
        in_specs=placed,
        out_specs=(
            P("dp", None),
            P("dp", None),
            P(None, "tensor"),
            P(None, "tensor"),
            P(None, "tensor"),
            P("tensor"),
            P("tensor"),
            P("tensor", None),
            P(),
            P(),
            P(),
            P(None, "tensor"),
            P("tensor"),
            P("tensor", None),
            P(),
            P(),
            P(),
        ),
        check_vma=False,
    )
```

```python
import functools

import jax
import jax.numpy as jnp
from jax import lax
from jax.experimental import pallas as pl
from jax.experimental.pallas import tpu as pltpu
from jax.sharding import PartitionSpec as P

DH = 64
LANES = 128
QUERY_BLOCK = 256
ROW_BLOCK = 256
MIB = 1 << 20

score_scale = 0.125
norm_eps = 1e-05
far_negative = -1e30
log2_e = 1.4426950408889634


def contract(left_side, right_side, left_dim, right_dim):
    return lax.dot_general(
        left_side,
        right_side,
        (((left_dim,), (right_dim,)), ((), ())),
        preferred_element_type=jnp.float32,
    )


def sequence_ends(lengths_ref, count):
    ends = []
    total = jnp.int32(0)
    for at in range(count):
        total = total + lengths_ref[0, at]
        ends.append(total)
    return ends


def key_window(ends, first_row, rows):
    last_row = first_row + QUERY_BLOCK - 1
    start = jnp.int32(0)
    stop = jnp.int32(rows)
    for end in ends:
        start = jnp.where(end <= first_row, jnp.maximum(start, end), start)
        stop = jnp.where(end > last_row, jnp.minimum(stop, end), stop)
    start = (start // LANES) * LANES
    stop = ((stop + LANES - 1) // LANES) * LANES
    return start, stop


def window_bias(ends, first_row, key_start, width, key_axis):
    line = (1, QUERY_BLOCK) if key_axis == 0 else (QUERY_BLOCK, 1)
    whole = (width, QUERY_BLOCK) if key_axis == 0 else (QUERY_BLOCK, width)
    query_at = lax.broadcasted_iota(jnp.int32, line, 1 - key_axis) + first_row
    seq_start = jnp.zeros(line, jnp.int32)
    seq_stop = jnp.full(line, 1 << 30, jnp.int32)
    for end in ends:
        seq_start = jnp.where(query_at >= end, jnp.maximum(seq_start, end), seq_start)
        seq_stop = jnp.where(query_at < end, jnp.minimum(seq_stop, end), seq_stop)
    key_at = lax.broadcasted_iota(jnp.int32, whole, key_axis) + key_start
    seen = (key_at >= seq_start) & (key_at < seq_stop)
    bias = jnp.where(seen, 0.0, far_negative).astype(jnp.float32)
    return jnp.concatenate([bias, bias], axis=1 - key_axis)


def split_heads(block):
    lane = lax.broadcasted_iota(jnp.int32, block.shape, 1)
    wide = block.astype(jnp.float32)
    return jnp.concatenate(
        [jnp.where(lane < DH, wide, 0.0), jnp.where(lane < DH, 0.0, wide)], axis=0
    ).astype(jnp.bfloat16)


def merge_heads(stacked):
    rows = stacked.shape[0] // 2
    lane = lax.broadcasted_iota(jnp.int32, (rows, LANES), 1)
    return jnp.where(lane < DH, stacked[:rows], stacked[rows:]).astype(jnp.bfloat16)


def put_halves(moves, sent_far, kept_far, sums, mine):
    rows = sent_far.shape[0]
    for far, place in ((sent_far, 1 - mine), (kept_far, mine)):
        moves.out(sums.at[pl.ds(pl.multiple_of(place * rows, 8), rows), :], far)


def over_query_blocks(ends, rows, widths, body):
    @pl.loop(0, rows // QUERY_BLOCK)
    def _(block):
        first_row = pl.multiple_of(block * QUERY_BLOCK, QUERY_BLOCK)
        start, stop = key_window(ends, first_row, rows)
        span = stop - start
        lower = 0
        for width in widths:
            chosen = (span > lower) & (span <= width)
            key_start = pl.multiple_of(jnp.minimum(start, rows - width), LANES)
            pl.when(chosen)(functools.partial(body, block, first_row, key_start, width))
            lower = width


def row_mean(values):
    return jnp.mean(values, axis=-1, keepdims=True)


def standardize(values):
    centre = values - row_mean(values)
    rate = lax.rsqrt(row_mean(centre * centre) + norm_eps)
    return centre * rate, rate


def norm_back(upstream, unit, rate, gain):
    scaled = upstream * gain
    return rate * (scaled - row_mean(scaled) - unit * row_mean(scaled * unit))


def column_sum(member):
    return jnp.sum(member, axis=0, keepdims=True)


def row_blocks(rows):
    return [slice(at, at + ROW_BLOCK) for at in range(0, rows, ROW_BLOCK)]


class Moves:
    def __init__(self, semaphores):
        self.semaphores = semaphores
        self.used = 0
        self.outward = []

    def start(self, source, target):
        copy = pltpu.make_async_copy(source, target, self.semaphores.at[self.used])
        self.used += 1
        copy.start()
        return copy

    def out(self, source, target):
        self.outward.append(self.start(source, target))

    def finish(self):
        for copy in self.outward:
            copy.wait()


def attend_kernel(widths, seqs, *refs):
    (
        lengths_ref,
        tokens_far,
        q_weight_far,
        k_weight_far,
        v_weight_far,
        out_weight_far,
        q_bias_far,
        v_bias_far,
        queries_far,
        keys_far,
        values_far,
        context_far,
        totals_far,
        *parts_far,
        tokens_ref,
        q_weight_ref,
        k_weight_ref,
        v_weight_ref,
        out_weight_ref,
        queries_ref,
        keys_ref,
        values_ref,
        context_ref,
        total_ref,
        part_ref,
        q_bias_ref,
        v_bias_ref,
        semaphores,
    ) = refs
    rows = tokens_ref.shape[0]
    pairs = q_weight_ref.shape[1] // LANES
    moves = Moves(semaphores)
    tokens_in = moves.start(tokens_far, tokens_ref)
    biases_in = [moves.start(q_bias_far, q_bias_ref), moves.start(v_bias_far, v_bias_ref)]
    weights_in = [
        moves.start(far, near)
        for far, near in (
            (q_weight_far, q_weight_ref),
            (k_weight_far, k_weight_ref),
            (v_weight_far, v_weight_ref),
            (out_weight_far, out_weight_ref),
        )
    ]
    tokens_in.wait()
    for copy in biases_in:
        copy.wait()
    tokens = tokens_ref[...]
    for copy, weight_ref, bias, near, far in (
        (weights_in[0], q_weight_ref, q_bias_ref, queries_ref, queries_far),
        (weights_in[1], k_weight_ref, None, keys_ref, keys_far),
        (weights_in[2], v_weight_ref, v_bias_ref, values_ref, values_far),
    ):
        copy.wait()
        product = contract(tokens, weight_ref[...], 1, 0)
        if bias is not None:
            product = product + bias[...].reshape(1, -1)
        near[...] = product.astype(jnp.bfloat16)
        moves.out(near, far)
    ends = sequence_ends(lengths_ref, seqs)

    def body(block, first_row, key_start, width):
        bias = window_bias(ends, first_row, key_start, width, 1)
        for pair in range(pairs):
            lanes = slice(pair * LANES, (pair + 1) * LANES)
            both = split_heads(queries_ref[pl.ds(first_row, QUERY_BLOCK), lanes])
            keys = keys_ref[pl.ds(key_start, width), lanes]
            scores = contract(both, keys, 1, 1) * (score_scale * log2_e) + bias
            peak = jnp.max(scores, axis=1, keepdims=True)
            exponents = jnp.exp2(scores - peak)
            total = jnp.sum(exponents, axis=1, keepdims=True)
            spread = jnp.broadcast_to(peak + jnp.log2(total), (2 * QUERY_BLOCK, LANES))
            total_ref[pl.ds(block * pairs + pair, 1), :] = spread.T[0:1]
            probs = (exponents * (1.0 / total)).astype(jnp.bfloat16)
            context = contract(probs, values_ref[pl.ds(key_start, width), lanes], 1, 0)
            context_ref[pl.ds(first_row, QUERY_BLOCK), lanes] = merge_heads(context)

    over_query_blocks(ends, rows, widths, body)
    moves.out(context_ref, context_far)
    moves.out(total_ref, totals_far)
    weights_in[3].wait()
    for at, far in zip(row_blocks(rows), parts_far, strict=True):
        part_ref[at] = contract(context_ref[at], out_weight_ref[...], 1, 0)
        moves.out(part_ref.at[at], far)
    moves.finish()


def attend_back_kernel(widths, seqs, *refs):
    (
        lengths_ref,
        back_low_far,
        back_high_far,
        out_weight_far,
        queries_far,
        keys_far,
        values_far,
        totals_far,
        back_all_far,
        back_attn_ref,
        out_weight_ref,
        queries_ref,
        keys_ref,
        values_ref,
        total_ref,
        back_context_ref,
        back_all_ref,
        back_keys_ref,
        back_values_ref,
        semaphores,
    ) = refs
    rows, width_here = queries_ref.shape
    pairs = width_here // LANES
    half_rows = rows // 2
    moves = Moves(semaphores)
    early = [
        moves.start(far, near)
        for far, near in (
            (out_weight_far, out_weight_ref),
            (back_low_far, back_attn_ref.at[:half_rows]),
            (back_high_far, back_attn_ref.at[half_rows:]),
        )
    ]
    late = [
        moves.start(far, near)
        for far, near in (
            (queries_far, queries_ref),
            (keys_far, keys_ref),
            (values_far, values_ref),
            (totals_far, total_ref),
        )
    ]
    back_keys_ref[...] = jnp.zeros_like(back_keys_ref)
    back_values_ref[...] = jnp.zeros_like(back_values_ref)
    for copy in early:
        copy.wait()
    back_context_ref[...] = contract(back_attn_ref[...], out_weight_ref[...], 1, 1).astype(
        jnp.bfloat16
    )
    for copy in late:
        copy.wait()
    ends = sequence_ends(lengths_ref, seqs)

    def body(block, first_row, key_start, width):
        bias = window_bias(ends, first_row, key_start, width, 0)
        for pair in range(pairs):
            lanes = slice(pair * LANES, (pair + 1) * LANES)
            both = split_heads(queries_ref[pl.ds(first_row, QUERY_BLOCK), lanes])
            back_both = split_heads(back_context_ref[pl.ds(first_row, QUERY_BLOCK), lanes])
            keys = keys_ref[pl.ds(key_start, width), lanes]
            values = values_ref[pl.ds(key_start, width), lanes]
            scores = contract(keys, both, 1, 1) * (score_scale * log2_e) + bias
            probs = jnp.exp2(scores - total_ref[pl.ds(block * pairs + pair, 1), :])
            back_probs = contract(values, back_both, 1, 1)
            inner = jnp.sum(back_probs * probs, axis=0, keepdims=True)
            back_scores = (probs * (back_probs - inner) * score_scale).astype(jnp.bfloat16)
            back_values_ref[pl.ds(key_start, width), lanes] += contract(
                probs.astype(jnp.bfloat16), back_both, 1, 0
            )
            back_keys_ref[pl.ds(key_start, width), lanes] += contract(back_scores, both, 1, 0)
            back_queries = contract(back_scores, keys, 0, 0)
            back_all_ref[pl.ds(first_row, QUERY_BLOCK), lanes] = merge_heads(back_queries)

    over_query_blocks(ends, rows, widths, body)
    back_all_ref[:, width_here : 2 * width_here] = back_keys_ref[...].astype(jnp.bfloat16)
    back_all_ref[:, 2 * width_here :] = back_values_ref[...].astype(jnp.bfloat16)
    moves.out(back_all_ref, back_all_far)
    moves.finish()


def grad_attn_kernel(*refs):
    (
        bits_ref,
        tokens_far,
        back_all_far,
        context_far,
        back_low_far,
        back_high_far,
        small_ref,
        first_sent_far,
        first_kept_far,
        second_sent_far,
        second_kept_far,
        tokens_ref,
        back_all_ref,
        context_ref,
        back_attn_ref,
        first_pack_ref,
        second_pack_ref,
        semaphores,
    ) = refs
    rows, model = tokens_ref.shape
    width_here = context_ref.shape[1]
    half_rows = rows // 2
    moves = Moves(semaphores)
    arriving = [
        moves.start(far, near)
        for far, near in (
            (tokens_far, tokens_ref),
            (back_all_far, back_all_ref),
            (context_far, context_ref),
            (back_low_far, back_attn_ref.at[:half_rows]),
            (back_high_far, back_attn_ref.at[half_rows:]),
        )
    ]
    for copy in arriving[:2]:
        copy.wait()
    tokens = tokens_ref[...]
    first_pack_ref[...] = contract(tokens, back_all_ref[:, : 2 * width_here], 0, 0)
    put_halves(moves, first_sent_far, first_kept_far, first_pack_ref, bits_ref[0, 0])
    grad_values = contract(tokens, back_all_ref[:, 2 * width_here :], 0, 0)
    for copy in arriving[2:]:
        copy.wait()
    grad_out = contract(context_ref[...], back_attn_ref[...], 0, 0)
    out_half, value_half, small_half = width_here // 2, model // 4, small_ref.shape[0] // 2
    top = 0
    for at in range(2):
        second_pack_ref[top : top + out_half, :] = grad_out[at * out_half : (at + 1) * out_half]
        top += out_half
        for side in range(2):
            start = side * (model // 2) + at * value_half
            second_pack_ref[
                top : top + value_half, side * width_here : (side + 1) * width_here
            ] = grad_values[start : start + value_half]
        top += value_half
        second_pack_ref[top : top + small_half, :] = small_ref[
            at * small_half : (at + 1) * small_half
        ]
        if at == 0:
            for side in range(2):
                member = back_all_ref[:, 2 * side * width_here : (2 * side + 1) * width_here]
                second_pack_ref[top : top + 1, side * width_here : (side + 1) * width_here] = (
                    column_sum(member.astype(jnp.float32))
                )
        top += small_half
    put_halves(moves, second_sent_far, second_kept_far, second_pack_ref, bits_ref[0, 1])
    moves.finish()


def input_part_kernel(*refs):
    (
        back_all_far,
        q_weight_far,
        k_weight_far,
        v_weight_far,
        *parts_far,
        back_all_ref,
        weights_ref,
        part_ref,
        semaphores,
    ) = refs
    width_here = q_weight_far.shape[1]
    moves = Moves(semaphores)
    arriving = [
        moves.start(far, weights_ref.at[:, at * width_here : (at + 1) * width_here])
        for at, far in enumerate((q_weight_far, k_weight_far, v_weight_far))
    ]
    blocks = row_blocks(back_all_ref.shape[0])
    arriving += [moves.start(back_all_far.at[at], back_all_ref.at[at]) for at in blocks]
    for copy in arriving:
        copy.wait()
    for at, far in zip(blocks, parts_far, strict=True):
        part_ref[at] = contract(back_all_ref[at], weights_ref[...], 1, 1)
        moves.out(part_ref.at[at], far)
    moves.finish()


def feed_kernel(first_row, *refs):
    (
        tokens_far,
        *own_fars,
        out_bias_ref,
        gain_ref,
        shift_ref,
        up_weight_ref,
        up_bias_ref,
        down_weight_far,
        first_sum_far,
        first_low_far,
        active_far,
        part_low_far,
        part_high_far,
        tokens_ref,
        own_ref,
        first_sum_ref,
        first_low_ref,
        active_ref,
        part_ref,
        down_weight_ref,
        semaphores,
    ) = refs
    rows = own_ref.shape[0]
    own_fars, other_refs = own_fars[: len(own_fars) // 2], own_fars[len(own_fars) // 2 :]
    moves = Moves(semaphores)
    arriving = []
    for at, own_far in zip(row_blocks(rows), own_fars, strict=True):
        there = slice(first_row + at.start, first_row + at.stop)
        arriving.append(
            (
                moves.start(own_far, own_ref.at[at]),
                moves.start(tokens_far.at[there], tokens_ref.at[at]),
            )
        )
        if at.start == 0:
            down_in = moves.start(down_weight_far, down_weight_ref)
    for at, copies, other_ref, part_far in zip(
        row_blocks(rows), arriving, other_refs, (part_low_far, part_high_far), strict=True
    ):
        for copy in copies:
            copy.wait()
        first_sum = (
            tokens_ref[at].astype(jnp.float32)
            + (own_ref[at] + other_ref[...])
            + out_bias_ref[...].reshape(1, -1)
        )
        first_sum_ref[at] = first_sum
        moves.out(first_sum_ref.at[at], first_sum_far.at[at])
        unit, unused = standardize(first_sum)
        first_low = (
            unit * gain_ref[...].reshape(1, -1) + shift_ref[...].reshape(1, -1)
        ).astype(jnp.bfloat16)
        first_low_ref[at] = first_low
        moves.out(first_low_ref.at[at], first_low_far.at[at])
        inner = contract(first_low, up_weight_ref[...], 1, 0) + up_bias_ref[...].reshape(1, -1)
        active = (inner * (0.5 * (1.0 + lax.erf(inner * 0.7071067811865476)))).astype(
            jnp.bfloat16
        )
        active_ref[at] = active
        moves.out(active_ref.at[at], active_far.at[at])
        if at.start == 0:
            down_in.wait()
        part_ref[at] = contract(active, down_weight_ref[...], 1, 0)
        moves.out(part_ref.at[at], part_far)
    moves.finish()


def second_norm_kernel(first_row, last, *refs):
    refs = list(refs)
    if last:
        bits_ref, active_low_far, active_high_far, back_low_far, layer_before_far = refs[:5]
        del refs[:5]
    (
        first_sum_far,
        own_low_far,
        own_high_far,
        *other_refs,
        cotangent_far,
        first_gain_ref,
        first_shift_ref,
        down_bias_ref,
        gain_ref,
        shift_ref,
    ) = refs[:11]
    layer_far, back_second_far, back_down_far, sums_ref = refs[11:15]
    rest = refs[15:]
    if last:
        grads_far, rest = rest[:4], rest[4:]
    first_sum_ref, own_ref, cotangent_ref, layer_ref, back_second_ref, back_down_ref, *rest = rest
    semaphores = rest[-1]
    rows = own_ref.shape[0]
    moves = Moves(semaphores)
    arriving = []
    for at, own_far in zip(row_blocks(rows), (own_low_far, own_high_far), strict=True):
        there = slice(first_row + at.start, first_row + at.stop)
        arriving.append(
            (
                moves.start(own_far, own_ref.at[at]),
                moves.start(first_sum_far.at[at], first_sum_ref.at[at]),
                moves.start(cotangent_far.at[there], cotangent_ref.at[at]),
            )
        )
    if last:
        active_ref, back_before_ref, grads_ref, unused = rest
        early = [
            moves.start(active_low_far, active_ref.at[:rows]),
            moves.start(back_low_far, back_before_ref),
        ]
        late = moves.start(active_high_far, active_ref.at[rows:])
    bias_sum, gain_sum, shift_sum = 0.0, 0.0, 0.0
    gain = gain_ref[...].reshape(1, -1)
    shift = shift_ref[...].reshape(1, -1)
    for at, copies, other_ref in zip(row_blocks(rows), arriving, other_refs, strict=True):
        for copy in copies:
            copy.wait()
        unit, unused = standardize(first_sum_ref[at])
        first = unit * first_gain_ref[...].reshape(1, -1) + first_shift_ref[...].reshape(1, -1)
        second_sum = first + (own_ref[at] + other_ref[...]) + down_bias_ref[...].reshape(1, -1)
        unit, rate = standardize(second_sum)
        layer_ref[at] = (unit * gain + shift).astype(jnp.bfloat16)
        there = slice(first_row + at.start, first_row + at.stop)
        moves.out(layer_ref.at[at], layer_far.at[there])
        upstream = cotangent_ref[at].astype(jnp.float32)
        back_second = norm_back(upstream, unit, rate, gain)
        back_second_ref[at] = back_second
        moves.out(back_second_ref.at[at], back_second_far.at[at])
        back_down_ref[at] = back_second.astype(jnp.bfloat16)
        moves.out(back_down_ref.at[at], back_down_far.at[at])
        bias_sum += column_sum(back_second)
        gain_sum += column_sum(upstream * unit)
        shift_sum += column_sum(upstream)
    put_sums(sums_ref, bias_sum, gain_sum, shift_sum)
    if last:
        for copy in early:
            copy.wait()
        late.wait()
        height = grads_ref.shape[1]
        for slot, (block, same) in enumerate(((0, False), (1, False), (0, True), (1, True))):
            mine = bits_ref[0, block]
            place = mine if same else 1 - mine
            units = pl.ds(pl.multiple_of((2 * block + place) * height, LANES), height)
            grads_ref[slot] = contract(
                active_ref[:rows, units], back_before_ref[...], 0, 0
            ) + contract(active_ref[rows:, units], back_down_ref[...], 0, 0)
            moves.out(grads_ref.at[slot], grads_far[slot])
    moves.finish()


def put_sums(sums_ref, *members):
    sums_ref[...] = jnp.zeros_like(sums_ref)
    for at, member in enumerate(members):
        sums_ref[at : at + 1, :] = member


def feed_back_kernel(last, *refs):
    refs = list(refs)
    if last:
        bits_ref, first_before_far, inner_before_far = refs[:3]
        del refs[:3]
    (
        back_down_far,
        first_low_far,
        up_weight_ref,
        up_bias_ref,
        down_weight_ref,
        part_low_far,
        part_high_far,
        inner_far,
        sums_ref,
        *rest,
    ) = refs
    if last:
        grads_far, rest = rest[:4], rest[4:]
    back_down_ref, first_low_ref, part_ref, inner_ref, *rest = rest
    semaphores = rest[-1]
    rows = back_down_ref.shape[0]
    moves = Moves(semaphores)
    arriving = [
        (
            moves.start(first_low_far.at[at], first_low_ref.at[at]),
            moves.start(back_down_far.at[at], back_down_ref.at[at]),
        )
        for at in row_blocks(rows)
    ]
    if last:
        first_before_ref, inner_before_ref, grads_ref, unused = rest
        late = [
            moves.start(first_before_far, first_before_ref),
            moves.start(inner_before_far, inner_before_ref),
        ]
    total = 0.0
    for at, copies, part_far in zip(
        row_blocks(rows), arriving, (part_low_far, part_high_far), strict=True
    ):
        for copy in copies:
            copy.wait()
        inner = contract(first_low_ref[at], up_weight_ref[...], 1, 0) + up_bias_ref[...].reshape(
            1, -1
        )
        slope = 0.5 * (1.0 + lax.erf(inner * 0.7071067811865476)) + inner * (
            0.3989422804014327 * jnp.exp(-0.5 * inner * inner)
        )
        back_active = contract(back_down_ref[at], down_weight_ref[...], 1, 1)
        back_inner = (back_active * slope).astype(jnp.bfloat16)
        inner_ref[at] = back_inner
        if not last:
            moves.out(inner_ref.at[at], inner_far.at[at])
        part_ref[at] = contract(back_inner, up_weight_ref[...], 1, 1)
        moves.out(part_ref.at[at], part_far)
        total += column_sum(back_inner.astype(jnp.float32))
    put_sums(sums_ref, total)
    if last:
        moves.out(inner_ref.at[:16], inner_far)
        for copy in late:
            copy.wait()
        height, columns = grads_ref.shape[1:]
        for slot, (block, same) in enumerate(((0, False), (1, False), (0, True), (1, True))):
            mine = bits_ref[0, block]
            place = mine if same else 1 - mine
            features = pl.ds(pl.multiple_of(place * height, LANES), height)
            units = slice(block * columns, (block + 1) * columns)
            grads_ref[slot] = contract(
                first_before_ref[:, features], inner_before_ref[:, units], 0, 0
            ) + contract(first_low_ref[:, features], inner_ref[:, units], 0, 0)
            moves.out(grads_ref.at[slot], grads_far[slot])
    moves.finish()


def first_norm_kernel(*refs):
    (
        first_sum_far,
        own_low_far,
        own_high_far,
        *other_refs,
        back_second_far,
        gain_ref,
        back_first_far,
        back_attn_far,
        sums_ref,
        first_sum_ref,
        own_ref,
        back_second_ref,
        back_first_ref,
        back_attn_ref,
        semaphores,
    ) = refs
    rows = own_ref.shape[0]
    moves = Moves(semaphores)
    arriving = [
        (
            moves.start(own_far, own_ref.at[at]),
            moves.start(first_sum_far.at[at], first_sum_ref.at[at]),
            moves.start(back_second_far.at[at], back_second_ref.at[at]),
        )
        for at, own_far in zip(row_blocks(rows), (own_low_far, own_high_far), strict=True)
    ]
    bias_sum, gain_sum, shift_sum = 0.0, 0.0, 0.0
    gain = gain_ref[...].reshape(1, -1)
    for at, copies, other_ref in zip(row_blocks(rows), arriving, other_refs, strict=True):
        for copy in copies:
            copy.wait()
        unit, rate = standardize(first_sum_ref[at])
        upstream = (own_ref[at] + other_ref[...]) + back_second_ref[at]
        back_first_sum = norm_back(upstream, unit, rate, gain)
        back_first_ref[at] = back_first_sum
        moves.out(back_first_ref.at[at], back_first_far.at[at])
        back_attn_ref[at] = back_first_sum.astype(jnp.bfloat16)
        moves.out(back_attn_ref.at[at], back_attn_far.at[at])
        bias_sum += column_sum(back_first_sum)
        gain_sum += column_sum(upstream * unit)
        shift_sum += column_sum(upstream)
    put_sums(sums_ref, bias_sum, gain_sum, shift_sum)
    moves.finish()


def input_kernel(blocks, *refs):
    own_fars, other_refs = refs[:blocks], refs[blocks : 2 * blocks]
    *first_fars, grad_far, own_ref, first_ref, grad_ref, semaphores = refs[2 * blocks :]
    rows = own_ref.shape[0]
    moves = Moves(semaphores)
    arriving = []
    per = blocks // len(first_fars)
    for block, (at, own_far) in enumerate(zip(row_blocks(rows), own_fars, strict=True)):
        inside = slice(block % per * ROW_BLOCK, (block % per + 1) * ROW_BLOCK)
        arriving.append(
            (
                moves.start(own_far, own_ref.at[at]),
                moves.start(first_fars[block // per].at[inside], first_ref.at[at]),
            )
        )
    for at, copies, other_ref in zip(row_blocks(rows), arriving, other_refs, strict=True):
        for copy in copies:
            copy.wait()
        grad_ref[at] = ((own_ref[at] + other_ref[...]) + first_ref[at]).astype(jnp.bfloat16)
        moves.out(grad_ref.at[at], grad_far.at[at])
    moves.finish()


def struct(shape, dtype):
    return jax.ShapeDtypeStruct(shape, dtype)


def in_smem():
    return pl.BlockSpec(memory_space=pltpu.SMEM)


def in_vmem():
    return pl.BlockSpec(memory_space=pltpu.VMEM)


def in_hbm():
    return pl.BlockSpec(memory_space=pltpu.HBM)


def key_widths(rows):
    return tuple(width for width in (512, 768) if width < rows) + (rows,)


def call(body, name, operands, outs, scratch=(), near=(), near_outs=(), scalars=0, room=4, aliases=None):
    bytes_here = sum(
        jnp.dtype(dtype).itemsize * functools.reduce(lambda a, b: a * b, shape) for shape, dtype in scratch
    )
    specs = [
        in_smem() if at < scalars else in_vmem() if at in near else in_hbm()
        for at in range(len(operands))
    ]
    return pl.pallas_call(
        body,
        out_shape=tuple(
            struct(*out) if at in near_outs else pltpu.HBM(*out) for at, out in enumerate(outs)
        ),
        in_specs=specs,
        out_specs=tuple(in_vmem() if at in near_outs else in_hbm() for at in range(len(outs))),
        scratch_shapes=[pltpu.VMEM(*shape) for shape in scratch]
        + [pltpu.SemaphoreType.DMA((48,))],
        input_output_aliases=aliases or {},
        compiler_params=pltpu.CompilerParams(vmem_limit_bytes=bytes_here + room * MIB),
        name=name,
    )(
        *(
            operand
            if at < scalars or at in near
            else pltpu.with_memory_space_constraint(operand, pltpu.HBM)
            for at, operand in enumerate(operands)
        )
    )


low, exact = jnp.bfloat16, jnp.float32


def place_kernel(moves, starts_ref, *refs):
    copies = []
    inputs = 1 + max(source for source, *unused in moves)
    for at, (source, rows, columns, target, row_start, column_start) in enumerate(moves):
        start = row_start(starts_ref) if callable(row_start) else row_start
        size = rows[1] - rows[0]
        copies.append(
            pltpu.make_async_copy(
                refs[source].at[pl.ds(rows[0], size), pl.ds(columns[0], columns[1] - columns[0])],
                refs[inputs + target].at[
                    pl.ds(pl.multiple_of(start, 8), size),
                    pl.ds(column_start, columns[1] - columns[0]),
                ],
                refs[-1].at[at],
            )
        )
    for copy in copies:
        copy.start()
    for copy in copies:
        copy.wait()


def place_blocks(starts, operands, shapes, moves, name):
    anywhere = pl.BlockSpec(memory_space=pl.ANY)
    return pl.pallas_call(
        functools.partial(place_kernel, moves),
        out_shape=tuple(struct(shape, jnp.float32) for shape in shapes),
        in_specs=[in_smem()] + [in_vmem()] * len(operands),
        out_specs=(anywhere,) * len(shapes),
        scratch_shapes=[pltpu.SemaphoreType.DMA((len(moves),))],
        compiler_params=pltpu.CompilerParams(vmem_limit_bytes=4 * MIB),
        name=name,
    )(starts, *operands)


def at_bit(rows, bit, same):
    def first(bits_ref):
        return (bits_ref[0, bit] if same else 1 - bits_ref[0, bit]) * rows

    return first


def swap_cores(value, tensor_count):
    return lax.ppermute(value, "tensor", [(i, i ^ 1) for i in range(tensor_count)])


class Ring:
    def __init__(self, count, place):
        self.count = count
        self.place = place
        top = count.bit_length() - 1
        self.bits = (0, 1, top - 2, top - 1)
        self.between = range(2, top - 2)

    def swap(self, value, bit):
        return lax.ppermute(value, "dp", [(i, i ^ (1 << bit)) for i in range(self.count)])

    def mine(self, name):
        return (self.place >> self.bits[name]) & 1

    def half(self, value, name, same):
        rows = value.shape[0] // 2
        mine = self.mine(name)
        return lax.dynamic_slice_in_dim(value, (mine if same else 1 - mine) * rows, rows, 0)


class Chunk:
    def __init__(self, ring, bits, path, sent, kept):
        self.ring = ring
        self.bits = bits
        *self.path, self.middle = path
        self.held = (kept,)
        self.arriving = None
        self.sent = sent
        self.step = 0

    def inputs(self):
        return self.held + (() if self.arriving is None else (self.arriving,))

    def swap(self, value, name):
        self.arriving = self.ring.swap(value, self.ring.bits[name])

    def join(self, value, arriving, name):
        rows, columns = value.shape
        [joined] = place_blocks(
            self.bits,
            (value, arriving),
            ((2 * rows, columns),),
            (
                (0, (0, rows), (0, columns), 0, at_bit(rows, name, True), 0),
                (1, (0, rows), (0, columns), 0, at_bit(rows, name, False), 0),
            ),
            "join",
        )
        return joined

    def advance(self, inputs):
        ring = self.ring
        step = self.step
        depth = len(self.path)
        self.step += 1
        if step == 0:
            self.swap(self.sent, self.path[0])
            return None
        if step < depth:
            name = self.path[step]
            sent = functools.reduce(jnp.add, [ring.half(member, name, False) for member in inputs])
            self.held = tuple(ring.half(member, name, True) for member in inputs)
            self.swap(sent, name)
            return sent
        if step == depth:
            value = functools.reduce(jnp.add, inputs)
            for bit in ring.between:
                value = value + ring.swap(value, bit)
            self.swap(value, self.middle)
        else:
            value, arrived = inputs
            back = 2 * depth - step
            if back == depth - 1:
                value = value + arrived
            else:
                value = self.join(value, arrived, self.path[back + 1])
            self.swap(value, self.path[back])
        self.held = (value,)
        return value


class Sequence:
    def __init__(self):
        self.last = None

    def after(self, values):
        if self.last is None:
            return tuple(values)
        held = lax.optimization_barrier((*values, self.last))
        return held[:-1]

    def ran(self, result):
        if result is not None:
            self.last = result


paths = {
    "D0": (0, 1, 2, 3),
    "D1": (1, 2, 0, 3),
    "U0": (0, 1, 2, 3),
    "U1": (1, 2, 0, 3),
    "A0": (0, 1, 2, 3),
    "A1": (1, 0, 2, 3),
}

plan = (
    "D1", "D0", "FB0", "FB1", "LN", "D1", "D0", "LN", "AB", "U1", "D0", "U0", "D1", "U0", "GA",
    "A1", "D0", "U1", "A0", "U0", "U1", "D0", "D1", "U0", "D1", "U1", "A0", "A1", "D0", "D1", "U0",
    "A0", "U1", "D0", "D1", "A1", "U0", "U1", "A0", "A1", "U1", "A1", "U0", "PD", "A0", "A0", "A1",
    "IP", "PU", "A1", "A0", "GI", "PA",
)


def local(
    dp_count,
    tensor_count,
    tokens_in,
    cotangent,
    seq_lengths,
    q_weight,
    k_weight,
    v_weight,
    q_bias,
    v_bias,
    out_weight,
    out_bias,
    first_gain,
    first_shift,
    up_weight,
    up_bias,
    down_weight,
    down_bias,
    second_gain,
    second_shift,
):
    place = lax.axis_index("dp")
    ring = Ring(dp_count, place)
    bits = jnp.stack([ring.mine(name) for name in range(4)]).reshape(1, 4)

    def first_bits(name):
        return jnp.stack([ring.mine(paths[name + at][0]) for at in "01"]).reshape(1, 2)

    model = q_weight.shape[0]
    width = q_weight.shape[1]
    hidden = up_weight.shape[1]
    rows = tokens_in.shape[0]
    half_rows = rows // 2
    block = (ROW_BLOCK, model)
    blocks = rows // ROW_BLOCK
    half_blocks = blocks // 2
    half_exact = ((half_rows, model), exact)
    half_low = ((half_rows, model), low)
    half_active = ((half_rows, hidden), low)
    rows_width = ((rows, width), low)
    into = ((model, width), low)
    outof = ((width, model), low)
    seqs = seq_lengths.shape[1]
    widths = key_widths(rows)
    totals_shape = ((rows // QUERY_BLOCK * (width // LANES), 2 * QUERY_BLOCK), exact)
    queries, keys, values, context, totals, *attn_parts = call(
        functools.partial(attend_kernel, widths, seqs),
        "attend",
        (seq_lengths, tokens_in, q_weight, k_weight, v_weight, out_weight, q_bias, v_bias),
        [rows_width] * 4 + [totals_shape] + [(block, exact)] * blocks,
        [((rows, model), low), into, into, into, outof]
        + [rows_width] * 4
        + [totals_shape, ((rows, model), exact)]
        + [((width,), exact)] * 2,
        scalars=1,
        room=8,
    )
    order = Sequence()

    def swapped(parts):
        return tuple(swap_cores(part, tensor_count) for part in parts)

    attn_others = swapped(attn_parts)
    fed = []
    for at in range(2):
        mine = slice(at * half_blocks, (at + 1) * half_blocks)
        fed.append(
            call(
                functools.partial(feed_kernel, at * half_rows),
                "feed",
                (tokens_in, *attn_parts[mine], *attn_others[mine])
                + (out_bias, first_gain, first_shift, up_weight, up_bias, down_weight),
                [half_exact, half_low, half_active] + [(block, exact)] * half_blocks,
                [half_low, half_exact, half_exact, half_low, half_active, half_exact]
                + [((hidden, model), low)],
                near=range(1 + half_blocks, 1 + 2 * half_blocks + 5),
            )
        )
    first_sums, first_lows, actives = zip(*[member[:3] for member in fed], strict=True)
    down_parts = [member[3:] for member in fed]
    down_others = [swapped(parts) for parts in down_parts]
    second_vectors = (first_gain, first_shift, down_bias, second_gain, second_shift)
    sums_shape = ((8, model), exact)

    def second_norm(at, before, scratch, extra_outs):
        lead = len(before)
        return call(
            functools.partial(second_norm_kernel, at * half_rows, at == 1),
            "second_norm",
            (*before, first_sums[at], *down_parts[at], *down_others[at], cotangent)
            + second_vectors,
            [((rows, model), low), half_exact, half_low, sums_shape] + extra_outs,
            [half_exact, half_exact, half_low, half_low, half_exact, half_low] + scratch,
            near=[*range(lead + 1 + half_blocks, lead + 1 + 2 * half_blocks)]
            + [*range(lead + 2 + 2 * half_blocks, lead + 7 + 2 * half_blocks)],
            near_outs=(3,),
            scalars=1 if before else 0,
            room=8,
            aliases={4: 0} if before else None,
        )

    layer_out, back_second, back_down, second_sums = second_norm(0, (), [], [])
    down_piece = (hidden // 4, model)
    layer_out, *rest = second_norm(
        1,
        (first_bits("D"), *actives, back_down, layer_out),
        [((rows, hidden), low), half_low, ((4, *down_piece), exact)],
        [(down_piece, exact)] * 4,
    )
    back_seconds, back_downs = (back_second, rest[0]), (back_down, rest[1])
    second_sums = second_sums + rest[2]
    down_pieces = rest[3:]
    order.ran(down_pieces[0])
    chunks = {}

    def begin(name, pieces):
        chunks[name + "0"] = Chunk(ring, bits, paths[name + "0"], pieces[0], pieces[2])
        chunks[name + "1"] = Chunk(ring, bits, paths[name + "1"], pieces[1], pieces[3])

    def run(*names):
        for name in names:
            chunk = chunks[name]
            inputs = chunk.inputs()
            order.ran(chunk.advance(order.after(inputs) if chunk.step else inputs))

    up_piece = (model // 2, hidden // 2)
    fed_back = []
    normed_back = []
    made = {}

    def feed_back(at, before, inner_rows, scratch, extra_outs):
        [back_down] = order.after((back_downs[at],))
        lead = len(before)
        results = call(
            functools.partial(feed_back_kernel, at == 1),
            "feed_back",
            (*before, back_down, first_lows[at], up_weight, up_bias, down_weight),
            [(block, exact)] * half_blocks
            + [((inner_rows, hidden), low), ((8, hidden), exact)]
            + extra_outs,
            [half_low, half_low, half_exact, half_active] + scratch,
            near=range(lead + 2, lead + 5),
            near_outs=(half_blocks + 1,),
            scalars=1 if before else 0,
            room=6,
        )
        order.ran(results[half_blocks])
        fed_back.append(results)

    def feed_back_first():
        feed_back(0, (), half_rows, [], [])

    def feed_back_last():
        feed_back(
            1,
            (first_bits("U"), first_lows[0], fed_back[0][half_blocks]),
            16,
            [half_low, half_active, ((4, *up_piece), exact)],
            [(up_piece, exact)] * 4,
        )
        begin("U", fed_back[1][half_blocks + 2 :])

    def first_norm_back():
        at = len(normed_back)
        parts = fed_back[at][:half_blocks]
        others = order.after(swapped(parts))
        normed_back.append(
            call(
                first_norm_kernel,
                "first_norm_back",
                (first_sums[at], *parts, *others, back_seconds[at], first_gain),
                [half_exact, half_low, sums_shape],
                [half_exact, half_exact, half_exact, half_exact, half_low],
                near=[*range(1 + half_blocks, 1 + 2 * half_blocks), 2 + 2 * half_blocks],
                near_outs=(2,),
                room=8,
            )
        )
        order.ran(normed_back[-1][1])

    back_all_shape = ((rows, 3 * width), low)

    def attend_back():
        back_attn = order.after([member[1] for member in normed_back])
        made["attns"] = back_attn
        [made["all"]] = call(
            functools.partial(attend_back_kernel, widths, seqs),
            "attend_back",
            (seq_lengths, *back_attn, out_weight, queries, keys, values, totals),
            [back_all_shape],
            [((rows, model), low), outof, rows_width, rows_width, rows_width, totals_shape]
            + [rows_width, back_all_shape, ((rows, width), exact), ((rows, width), exact)],
            scalars=1,
            room=12,
        )
        order.ran(made["all"])

    def grad_attn():
        norm_sums = [member[2] for member in normed_back]
        up_sums = fed_back[0][half_blocks + 1] + fed_back[1][half_blocks + 1]
        small = jnp.concatenate(
            [
                jnp.zeros((1, model), jnp.float32),
                up_sums[0].reshape(-1, model),
                (norm_sums[0] + norm_sums[1])[:3],
                second_sums[:3],
            ]
        )
        small = jnp.pad(small, ((0, -small.shape[0] % 64), (0, 0)))
        made["small"] = small.shape[0]
        first_piece = ((model // 2, 2 * width), exact)
        second_rows = (width + model // 2 + small.shape[0]) // 2
        second_piece = ((second_rows, model), exact)
        [back_all] = order.after((made["all"],))
        pieces = call(
            grad_attn_kernel,
            "grad_attn",
            (first_bits("A"), tokens_in, back_all, context, *made["attns"], small),
            [first_piece, first_piece, second_piece, second_piece],
            [((rows, model), low), back_all_shape, rows_width, ((rows, model), low)]
            + [((model, 2 * width), exact), ((2 * second_rows, model), exact)],
            near=(6,),
            scalars=1,
            room=8,
        )
        order.ran(pieces[0])
        begin("A", [pieces[at] for at in (0, 2, 1, 3)])

    def input_part():
        [back_all] = order.after((made["all"],))
        made["parts"] = call(
            input_part_kernel,
            "input_part",
            (back_all, q_weight, k_weight, v_weight),
            [(block, exact)] * blocks,
            [back_all_shape, ((model, 3 * width), low), ((rows, model), exact)],
        )
        order.ran(made["parts"][-1])

    def grad_input():
        parts = made["parts"]
        others = order.after(swapped(parts))
        [result] = call(
            functools.partial(input_kernel, blocks),
            "grad_input",
            (*parts, *others, normed_back[0][0], normed_back[1][0]),
            [((rows, model), low)],
            [((rows, model), exact), ((rows, model), exact), ((rows, model), low)],
            near=range(blocks, 2 * blocks),
        )
        order.ran(result)
        made["input"] = result

    def finish(name, shapes, moves):
        operands = ()
        for chunk in (chunks[name + "0"], chunks[name + "1"]):
            operands += order.after(chunk.inputs())
        results = place_blocks(bits, operands, shapes, moves, "place")
        order.ran(results[0])
        return results

    def halves_at(name, rows, columns, target, row_offset, column, height):
        moves = []
        for at, same in enumerate((True, False)):
            first = at_bit(height, paths[name][0], same)
            moves.append(
                (
                    2 * int(name[1]) + at,
                    rows,
                    columns,
                    target,
                    lambda ref, first=first: row_offset + first(ref),
                    column,
                )
            )
        return moves

    half = hidden // 2
    quarter = half // 2
    columns_here = model // 2
    out_half, value_half = width // 2, model // 4
    tail_start = out_half + value_half
    square = (model, width)

    def place_down():
        [made["down"]] = finish(
            "D",
            ((hidden, model),),
            halves_at("D0", (0, quarter), (0, model), 0, 0, 0, quarter)
            + halves_at("D1", (0, quarter), (0, model), 0, half, 0, quarter),
        )

    def place_up():
        [made["up"]] = finish(
            "U",
            ((model, hidden),),
            halves_at("U0", (0, columns_here), (0, half), 0, 0, 0, columns_here)
            + halves_at("U1", (0, columns_here), (0, half), 0, 0, half, columns_here),
        )

    def place_attn():
        small_half = made["small"] // 2
        made["attn"] = finish(
            "A",
            (square, square, square, (width, model), (2 * small_half, model)),
            halves_at("A0", (0, columns_here), (0, width), 0, 0, 0, columns_here)
            + halves_at("A0", (0, columns_here), (width, 2 * width), 1, 0, 0, columns_here)
            + halves_at("A1", (out_half, tail_start), (0, width), 2, 0, 0, value_half)
            + halves_at(
                "A1", (out_half, tail_start), (width, 2 * width), 2, columns_here, 0, value_half
            )
            + halves_at("A1", (0, out_half), (0, model), 3, 0, 0, out_half)
            + halves_at("A1", (tail_start, tail_start + small_half), (0, model), 4, 0, 0, small_half),
        )

    steps = {
        "FB0": feed_back_first,
        "FB1": feed_back_last,
        "LN": first_norm_back,
        "AB": attend_back,
        "GA": grad_attn,
        "IP": input_part,
        "GI": grad_input,
        "PD": place_down,
        "PU": place_up,
        "PA": place_attn,
    }
    begin("D", down_pieces)
    for name in plan:
        if name in steps:
            steps[name]()
        else:
            run(name)
    grad_q, grad_k, grad_v, grad_out, tail = made["attn"]
    up_rows = hidden // model
    return (
        layer_out,
        made["input"],
        grad_q,
        grad_k,
        grad_v,
        tail[0, :width],
        tail[0, width:],
        grad_out,
        tail[up_rows + 1],
        tail[up_rows + 2],
        tail[up_rows + 3],
        made["up"],
        tail[1 : up_rows + 1].reshape(-1),
        made["down"],
        tail[up_rows + 4],
        tail[up_rows + 5],
        tail[up_rows + 6],
    )


def solution(mesh):
    placed = (
        P("dp", None),
        P("dp", None),
        P("dp", None),
        P(None, "tensor"),
        P(None, "tensor"),
        P(None, "tensor"),
        P("tensor"),
        P("tensor"),
        P("tensor", None),
        P(),
        P(),
        P(),
        P(None, "tensor"),
        P("tensor"),
        P("tensor", None),
        P(),
        P(),
        P(),
    )
    counts = (mesh.shape["dp"], mesh.shape["tensor"])

    def on_device(*args):
        return local(*counts, *args)

    return jax.shard_map(
        on_device,
        mesh=mesh,
        in_specs=placed,
        out_specs=(
            P("dp", None),
            P("dp", None),
            P(None, "tensor"),
            P(None, "tensor"),
            P(None, "tensor"),
            P("tensor"),
            P("tensor"),
            P("tensor", None),
            P(),
            P(),
            P(),
            P(None, "tensor"),
            P("tensor"),
            P("tensor", None),
            P(),
            P(),
            P(),
        ),
        check_vma=False,
    )
```

```python
import functools

import jax
import jax.numpy as jnp
from jax import lax
from jax.experimental import pallas as pl
from jax.experimental.pallas import tpu as pltpu
from jax.sharding import PartitionSpec as P

DH = 64
LANES = 128
QUERY_BLOCK = 256
ROW_BLOCK = 256
MIB = 1 << 20

score_scale = 0.125
norm_eps = 1e-05
far_negative = -1e30
log2_e = 1.4426950408889634


def contract(left_side, right_side, left_dim, right_dim):
    return lax.dot_general(
        left_side,
        right_side,
        (((left_dim,), (right_dim,)), ((), ())),
        preferred_element_type=jnp.float32,
    )


def sequence_ends(lengths_ref, count):
    ends = []
    total = jnp.int32(0)
    for at in range(count):
        total = total + lengths_ref[0, at]
        ends.append(total)
    return ends


def key_window(ends, first_row, rows):
    last_row = first_row + QUERY_BLOCK - 1
    start = jnp.int32(0)
    stop = jnp.int32(rows)
    for end in ends:
        start = jnp.where(end <= first_row, jnp.maximum(start, end), start)
        stop = jnp.where(end > last_row, jnp.minimum(stop, end), stop)
    start = (start // LANES) * LANES
    stop = ((stop + LANES - 1) // LANES) * LANES
    return start, stop


def window_bias(ends, first_row, key_start, width, key_axis):
    line = (1, QUERY_BLOCK) if key_axis == 0 else (QUERY_BLOCK, 1)
    whole = (width, QUERY_BLOCK) if key_axis == 0 else (QUERY_BLOCK, width)
    query_at = lax.broadcasted_iota(jnp.int32, line, 1 - key_axis) + first_row
    seq_start = jnp.zeros(line, jnp.int32)
    seq_stop = jnp.full(line, 1 << 30, jnp.int32)
    for end in ends:
        seq_start = jnp.where(query_at >= end, jnp.maximum(seq_start, end), seq_start)
        seq_stop = jnp.where(query_at < end, jnp.minimum(seq_stop, end), seq_stop)
    key_at = lax.broadcasted_iota(jnp.int32, whole, key_axis) + key_start
    seen = (key_at >= seq_start) & (key_at < seq_stop)
    bias = jnp.where(seen, 0.0, far_negative).astype(jnp.float32)
    return jnp.concatenate([bias, bias], axis=1 - key_axis)


def split_heads(block):
    lane = lax.broadcasted_iota(jnp.int32, block.shape, 1)
    wide = block.astype(jnp.float32)
    return jnp.concatenate(
        [jnp.where(lane < DH, wide, 0.0), jnp.where(lane < DH, 0.0, wide)], axis=0
    ).astype(jnp.bfloat16)


def merge_heads(stacked):
    rows = stacked.shape[0] // 2
    lane = lax.broadcasted_iota(jnp.int32, (rows, LANES), 1)
    return jnp.where(lane < DH, stacked[:rows], stacked[rows:]).astype(jnp.bfloat16)


def put_halves(moves, sent_far, kept_far, sums, mine):
    rows = sent_far.shape[0]
    for far, place in ((sent_far, 1 - mine), (kept_far, mine)):
        moves.out(sums.at[pl.ds(pl.multiple_of(place * rows, 8), rows), :], far)


def over_query_blocks(ends, rows, widths, body):
    @pl.loop(0, rows // QUERY_BLOCK)
    def _(block):
        first_row = pl.multiple_of(block * QUERY_BLOCK, QUERY_BLOCK)
        start, stop = key_window(ends, first_row, rows)
        span = stop - start
        lower = 0
        for width in widths:
            chosen = (span > lower) & (span <= width)
            key_start = pl.multiple_of(jnp.minimum(start, rows - width), LANES)
            pl.when(chosen)(functools.partial(body, block, first_row, key_start, width))
            lower = width


def row_mean(values):
    return jnp.mean(values, axis=-1, keepdims=True)


def standardize(values):
    centre = values - row_mean(values)
    rate = lax.rsqrt(row_mean(centre * centre) + norm_eps)
    return centre * rate, rate


def norm_back(upstream, unit, rate, gain):
    scaled = upstream * gain
    return rate * (scaled - row_mean(scaled) - unit * row_mean(scaled * unit))


def column_sum(member):
    return jnp.sum(member, axis=0, keepdims=True)


def row_blocks(rows):
    return [slice(at, at + ROW_BLOCK) for at in range(0, rows, ROW_BLOCK)]


class Moves:
    def __init__(self, semaphores):
        self.semaphores = semaphores
        self.used = 0
        self.outward = []

    def start(self, source, target):
        copy = pltpu.make_async_copy(source, target, self.semaphores.at[self.used])
        self.used += 1
        copy.start()
        return copy

    def out(self, source, target):
        self.outward.append(self.start(source, target))

    def finish(self):
        for copy in self.outward:
            copy.wait()


def attend_kernel(widths, seqs, *refs):
    (
        lengths_ref,
        tokens_far,
        q_weight_far,
        k_weight_far,
        v_weight_far,
        out_weight_far,
        q_bias_far,
        v_bias_far,
        queries_far,
        keys_far,
        values_far,
        context_far,
        totals_far,
        *parts_far,
        tokens_ref,
        q_weight_ref,
        k_weight_ref,
        v_weight_ref,
        out_weight_ref,
        queries_ref,
        keys_ref,
        values_ref,
        context_ref,
        total_ref,
        part_ref,
        q_bias_ref,
        v_bias_ref,
        semaphores,
    ) = refs
    rows = tokens_ref.shape[0]
    pairs = q_weight_ref.shape[1] // LANES
    moves = Moves(semaphores)
    tokens_in = moves.start(tokens_far, tokens_ref)
    biases_in = [moves.start(q_bias_far, q_bias_ref), moves.start(v_bias_far, v_bias_ref)]
    weights_in = [
        moves.start(far, near)
        for far, near in (
            (q_weight_far, q_weight_ref),
            (k_weight_far, k_weight_ref),
            (v_weight_far, v_weight_ref),
            (out_weight_far, out_weight_ref),
        )
    ]
    tokens_in.wait()
    for copy in biases_in:
        copy.wait()
    tokens = tokens_ref[...]
    for copy, weight_ref, bias, near, far in (
        (weights_in[0], q_weight_ref, q_bias_ref, queries_ref, queries_far),
        (weights_in[1], k_weight_ref, None, keys_ref, keys_far),
        (weights_in[2], v_weight_ref, v_bias_ref, values_ref, values_far),
    ):
        copy.wait()
        product = contract(tokens, weight_ref[...], 1, 0)
        if bias is not None:
            product = product + bias[...].reshape(1, -1)
        near[...] = product.astype(jnp.bfloat16)
        moves.out(near, far)
    ends = sequence_ends(lengths_ref, seqs)

    def body(block, first_row, key_start, width):
        bias = window_bias(ends, first_row, key_start, width, 1)
        for pair in range(pairs):
            lanes = slice(pair * LANES, (pair + 1) * LANES)
            both = split_heads(queries_ref[pl.ds(first_row, QUERY_BLOCK), lanes])
            keys = keys_ref[pl.ds(key_start, width), lanes]
            scores = contract(both, keys, 1, 1) * (score_scale * log2_e) + bias
            peak = jnp.max(scores, axis=1, keepdims=True)
            exponents = jnp.exp2(scores - peak)
            total = jnp.sum(exponents, axis=1, keepdims=True)
            spread = jnp.broadcast_to(peak + jnp.log2(total), (2 * QUERY_BLOCK, LANES))
            total_ref[pl.ds(block * pairs + pair, 1), :] = spread.T[0:1]
            probs = (exponents * (1.0 / total)).astype(jnp.bfloat16)
            context = contract(probs, values_ref[pl.ds(key_start, width), lanes], 1, 0)
            context_ref[pl.ds(first_row, QUERY_BLOCK), lanes] = merge_heads(context)

    over_query_blocks(ends, rows, widths, body)
    moves.out(context_ref, context_far)
    moves.out(total_ref, totals_far)
    weights_in[3].wait()
    for at, far in zip(row_blocks(rows), parts_far, strict=True):
        part_ref[at] = contract(context_ref[at], out_weight_ref[...], 1, 0)
        moves.out(part_ref.at[at], far)
    moves.finish()


def attend_back_kernel(widths, seqs, *refs):
    (
        lengths_ref,
        back_low_far,
        back_high_far,
        out_weight_far,
        queries_far,
        keys_far,
        values_far,
        totals_far,
        back_all_far,
        back_attn_ref,
        out_weight_ref,
        queries_ref,
        keys_ref,
        values_ref,
        total_ref,
        back_context_ref,
        back_all_ref,
        back_keys_ref,
        back_values_ref,
        semaphores,
    ) = refs
    rows, width_here = queries_ref.shape
    pairs = width_here // LANES
    half_rows = rows // 2
    moves = Moves(semaphores)
    early = [
        moves.start(far, near)
        for far, near in (
            (out_weight_far, out_weight_ref),
            (back_low_far, back_attn_ref.at[:half_rows]),
            (back_high_far, back_attn_ref.at[half_rows:]),
        )
    ]
    late = [
        moves.start(far, near)
        for far, near in (
            (queries_far, queries_ref),
            (keys_far, keys_ref),
            (values_far, values_ref),
            (totals_far, total_ref),
        )
    ]
    back_keys_ref[...] = jnp.zeros_like(back_keys_ref)
    back_values_ref[...] = jnp.zeros_like(back_values_ref)
    for copy in early:
        copy.wait()
    back_context_ref[...] = contract(back_attn_ref[...], out_weight_ref[...], 1, 1).astype(
        jnp.bfloat16
    )
    for copy in late:
        copy.wait()
    ends = sequence_ends(lengths_ref, seqs)

    def body(block, first_row, key_start, width):
        bias = window_bias(ends, first_row, key_start, width, 0)
        for pair in range(pairs):
            lanes = slice(pair * LANES, (pair + 1) * LANES)
            both = split_heads(queries_ref[pl.ds(first_row, QUERY_BLOCK), lanes])
            back_both = split_heads(back_context_ref[pl.ds(first_row, QUERY_BLOCK), lanes])
            keys = keys_ref[pl.ds(key_start, width), lanes]
            values = values_ref[pl.ds(key_start, width), lanes]
            scores = contract(keys, both, 1, 1) * (score_scale * log2_e) + bias
            probs = jnp.exp2(scores - total_ref[pl.ds(block * pairs + pair, 1), :])
            back_probs = contract(values, back_both, 1, 1)
            inner = jnp.sum(back_probs * probs, axis=0, keepdims=True)
            back_scores = (probs * (back_probs - inner) * score_scale).astype(jnp.bfloat16)
            back_values_ref[pl.ds(key_start, width), lanes] += contract(
                probs.astype(jnp.bfloat16), back_both, 1, 0
            )
            back_keys_ref[pl.ds(key_start, width), lanes] += contract(back_scores, both, 1, 0)
            back_queries = contract(back_scores, keys, 0, 0)
            back_all_ref[pl.ds(first_row, QUERY_BLOCK), lanes] = merge_heads(back_queries)

    over_query_blocks(ends, rows, widths, body)
    back_all_ref[:, width_here : 2 * width_here] = back_keys_ref[...].astype(jnp.bfloat16)
    back_all_ref[:, 2 * width_here :] = back_values_ref[...].astype(jnp.bfloat16)
    moves.out(back_all_ref, back_all_far)
    moves.finish()


def grad_attn_kernel(*refs):
    (
        bits_ref,
        tokens_far,
        back_all_far,
        context_far,
        back_low_far,
        back_high_far,
        small_ref,
        first_sent_far,
        first_kept_far,
        second_sent_far,
        second_kept_far,
        tokens_ref,
        back_all_ref,
        context_ref,
        back_attn_ref,
        first_pack_ref,
        second_pack_ref,
        semaphores,
    ) = refs
    rows, model = tokens_ref.shape
    width_here = context_ref.shape[1]
    half_rows = rows // 2
    moves = Moves(semaphores)
    arriving = [
        moves.start(far, near)
        for far, near in (
            (tokens_far, tokens_ref),
            (back_all_far, back_all_ref),
            (context_far, context_ref),
            (back_low_far, back_attn_ref.at[:half_rows]),
            (back_high_far, back_attn_ref.at[half_rows:]),
        )
    ]
    for copy in arriving[:2]:
        copy.wait()
    tokens = tokens_ref[...]
    first_pack_ref[...] = contract(tokens, back_all_ref[:, : 2 * width_here], 0, 0)
    put_halves(moves, first_sent_far, first_kept_far, first_pack_ref, bits_ref[0, 0])
    grad_values = contract(tokens, back_all_ref[:, 2 * width_here :], 0, 0)
    for copy in arriving[2:]:
        copy.wait()
    grad_out = contract(context_ref[...], back_attn_ref[...], 0, 0)
    out_half, value_half, small_half = width_here // 2, model // 4, small_ref.shape[0] // 2
    top = 0
    for at in range(2):
        second_pack_ref[top : top + out_half, :] = grad_out[at * out_half : (at + 1) * out_half]
        top += out_half
        for side in range(2):
            start = side * (model // 2) + at * value_half
            second_pack_ref[
                top : top + value_half, side * width_here : (side + 1) * width_here
            ] = grad_values[start : start + value_half]
        top += value_half
        second_pack_ref[top : top + small_half, :] = small_ref[
            at * small_half : (at + 1) * small_half
        ]
        if at == 0:
            for side in range(2):
                member = back_all_ref[:, 2 * side * width_here : (2 * side + 1) * width_here]
                second_pack_ref[top : top + 1, side * width_here : (side + 1) * width_here] = (
                    column_sum(member.astype(jnp.float32))
                )
        top += small_half
    put_halves(moves, second_sent_far, second_kept_far, second_pack_ref, bits_ref[0, 1])
    moves.finish()


def input_part_kernel(*refs):
    (
        back_all_far,
        q_weight_far,
        k_weight_far,
        v_weight_far,
        *parts_far,
        back_all_ref,
        weights_ref,
        part_ref,
        semaphores,
    ) = refs
    width_here = q_weight_far.shape[1]
    moves = Moves(semaphores)
    arriving = [
        moves.start(far, weights_ref.at[:, at * width_here : (at + 1) * width_here])
        for at, far in enumerate((q_weight_far, k_weight_far, v_weight_far))
    ]
    blocks = row_blocks(back_all_ref.shape[0])
    arriving += [moves.start(back_all_far.at[at], back_all_ref.at[at]) for at in blocks]
    for copy in arriving:
        copy.wait()
    for at, far in zip(blocks, parts_far, strict=True):
        part_ref[at] = contract(back_all_ref[at], weights_ref[...], 1, 1)
        moves.out(part_ref.at[at], far)
    moves.finish()


def feed_kernel(first_row, *refs):
    (
        tokens_far,
        *own_fars,
        out_bias_ref,
        gain_ref,
        shift_ref,
        up_weight_ref,
        up_bias_ref,
        down_weight_far,
        first_sum_far,
        first_low_far,
        active_far,
        part_low_far,
        part_high_far,
        tokens_ref,
        own_ref,
        first_sum_ref,
        first_low_ref,
        active_ref,
        part_ref,
        down_weight_ref,
        semaphores,
    ) = refs
    rows = own_ref.shape[0]
    own_fars, other_refs = own_fars[: len(own_fars) // 2], own_fars[len(own_fars) // 2 :]
    moves = Moves(semaphores)
    arriving = []
    for at, own_far in zip(row_blocks(rows), own_fars, strict=True):
        there = slice(first_row + at.start, first_row + at.stop)
        arriving.append(
            (
                moves.start(own_far, own_ref.at[at]),
                moves.start(tokens_far.at[there], tokens_ref.at[at]),
            )
        )
        if at.start == 0:
            down_in = moves.start(down_weight_far, down_weight_ref)
    for at, copies, other_ref, part_far in zip(
        row_blocks(rows), arriving, other_refs, (part_low_far, part_high_far), strict=True
    ):
        for copy in copies:
            copy.wait()
        first_sum = (
            tokens_ref[at].astype(jnp.float32)
            + (own_ref[at] + other_ref[...])
            + out_bias_ref[...].reshape(1, -1)
        )
        first_sum_ref[at] = first_sum
        moves.out(first_sum_ref.at[at], first_sum_far.at[at])
        unit, unused = standardize(first_sum)
        first_low = (
            unit * gain_ref[...].reshape(1, -1) + shift_ref[...].reshape(1, -1)
        ).astype(jnp.bfloat16)
        first_low_ref[at] = first_low
        moves.out(first_low_ref.at[at], first_low_far.at[at])
        inner = contract(first_low, up_weight_ref[...], 1, 0) + up_bias_ref[...].reshape(1, -1)
        active = (inner * (0.5 * (1.0 + lax.erf(inner * 0.7071067811865476)))).astype(
            jnp.bfloat16
        )
        active_ref[at] = active
        moves.out(active_ref.at[at], active_far.at[at])
        if at.start == 0:
            down_in.wait()
        part_ref[at] = contract(active, down_weight_ref[...], 1, 0)
        moves.out(part_ref.at[at], part_far)
    moves.finish()


def second_norm_kernel(first_row, last, *refs):
    refs = list(refs)
    if last:
        bits_ref, active_low_far, active_high_far, back_low_far, layer_before_far = refs[:5]
        del refs[:5]
    (
        first_sum_far,
        own_low_far,
        own_high_far,
        *other_refs,
        cotangent_far,
        first_gain_ref,
        first_shift_ref,
        down_bias_ref,
        gain_ref,
        shift_ref,
    ) = refs[:11]
    layer_far, back_second_far, back_down_far, sums_ref = refs[11:15]
    rest = refs[15:]
    if last:
        grads_far, rest = rest[:4], rest[4:]
    first_sum_ref, own_ref, cotangent_ref, layer_ref, back_second_ref, back_down_ref, *rest = rest
    semaphores = rest[-1]
    rows = own_ref.shape[0]
    moves = Moves(semaphores)
    arriving = []
    for at, own_far in zip(row_blocks(rows), (own_low_far, own_high_far), strict=True):
        there = slice(first_row + at.start, first_row + at.stop)
        arriving.append(
            (
                moves.start(own_far, own_ref.at[at]),
                moves.start(first_sum_far.at[at], first_sum_ref.at[at]),
                moves.start(cotangent_far.at[there], cotangent_ref.at[at]),
            )
        )
    if last:
        active_ref, back_before_ref, grads_ref, unused = rest
        early = [
            moves.start(active_low_far, active_ref.at[:rows]),
            moves.start(back_low_far, back_before_ref),
        ]
        late = moves.start(active_high_far, active_ref.at[rows:])
    bias_sum, gain_sum, shift_sum = 0.0, 0.0, 0.0
    gain = gain_ref[...].reshape(1, -1)
    shift = shift_ref[...].reshape(1, -1)
    for at, copies, other_ref in zip(row_blocks(rows), arriving, other_refs, strict=True):
        for copy in copies:
            copy.wait()
        unit, unused = standardize(first_sum_ref[at])
        first = unit * first_gain_ref[...].reshape(1, -1) + first_shift_ref[...].reshape(1, -1)
        second_sum = first + (own_ref[at] + other_ref[...]) + down_bias_ref[...].reshape(1, -1)
        unit, rate = standardize(second_sum)
        layer_ref[at] = (unit * gain + shift).astype(jnp.bfloat16)
        there = slice(first_row + at.start, first_row + at.stop)
        moves.out(layer_ref.at[at], layer_far.at[there])
        upstream = cotangent_ref[at].astype(jnp.float32)
        back_second = norm_back(upstream, unit, rate, gain)
        back_second_ref[at] = back_second
        moves.out(back_second_ref.at[at], back_second_far.at[at])
        back_down_ref[at] = back_second.astype(jnp.bfloat16)
        moves.out(back_down_ref.at[at], back_down_far.at[at])
        bias_sum += column_sum(back_second)
        gain_sum += column_sum(upstream * unit)
        shift_sum += column_sum(upstream)
    put_sums(sums_ref, bias_sum, gain_sum, shift_sum)
    if last:
        for copy in early:
            copy.wait()
        late.wait()
        height = grads_ref.shape[1]
        for slot, (block, same) in enumerate(((0, False), (1, False), (0, True), (1, True))):
            mine = bits_ref[0, block]
            place = mine if same else 1 - mine
            units = pl.ds(pl.multiple_of((2 * block + place) * height, LANES), height)
            grads_ref[slot] = contract(
                active_ref[:rows, units], back_before_ref[...], 0, 0
            ) + contract(active_ref[rows:, units], back_down_ref[...], 0, 0)
            moves.out(grads_ref.at[slot], grads_far[slot])
    moves.finish()


def put_sums(sums_ref, *members):
    sums_ref[...] = jnp.zeros_like(sums_ref)
    for at, member in enumerate(members):
        sums_ref[at : at + 1, :] = member


def feed_back_kernel(last, *refs):
    refs = list(refs)
    if last:
        bits_ref, first_before_far, inner_before_far = refs[:3]
        del refs[:3]
    (
        back_down_far,
        first_low_far,
        up_weight_ref,
        up_bias_ref,
        down_weight_ref,
        part_low_far,
        part_high_far,
        inner_far,
        sums_ref,
        *rest,
    ) = refs
    if last:
        grads_far, rest = rest[:4], rest[4:]
    back_down_ref, first_low_ref, part_ref, inner_ref, *rest = rest
    semaphores = rest[-1]
    rows = back_down_ref.shape[0]
    moves = Moves(semaphores)
    arriving = [
        (
            moves.start(first_low_far.at[at], first_low_ref.at[at]),
            moves.start(back_down_far.at[at], back_down_ref.at[at]),
        )
        for at in row_blocks(rows)
    ]
    if last:
        first_before_ref, inner_before_ref, grads_ref, unused = rest
        late = [
            moves.start(first_before_far, first_before_ref),
            moves.start(inner_before_far, inner_before_ref),
        ]
    total = 0.0
    for at, copies, part_far in zip(
        row_blocks(rows), arriving, (part_low_far, part_high_far), strict=True
    ):
        for copy in copies:
            copy.wait()
        inner = contract(first_low_ref[at], up_weight_ref[...], 1, 0) + up_bias_ref[...].reshape(
            1, -1
        )
        slope = 0.5 * (1.0 + lax.erf(inner * 0.7071067811865476)) + inner * (
            0.3989422804014327 * jnp.exp(-0.5 * inner * inner)
        )
        back_active = contract(back_down_ref[at], down_weight_ref[...], 1, 1)
        back_inner = (back_active * slope).astype(jnp.bfloat16)
        inner_ref[at] = back_inner
        if not last:
            moves.out(inner_ref.at[at], inner_far.at[at])
        part_ref[at] = contract(back_inner, up_weight_ref[...], 1, 1)
        moves.out(part_ref.at[at], part_far)
        total += column_sum(back_inner.astype(jnp.float32))
    put_sums(sums_ref, total)
    if last:
        moves.out(inner_ref.at[:16], inner_far)
        for copy in late:
            copy.wait()
        height, columns = grads_ref.shape[1:]
        for slot, (block, same) in enumerate(((0, False), (1, False), (0, True), (1, True))):
            mine = bits_ref[0, block]
            place = mine if same else 1 - mine
            features = pl.ds(pl.multiple_of(place * height, LANES), height)
            units = slice(block * columns, (block + 1) * columns)
            grads_ref[slot] = contract(
                first_before_ref[:, features], inner_before_ref[:, units], 0, 0
            ) + contract(first_low_ref[:, features], inner_ref[:, units], 0, 0)
            moves.out(grads_ref.at[slot], grads_far[slot])
    moves.finish()


def first_norm_kernel(*refs):
    (
        first_sum_far,
        own_low_far,
        own_high_far,
        *other_refs,
        back_second_far,
        gain_ref,
        back_first_far,
        back_attn_far,
        sums_ref,
        first_sum_ref,
        own_ref,
        back_second_ref,
        back_first_ref,
        back_attn_ref,
        semaphores,
    ) = refs
    rows = own_ref.shape[0]
    moves = Moves(semaphores)
    arriving = [
        (
            moves.start(own_far, own_ref.at[at]),
            moves.start(first_sum_far.at[at], first_sum_ref.at[at]),
            moves.start(back_second_far.at[at], back_second_ref.at[at]),
        )
        for at, own_far in zip(row_blocks(rows), (own_low_far, own_high_far), strict=True)
    ]
    bias_sum, gain_sum, shift_sum = 0.0, 0.0, 0.0
    gain = gain_ref[...].reshape(1, -1)
    for at, copies, other_ref in zip(row_blocks(rows), arriving, other_refs, strict=True):
        for copy in copies:
            copy.wait()
        unit, rate = standardize(first_sum_ref[at])
        upstream = (own_ref[at] + other_ref[...]) + back_second_ref[at]
        back_first_sum = norm_back(upstream, unit, rate, gain)
        back_first_ref[at] = back_first_sum
        moves.out(back_first_ref.at[at], back_first_far.at[at])
        back_attn_ref[at] = back_first_sum.astype(jnp.bfloat16)
        moves.out(back_attn_ref.at[at], back_attn_far.at[at])
        bias_sum += column_sum(back_first_sum)
        gain_sum += column_sum(upstream * unit)
        shift_sum += column_sum(upstream)
    put_sums(sums_ref, bias_sum, gain_sum, shift_sum)
    moves.finish()


def input_kernel(blocks, *refs):
    own_fars, other_refs = refs[:blocks], refs[blocks : 2 * blocks]
    *first_fars, grad_far, own_ref, first_ref, grad_ref, semaphores = refs[2 * blocks :]
    rows = own_ref.shape[0]
    moves = Moves(semaphores)
    arriving = []
    per = blocks // len(first_fars)
    for block, (at, own_far) in enumerate(zip(row_blocks(rows), own_fars, strict=True)):
        inside = slice(block % per * ROW_BLOCK, (block % per + 1) * ROW_BLOCK)
        arriving.append(
            (
                moves.start(own_far, own_ref.at[at]),
                moves.start(first_fars[block // per].at[inside], first_ref.at[at]),
            )
        )
    for at, copies, other_ref in zip(row_blocks(rows), arriving, other_refs, strict=True):
        for copy in copies:
            copy.wait()
        grad_ref[at] = ((own_ref[at] + other_ref[...]) + first_ref[at]).astype(jnp.bfloat16)
        moves.out(grad_ref.at[at], grad_far.at[at])
    moves.finish()


def struct(shape, dtype):
    return jax.ShapeDtypeStruct(shape, dtype)


def in_smem():
    return pl.BlockSpec(memory_space=pltpu.SMEM)


def in_vmem():
    return pl.BlockSpec(memory_space=pltpu.VMEM)


def in_hbm():
    return pl.BlockSpec(memory_space=pltpu.HBM)


def key_widths(rows):
    return tuple(width for width in (512, 768) if width < rows) + (rows,)


def call(body, name, operands, outs, scratch=(), near=(), near_outs=(), scalars=0, room=4, aliases=None):
    bytes_here = sum(
        jnp.dtype(dtype).itemsize * functools.reduce(lambda a, b: a * b, shape) for shape, dtype in scratch
    )
    specs = [
        in_smem() if at < scalars else in_vmem() if at in near else in_hbm()
        for at in range(len(operands))
    ]
    return pl.pallas_call(
        body,
        out_shape=tuple(
            struct(*out) if at in near_outs else pltpu.HBM(*out) for at, out in enumerate(outs)
        ),
        in_specs=specs,
        out_specs=tuple(in_vmem() if at in near_outs else in_hbm() for at in range(len(outs))),
        scratch_shapes=[pltpu.VMEM(*shape) for shape in scratch]
        + [pltpu.SemaphoreType.DMA((48,))],
        input_output_aliases=aliases or {},
        compiler_params=pltpu.CompilerParams(vmem_limit_bytes=bytes_here + room * MIB),
        name=name,
    )(
        *(
            operand
            if at < scalars or at in near
            else pltpu.with_memory_space_constraint(operand, pltpu.HBM)
            for at, operand in enumerate(operands)
        )
    )


low, exact = jnp.bfloat16, jnp.float32


def place_kernel(moves, starts_ref, *refs):
    copies = []
    inputs = 1 + max(source for source, *unused in moves)
    for at, (source, rows, columns, target, row_start, column_start) in enumerate(moves):
        start = row_start(starts_ref) if callable(row_start) else row_start
        size = rows[1] - rows[0]
        copies.append(
            pltpu.make_async_copy(
                refs[source].at[pl.ds(rows[0], size), pl.ds(columns[0], columns[1] - columns[0])],
                refs[inputs + target].at[
                    pl.ds(pl.multiple_of(start, 8), size),
                    pl.ds(column_start, columns[1] - columns[0]),
                ],
                refs[-1].at[at],
            )
        )
    for copy in copies:
        copy.start()
    for copy in copies:
        copy.wait()


def place_blocks(starts, operands, shapes, moves, name):
    anywhere = pl.BlockSpec(memory_space=pl.ANY)
    return pl.pallas_call(
        functools.partial(place_kernel, moves),
        out_shape=tuple(struct(shape, jnp.float32) for shape in shapes),
        in_specs=[in_smem()] + [in_vmem()] * len(operands),
        out_specs=(anywhere,) * len(shapes),
        scratch_shapes=[pltpu.SemaphoreType.DMA((len(moves),))],
        compiler_params=pltpu.CompilerParams(vmem_limit_bytes=4 * MIB),
        name=name,
    )(starts, *operands)


def at_bit(rows, bit, same):
    def first(bits_ref):
        return (bits_ref[0, bit] if same else 1 - bits_ref[0, bit]) * rows

    return first


def swap_cores(value, tensor_count):
    return lax.ppermute(value, "tensor", [(i, i ^ 1) for i in range(tensor_count)])


class Ring:
    def __init__(self, count, place):
        self.count = count
        self.place = place
        top = count.bit_length() - 1
        self.bits = (0, 1, top - 2, top - 1)
        self.between = range(2, top - 2)

    def swap(self, value, bit):
        return lax.ppermute(value, "dp", [(i, i ^ (1 << bit)) for i in range(self.count)])

    def mine(self, name):
        return (self.place >> self.bits[name]) & 1

    def half(self, value, name, same):
        rows = value.shape[0] // 2
        mine = self.mine(name)
        return lax.dynamic_slice_in_dim(value, (mine if same else 1 - mine) * rows, rows, 0)


class Chunk:
    def __init__(self, ring, bits, path, sent, kept):
        self.ring = ring
        self.bits = bits
        *self.path, self.middle = path
        self.held = (kept,)
        self.arriving = None
        self.sent = sent
        self.step = 0

    def inputs(self):
        return self.held + (() if self.arriving is None else (self.arriving,))

    def swap(self, value, name):
        self.arriving = self.ring.swap(value, self.ring.bits[name])

    def join(self, value, arriving, name):
        rows, columns = value.shape
        [joined] = place_blocks(
            self.bits,
            (value, arriving),
            ((2 * rows, columns),),
            (
                (0, (0, rows), (0, columns), 0, at_bit(rows, name, True), 0),
                (1, (0, rows), (0, columns), 0, at_bit(rows, name, False), 0),
            ),
            "join",
        )
        return joined

    def advance(self, inputs):
        ring = self.ring
        step = self.step
        depth = len(self.path)
        self.step += 1
        if step == 0:
            self.swap(self.sent, self.path[0])
            return None
        if step < depth:
            name = self.path[step]
            sent = functools.reduce(jnp.add, [ring.half(member, name, False) for member in inputs])
            self.held = tuple(ring.half(member, name, True) for member in inputs)
            self.swap(sent, name)
            return sent
        if step == depth:
            value = functools.reduce(jnp.add, inputs)
            for bit in ring.between:
                value = value + ring.swap(value, bit)
            self.swap(value, self.middle)
        else:
            value, arrived = inputs
            back = 2 * depth - step
            if back == depth - 1:
                value = value + arrived
            else:
                value = self.join(value, arrived, self.path[back + 1])
            self.swap(value, self.path[back])
        self.held = (value,)
        return value


class Sequence:
    def __init__(self):
        self.last = None

    def after(self, values):
        if self.last is None:
            return tuple(values)
        held = lax.optimization_barrier((*values, self.last))
        return held[:-1]

    def ran(self, result):
        if result is not None:
            self.last = result


paths = {
    "D0": (0, 1, 2, 3),
    "D1": (1, 2, 0, 3),
    "U0": (0, 1, 2, 3),
    "U1": (1, 2, 0, 3),
    "A0": (0, 1, 2, 3),
    "A1": (1, 0, 2, 3),
}

plan = (
    "D1", "D0", "FB0", "FB1", "LN", "U0", "D1", "D0", "LN", "AB", "U1", "D0", "U0", "D1", "GA",
    "A1", "D0", "U1", "A0", "U0", "D0", "D1", "U1", "D1", "U0", "U1", "A0", "D0", "D1", "A1", "U0",
    "A0", "U1", "D0", "A1", "D1", "U0", "U1", "A0", "A1", "U1", "A1", "U0", "PD", "A0", "IP", "A0",
    "A1", "PU", "A0", "A1", "GI", "PA",
)


def local(
    dp_count,
    tensor_count,
    tokens_in,
    cotangent,
    seq_lengths,
    q_weight,
    k_weight,
    v_weight,
    q_bias,
    v_bias,
    out_weight,
    out_bias,
    first_gain,
    first_shift,
    up_weight,
    up_bias,
    down_weight,
    down_bias,
    second_gain,
    second_shift,
):
    place = lax.axis_index("dp")
    ring = Ring(dp_count, place)
    bits = jnp.stack([ring.mine(name) for name in range(4)]).reshape(1, 4)

    def first_bits(name):
        return jnp.stack([ring.mine(paths[name + at][0]) for at in "01"]).reshape(1, 2)

    model = q_weight.shape[0]
    width = q_weight.shape[1]
    hidden = up_weight.shape[1]
    rows = tokens_in.shape[0]
    half_rows = rows // 2
    block = (ROW_BLOCK, model)
    blocks = rows // ROW_BLOCK
    half_blocks = blocks // 2
    half_exact = ((half_rows, model), exact)
    half_low = ((half_rows, model), low)
    half_active = ((half_rows, hidden), low)
    rows_width = ((rows, width), low)
    into = ((model, width), low)
    outof = ((width, model), low)
    seqs = seq_lengths.shape[1]
    widths = key_widths(rows)
    totals_shape = ((rows // QUERY_BLOCK * (width // LANES), 2 * QUERY_BLOCK), exact)
    queries, keys, values, context, totals, *attn_parts = call(
        functools.partial(attend_kernel, widths, seqs),
        "attend",
        (seq_lengths, tokens_in, q_weight, k_weight, v_weight, out_weight, q_bias, v_bias),
        [rows_width] * 4 + [totals_shape] + [(block, exact)] * blocks,
        [((rows, model), low), into, into, into, outof]
        + [rows_width] * 4
        + [totals_shape, ((rows, model), exact)]
        + [((width,), exact)] * 2,
        scalars=1,
        room=8,
    )
    order = Sequence()

    def swapped(parts):
        return tuple(swap_cores(part, tensor_count) for part in parts)

    attn_others = swapped(attn_parts)
    fed = []
    for at in range(2):
        mine = slice(at * half_blocks, (at + 1) * half_blocks)
        fed.append(
            call(
                functools.partial(feed_kernel, at * half_rows),
                "feed",
                (tokens_in, *attn_parts[mine], *attn_others[mine])
                + (out_bias, first_gain, first_shift, up_weight, up_bias, down_weight),
                [half_exact, half_low, half_active] + [(block, exact)] * half_blocks,
                [half_low, half_exact, half_exact, half_low, half_active, half_exact]
                + [((hidden, model), low)],
                near=range(1 + half_blocks, 1 + 2 * half_blocks + 5),
            )
        )
    first_sums, first_lows, actives = zip(*[member[:3] for member in fed], strict=True)
    down_parts = [member[3:] for member in fed]
    down_others = [swapped(parts) for parts in down_parts]
    second_vectors = (first_gain, first_shift, down_bias, second_gain, second_shift)
    sums_shape = ((8, model), exact)

    def second_norm(at, before, scratch, extra_outs):
        lead = len(before)
        return call(
            functools.partial(second_norm_kernel, at * half_rows, at == 1),
            "second_norm",
            (*before, first_sums[at], *down_parts[at], *down_others[at], cotangent)
            + second_vectors,
            [((rows, model), low), half_exact, half_low, sums_shape] + extra_outs,
            [half_exact, half_exact, half_low, half_low, half_exact, half_low] + scratch,
            near=[*range(lead + 1 + half_blocks, lead + 1 + 2 * half_blocks)]
            + [*range(lead + 2 + 2 * half_blocks, lead + 7 + 2 * half_blocks)],
            near_outs=(3,),
            scalars=1 if before else 0,
            room=8,
            aliases={4: 0} if before else None,
        )

    layer_out, back_second, back_down, second_sums = second_norm(0, (), [], [])
    down_piece = (hidden // 4, model)
    layer_out, *rest = second_norm(
        1,
        (first_bits("D"), *actives, back_down, layer_out),
        [((rows, hidden), low), half_low, ((4, *down_piece), exact)],
        [(down_piece, exact)] * 4,
    )
    back_seconds, back_downs = (back_second, rest[0]), (back_down, rest[1])
    second_sums = second_sums + rest[2]
    down_pieces = rest[3:]
    order.ran(down_pieces[0])
    chunks = {}

    def begin(name, pieces):
        chunks[name + "0"] = Chunk(ring, bits, paths[name + "0"], pieces[0], pieces[2])
        chunks[name + "1"] = Chunk(ring, bits, paths[name + "1"], pieces[1], pieces[3])

    def run(*names):
        for name in names:
            chunk = chunks[name]
            inputs = chunk.inputs()
            order.ran(chunk.advance(order.after(inputs) if chunk.step else inputs))

    up_piece = (model // 2, hidden // 2)
    fed_back = []
    normed_back = []
    made = {}

    def feed_back(at, before, inner_rows, scratch, extra_outs):
        [back_down] = order.after((back_downs[at],))
        lead = len(before)
        results = call(
            functools.partial(feed_back_kernel, at == 1),
            "feed_back",
            (*before, back_down, first_lows[at], up_weight, up_bias, down_weight),
            [(block, exact)] * half_blocks
            + [((inner_rows, hidden), low), ((8, hidden), exact)]
            + extra_outs,
            [half_low, half_low, half_exact, half_active] + scratch,
            near=range(lead + 2, lead + 5),
            near_outs=(half_blocks + 1,),
            scalars=1 if before else 0,
            room=6,
        )
        order.ran(results[half_blocks])
        fed_back.append(results)

    def feed_back_first():
        feed_back(0, (), half_rows, [], [])

    def feed_back_last():
        feed_back(
            1,
            (first_bits("U"), first_lows[0], fed_back[0][half_blocks]),
            16,
            [half_low, half_active, ((4, *up_piece), exact)],
            [(up_piece, exact)] * 4,
        )
        begin("U", fed_back[1][half_blocks + 2 :])

    def first_norm_back():
        at = len(normed_back)
        parts = fed_back[at][:half_blocks]
        others = order.after(swapped(parts))
        normed_back.append(
            call(
                first_norm_kernel,
                "first_norm_back",
                (first_sums[at], *parts, *others, back_seconds[at], first_gain),
                [half_exact, half_low, sums_shape],
                [half_exact, half_exact, half_exact, half_exact, half_low],
                near=[*range(1 + half_blocks, 1 + 2 * half_blocks), 2 + 2 * half_blocks],
                near_outs=(2,),
                room=8,
            )
        )
        order.ran(normed_back[-1][1])

    back_all_shape = ((rows, 3 * width), low)

    def attend_back():
        back_attn = order.after([member[1] for member in normed_back])
        made["attns"] = back_attn
        [made["all"]] = call(
            functools.partial(attend_back_kernel, widths, seqs),
            "attend_back",
            (seq_lengths, *back_attn, out_weight, queries, keys, values, totals),
            [back_all_shape],
            [((rows, model), low), outof, rows_width, rows_width, rows_width, totals_shape]
            + [rows_width, back_all_shape, ((rows, width), exact), ((rows, width), exact)],
            scalars=1,
            room=12,
        )
        order.ran(made["all"])

    def grad_attn():
        norm_sums = [member[2] for member in normed_back]
        up_sums = fed_back[0][half_blocks + 1] + fed_back[1][half_blocks + 1]
        small = jnp.concatenate(
            [
                jnp.zeros((1, model), jnp.float32),
                up_sums[0].reshape(-1, model),
                (norm_sums[0] + norm_sums[1])[:3],
                second_sums[:3],
            ]
        )
        small = jnp.pad(small, ((0, -small.shape[0] % 64), (0, 0)))
        made["small"] = small.shape[0]
        first_piece = ((model // 2, 2 * width), exact)
        second_rows = (width + model // 2 + small.shape[0]) // 2
        second_piece = ((second_rows, model), exact)
        [back_all] = order.after((made["all"],))
        pieces = call(
            grad_attn_kernel,
            "grad_attn",
            (first_bits("A"), tokens_in, back_all, context, *made["attns"], small),
            [first_piece, first_piece, second_piece, second_piece],
            [((rows, model), low), back_all_shape, rows_width, ((rows, model), low)]
            + [((model, 2 * width), exact), ((2 * second_rows, model), exact)],
            near=(6,),
            scalars=1,
            room=8,
        )
        order.ran(pieces[0])
        begin("A", [pieces[at] for at in (0, 2, 1, 3)])

    def input_part():
        [back_all] = order.after((made["all"],))
        made["parts"] = call(
            input_part_kernel,
            "input_part",
            (back_all, q_weight, k_weight, v_weight),
            [(block, exact)] * blocks,
            [back_all_shape, ((model, 3 * width), low), ((rows, model), exact)],
        )
        order.ran(made["parts"][-1])

    def grad_input():
        parts = made["parts"]
        others = order.after(swapped(parts))
        [result] = call(
            functools.partial(input_kernel, blocks),
            "grad_input",
            (*parts, *others, normed_back[0][0], normed_back[1][0]),
            [((rows, model), low)],
            [((rows, model), exact), ((rows, model), exact), ((rows, model), low)],
            near=range(blocks, 2 * blocks),
        )
        order.ran(result)
        made["input"] = result

    def finish(name, shapes, moves):
        operands = ()
        for chunk in (chunks[name + "0"], chunks[name + "1"]):
            operands += order.after(chunk.inputs())
        results = place_blocks(bits, operands, shapes, moves, "place")
        order.ran(results[0])
        return results

    def halves_at(name, rows, columns, target, row_offset, column, height):
        moves = []
        for at, same in enumerate((True, False)):
            first = at_bit(height, paths[name][0], same)
            moves.append(
                (
                    2 * int(name[1]) + at,
                    rows,
                    columns,
                    target,
                    lambda ref, first=first: row_offset + first(ref),
                    column,
                )
            )
        return moves

    half = hidden // 2
    quarter = half // 2
    columns_here = model // 2
    out_half, value_half = width // 2, model // 4
    tail_start = out_half + value_half
    square = (model, width)

    def place_down():
        [made["down"]] = finish(
            "D",
            ((hidden, model),),
            halves_at("D0", (0, quarter), (0, model), 0, 0, 0, quarter)
            + halves_at("D1", (0, quarter), (0, model), 0, half, 0, quarter),
        )

    def place_up():
        [made["up"]] = finish(
            "U",
            ((model, hidden),),
            halves_at("U0", (0, columns_here), (0, half), 0, 0, 0, columns_here)
            + halves_at("U1", (0, columns_here), (0, half), 0, 0, half, columns_here),
        )

    def place_attn():
        small_half = made["small"] // 2
        made["attn"] = finish(
            "A",
            (square, square, square, (width, model), (2 * small_half, model)),
            halves_at("A0", (0, columns_here), (0, width), 0, 0, 0, columns_here)
            + halves_at("A0", (0, columns_here), (width, 2 * width), 1, 0, 0, columns_here)
            + halves_at("A1", (out_half, tail_start), (0, width), 2, 0, 0, value_half)
            + halves_at(
                "A1", (out_half, tail_start), (width, 2 * width), 2, columns_here, 0, value_half
            )
            + halves_at("A1", (0, out_half), (0, model), 3, 0, 0, out_half)
            + halves_at("A1", (tail_start, tail_start + small_half), (0, model), 4, 0, 0, small_half),
        )

    steps = {
        "FB0": feed_back_first,
        "FB1": feed_back_last,
        "LN": first_norm_back,
        "AB": attend_back,
        "GA": grad_attn,
        "IP": input_part,
        "GI": grad_input,
        "PD": place_down,
        "PU": place_up,
        "PA": place_attn,
    }
    begin("D", down_pieces)
    for name in plan:
        if name in steps:
            steps[name]()
        else:
            run(name)
    grad_q, grad_k, grad_v, grad_out, tail = made["attn"]
    up_rows = hidden // model
    return (
        layer_out,
        made["input"],
        grad_q,
        grad_k,
        grad_v,
        tail[0, :width],
        tail[0, width:],
        grad_out,
        tail[up_rows + 1],
        tail[up_rows + 2],
        tail[up_rows + 3],
        made["up"],
        tail[1 : up_rows + 1].reshape(-1),
        made["down"],
        tail[up_rows + 4],
        tail[up_rows + 5],
        tail[up_rows + 6],
    )


def solution(mesh):
    placed = (
        P("dp", None),
        P("dp", None),
        P("dp", None),
        P(None, "tensor"),
        P(None, "tensor"),
        P(None, "tensor"),
        P("tensor"),
        P("tensor"),
        P("tensor", None),
        P(),
        P(),
        P(),
        P(None, "tensor"),
        P("tensor"),
        P("tensor", None),
        P(),
        P(),
        P(),
    )
    counts = (mesh.shape["dp"], mesh.shape["tensor"])

    def on_device(*args):
        return local(*counts, *args)

    return jax.shard_map(
        on_device,
        mesh=mesh,
        in_specs=placed,
        out_specs=(
            P("dp", None),
            P("dp", None),
            P(None, "tensor"),
            P(None, "tensor"),
            P(None, "tensor"),
            P("tensor"),
            P("tensor"),
            P("tensor", None),
            P(),
            P(),
            P(),
            P(None, "tensor"),
            P("tensor"),
            P("tensor", None),
            P(),
            P(),
            P(),
        ),
        check_vma=False,
    )
```

```python
import functools

import jax
import jax.numpy as jnp
from jax import lax
from jax.experimental import pallas as pl
from jax.experimental.pallas import tpu as pltpu
from jax.sharding import PartitionSpec as P

DH = 64
LANES = 128
QUERY_BLOCK = 256
ROW_BLOCK = 256
MIB = 1 << 20

score_scale = 0.125
norm_eps = 1e-05
far_negative = -1e30
log2_e = 1.4426950408889634


def contract(left_side, right_side, left_dim, right_dim):
    return lax.dot_general(
        left_side,
        right_side,
        (((left_dim,), (right_dim,)), ((), ())),
        preferred_element_type=jnp.float32,
    )


def sequence_ends(lengths_ref, count):
    ends = []
    total = jnp.int32(0)
    for at in range(count):
        total = total + lengths_ref[0, at]
        ends.append(total)
    return ends


def key_window(ends, first_row, rows):
    last_row = first_row + QUERY_BLOCK - 1
    start = jnp.int32(0)
    stop = jnp.int32(rows)
    for end in ends:
        start = jnp.where(end <= first_row, jnp.maximum(start, end), start)
        stop = jnp.where(end > last_row, jnp.minimum(stop, end), stop)
    start = (start // LANES) * LANES
    stop = ((stop + LANES - 1) // LANES) * LANES
    return start, stop


def window_bias(ends, first_row, key_start, width, key_axis):
    line = (1, QUERY_BLOCK) if key_axis == 0 else (QUERY_BLOCK, 1)
    whole = (width, QUERY_BLOCK) if key_axis == 0 else (QUERY_BLOCK, width)
    query_at = lax.broadcasted_iota(jnp.int32, line, 1 - key_axis) + first_row
    seq_start = jnp.zeros(line, jnp.int32)
    seq_stop = jnp.full(line, 1 << 30, jnp.int32)
    for end in ends:
        seq_start = jnp.where(query_at >= end, jnp.maximum(seq_start, end), seq_start)
        seq_stop = jnp.where(query_at < end, jnp.minimum(seq_stop, end), seq_stop)
    key_at = lax.broadcasted_iota(jnp.int32, whole, key_axis) + key_start
    seen = (key_at >= seq_start) & (key_at < seq_stop)
    bias = jnp.where(seen, 0.0, far_negative).astype(jnp.float32)
    return jnp.concatenate([bias, bias], axis=1 - key_axis)


def split_heads(block):
    lane = lax.broadcasted_iota(jnp.int32, block.shape, 1)
    wide = block.astype(jnp.float32)
    return jnp.concatenate(
        [jnp.where(lane < DH, wide, 0.0), jnp.where(lane < DH, 0.0, wide)], axis=0
    ).astype(jnp.bfloat16)


def merge_heads(stacked):
    rows = stacked.shape[0] // 2
    lane = lax.broadcasted_iota(jnp.int32, (rows, LANES), 1)
    return jnp.where(lane < DH, stacked[:rows], stacked[rows:]).astype(jnp.bfloat16)


def put_halves(moves, sent_far, kept_far, sums, mine):
    rows = sent_far.shape[0]
    for far, place in ((sent_far, 1 - mine), (kept_far, mine)):
        moves.out(sums.at[pl.ds(pl.multiple_of(place * rows, 8), rows), :], far)


def over_query_blocks(ends, rows, widths, body):
    @pl.loop(0, rows // QUERY_BLOCK)
    def _(block):
        first_row = pl.multiple_of(block * QUERY_BLOCK, QUERY_BLOCK)
        start, stop = key_window(ends, first_row, rows)
        span = stop - start
        lower = 0
        for width in widths:
            chosen = (span > lower) & (span <= width)
            key_start = pl.multiple_of(jnp.minimum(start, rows - width), LANES)
            pl.when(chosen)(functools.partial(body, block, first_row, key_start, width))
            lower = width


def row_mean(values):
    return jnp.mean(values, axis=-1, keepdims=True)


def standardize(values):
    centre = values - row_mean(values)
    rate = lax.rsqrt(row_mean(centre * centre) + norm_eps)
    return centre * rate, rate


def norm_back(upstream, unit, rate, gain):
    scaled = upstream * gain
    return rate * (scaled - row_mean(scaled) - unit * row_mean(scaled * unit))


def column_sum(member):
    return jnp.sum(member, axis=0, keepdims=True)


def row_blocks(rows):
    return [slice(at, at + ROW_BLOCK) for at in range(0, rows, ROW_BLOCK)]


class Moves:
    def __init__(self, semaphores):
        self.semaphores = semaphores
        self.used = 0
        self.outward = []

    def start(self, source, target):
        copy = pltpu.make_async_copy(source, target, self.semaphores.at[self.used])
        self.used += 1
        copy.start()
        return copy

    def out(self, source, target):
        self.outward.append(self.start(source, target))

    def finish(self):
        for copy in self.outward:
            copy.wait()


def attend_kernel(widths, seqs, *refs):
    (
        lengths_ref,
        tokens_far,
        q_weight_far,
        k_weight_far,
        v_weight_far,
        out_weight_far,
        q_bias_far,
        v_bias_far,
        queries_far,
        keys_far,
        values_far,
        context_far,
        totals_far,
        *parts_far,
        tokens_ref,
        q_weight_ref,
        k_weight_ref,
        v_weight_ref,
        out_weight_ref,
        queries_ref,
        keys_ref,
        values_ref,
        context_ref,
        total_ref,
        part_ref,
        q_bias_ref,
        v_bias_ref,
        semaphores,
    ) = refs
    rows = tokens_ref.shape[0]
    pairs = q_weight_ref.shape[1] // LANES
    moves = Moves(semaphores)
    tokens_in = moves.start(tokens_far, tokens_ref)
    biases_in = [moves.start(q_bias_far, q_bias_ref), moves.start(v_bias_far, v_bias_ref)]
    weights_in = [
        moves.start(far, near)
        for far, near in (
            (q_weight_far, q_weight_ref),
            (k_weight_far, k_weight_ref),
            (v_weight_far, v_weight_ref),
            (out_weight_far, out_weight_ref),
        )
    ]
    tokens_in.wait()
    for copy in biases_in:
        copy.wait()
    tokens = tokens_ref[...]
    for copy, weight_ref, bias, near, far in (
        (weights_in[0], q_weight_ref, q_bias_ref, queries_ref, queries_far),
        (weights_in[1], k_weight_ref, None, keys_ref, keys_far),
        (weights_in[2], v_weight_ref, v_bias_ref, values_ref, values_far),
    ):
        copy.wait()
        product = contract(tokens, weight_ref[...], 1, 0)
        if bias is not None:
            product = product + bias[...].reshape(1, -1)
        near[...] = product.astype(jnp.bfloat16)
        moves.out(near, far)
    ends = sequence_ends(lengths_ref, seqs)

    def body(block, first_row, key_start, width):
        bias = window_bias(ends, first_row, key_start, width, 1)
        for pair in range(pairs):
            lanes = slice(pair * LANES, (pair + 1) * LANES)
            both = split_heads(queries_ref[pl.ds(first_row, QUERY_BLOCK), lanes])
            keys = keys_ref[pl.ds(key_start, width), lanes]
            scores = contract(both, keys, 1, 1) * (score_scale * log2_e) + bias
            peak = jnp.max(scores, axis=1, keepdims=True)
            exponents = jnp.exp2(scores - peak)
            total = jnp.sum(exponents, axis=1, keepdims=True)
            spread = jnp.broadcast_to(peak + jnp.log2(total), (2 * QUERY_BLOCK, LANES))
            total_ref[pl.ds(block * pairs + pair, 1), :] = spread.T[0:1]
            probs = (exponents * (1.0 / total)).astype(jnp.bfloat16)
            context = contract(probs, values_ref[pl.ds(key_start, width), lanes], 1, 0)
            context_ref[pl.ds(first_row, QUERY_BLOCK), lanes] = merge_heads(context)

    over_query_blocks(ends, rows, widths, body)
    moves.out(context_ref, context_far)
    moves.out(total_ref, totals_far)
    weights_in[3].wait()
    for at, far in zip(row_blocks(rows), parts_far, strict=True):
        part_ref[at] = contract(context_ref[at], out_weight_ref[...], 1, 0)
        moves.out(part_ref.at[at], far)
    moves.finish()


def attend_back_kernel(widths, seqs, *refs):
    (
        lengths_ref,
        back_low_far,
        back_high_far,
        out_weight_far,
        queries_far,
        keys_far,
        values_far,
        totals_far,
        back_all_far,
        back_attn_ref,
        out_weight_ref,
        queries_ref,
        keys_ref,
        values_ref,
        total_ref,
        back_context_ref,
        back_all_ref,
        back_keys_ref,
        back_values_ref,
        semaphores,
    ) = refs
    rows, width_here = queries_ref.shape
    pairs = width_here // LANES
    half_rows = rows // 2
    moves = Moves(semaphores)
    early = [
        moves.start(far, near)
        for far, near in (
            (out_weight_far, out_weight_ref),
            (back_low_far, back_attn_ref.at[:half_rows]),
            (back_high_far, back_attn_ref.at[half_rows:]),
        )
    ]
    late = [
        moves.start(far, near)
        for far, near in (
            (queries_far, queries_ref),
            (keys_far, keys_ref),
            (values_far, values_ref),
            (totals_far, total_ref),
        )
    ]
    back_keys_ref[...] = jnp.zeros_like(back_keys_ref)
    back_values_ref[...] = jnp.zeros_like(back_values_ref)
    for copy in early:
        copy.wait()
    back_context_ref[...] = contract(back_attn_ref[...], out_weight_ref[...], 1, 1).astype(
        jnp.bfloat16
    )
    for copy in late:
        copy.wait()
    ends = sequence_ends(lengths_ref, seqs)

    def body(block, first_row, key_start, width):
        bias = window_bias(ends, first_row, key_start, width, 0)
        for pair in range(pairs):
            lanes = slice(pair * LANES, (pair + 1) * LANES)
            both = split_heads(queries_ref[pl.ds(first_row, QUERY_BLOCK), lanes])
            back_both = split_heads(back_context_ref[pl.ds(first_row, QUERY_BLOCK), lanes])
            keys = keys_ref[pl.ds(key_start, width), lanes]
            values = values_ref[pl.ds(key_start, width), lanes]
            scores = contract(keys, both, 1, 1) * (score_scale * log2_e) + bias
            probs = jnp.exp2(scores - total_ref[pl.ds(block * pairs + pair, 1), :])
            back_probs = contract(values, back_both, 1, 1)
            inner = jnp.sum(back_probs * probs, axis=0, keepdims=True)
            back_scores = (probs * (back_probs - inner) * score_scale).astype(jnp.bfloat16)
            back_values_ref[pl.ds(key_start, width), lanes] += contract(
                probs.astype(jnp.bfloat16), back_both, 1, 0
            )
            back_keys_ref[pl.ds(key_start, width), lanes] += contract(back_scores, both, 1, 0)
            back_queries = contract(back_scores, keys, 0, 0)
            back_all_ref[pl.ds(first_row, QUERY_BLOCK), lanes] = merge_heads(back_queries)

    over_query_blocks(ends, rows, widths, body)
    back_all_ref[:, width_here : 2 * width_here] = back_keys_ref[...].astype(jnp.bfloat16)
    back_all_ref[:, 2 * width_here :] = back_values_ref[...].astype(jnp.bfloat16)
    moves.out(back_all_ref, back_all_far)
    moves.finish()


def grad_attn_kernel(*refs):
    (
        bits_ref,
        tokens_far,
        back_all_far,
        context_far,
        back_low_far,
        back_high_far,
        small_ref,
        first_sent_far,
        first_kept_far,
        second_sent_far,
        second_kept_far,
        tokens_ref,
        back_all_ref,
        context_ref,
        back_attn_ref,
        first_pack_ref,
        second_pack_ref,
        semaphores,
    ) = refs
    rows, model = tokens_ref.shape
    width_here = context_ref.shape[1]
    half_rows = rows // 2
    moves = Moves(semaphores)
    arriving = [
        moves.start(far, near)
        for far, near in (
            (tokens_far, tokens_ref),
            (back_all_far, back_all_ref),
            (context_far, context_ref),
            (back_low_far, back_attn_ref.at[:half_rows]),
            (back_high_far, back_attn_ref.at[half_rows:]),
        )
    ]
    for copy in arriving[:2]:
        copy.wait()
    tokens = tokens_ref[...]
    first_pack_ref[...] = contract(tokens, back_all_ref[:, : 2 * width_here], 0, 0)
    put_halves(moves, first_sent_far, first_kept_far, first_pack_ref, bits_ref[0, 0])
    grad_values = contract(tokens, back_all_ref[:, 2 * width_here :], 0, 0)
    for copy in arriving[2:]:
        copy.wait()
    grad_out = contract(context_ref[...], back_attn_ref[...], 0, 0)
    out_half, value_half, small_half = width_here // 2, model // 4, small_ref.shape[0] // 2
    top = 0
    for at in range(2):
        second_pack_ref[top : top + out_half, :] = grad_out[at * out_half : (at + 1) * out_half]
        top += out_half
        for side in range(2):
            start = side * (model // 2) + at * value_half
            second_pack_ref[
                top : top + value_half, side * width_here : (side + 1) * width_here
            ] = grad_values[start : start + value_half]
        top += value_half
        second_pack_ref[top : top + small_half, :] = small_ref[
            at * small_half : (at + 1) * small_half
        ]
        if at == 0:
            for side in range(2):
                member = back_all_ref[:, 2 * side * width_here : (2 * side + 1) * width_here]
                second_pack_ref[top : top + 1, side * width_here : (side + 1) * width_here] = (
                    column_sum(member.astype(jnp.float32))
                )
        top += small_half
    put_halves(moves, second_sent_far, second_kept_far, second_pack_ref, bits_ref[0, 1])
    moves.finish()


def input_part_kernel(*refs):
    (
        back_all_far,
        q_weight_far,
        k_weight_far,
        v_weight_far,
        *parts_far,
        back_all_ref,
        weights_ref,
        part_ref,
        semaphores,
    ) = refs
    width_here = q_weight_far.shape[1]
    moves = Moves(semaphores)
    arriving = [
        moves.start(far, weights_ref.at[:, at * width_here : (at + 1) * width_here])
        for at, far in enumerate((q_weight_far, k_weight_far, v_weight_far))
    ]
    blocks = row_blocks(back_all_ref.shape[0])
    arriving += [moves.start(back_all_far.at[at], back_all_ref.at[at]) for at in blocks]
    for copy in arriving:
        copy.wait()
    for at, far in zip(blocks, parts_far, strict=True):
        part_ref[at] = contract(back_all_ref[at], weights_ref[...], 1, 1)
        moves.out(part_ref.at[at], far)
    moves.finish()


def feed_kernel(first_row, *refs):
    (
        tokens_far,
        *own_fars,
        out_bias_ref,
        gain_ref,
        shift_ref,
        up_weight_ref,
        up_bias_ref,
        down_weight_far,
        first_sum_far,
        first_low_far,
        active_far,
        part_low_far,
        part_high_far,
        tokens_ref,
        own_ref,
        first_sum_ref,
        first_low_ref,
        active_ref,
        part_ref,
        down_weight_ref,
        semaphores,
    ) = refs
    rows = own_ref.shape[0]
    own_fars, other_refs = own_fars[: len(own_fars) // 2], own_fars[len(own_fars) // 2 :]
    moves = Moves(semaphores)
    arriving = []
    for at, own_far in zip(row_blocks(rows), own_fars, strict=True):
        there = slice(first_row + at.start, first_row + at.stop)
        arriving.append(
            (
                moves.start(own_far, own_ref.at[at]),
                moves.start(tokens_far.at[there], tokens_ref.at[at]),
            )
        )
        if at.start == 0:
            down_in = moves.start(down_weight_far, down_weight_ref)
    for at, copies, other_ref, part_far in zip(
        row_blocks(rows), arriving, other_refs, (part_low_far, part_high_far), strict=True
    ):
        for copy in copies:
            copy.wait()
        first_sum = (
            tokens_ref[at].astype(jnp.float32)
            + (own_ref[at] + other_ref[...])
            + out_bias_ref[...].reshape(1, -1)
        )
        first_sum_ref[at] = first_sum
        moves.out(first_sum_ref.at[at], first_sum_far.at[at])
        unit, unused = standardize(first_sum)
        first_low = (
            unit * gain_ref[...].reshape(1, -1) + shift_ref[...].reshape(1, -1)
        ).astype(jnp.bfloat16)
        first_low_ref[at] = first_low
        moves.out(first_low_ref.at[at], first_low_far.at[at])
        inner = contract(first_low, up_weight_ref[...], 1, 0) + up_bias_ref[...].reshape(1, -1)
        active = (inner * (0.5 * (1.0 + lax.erf(inner * 0.7071067811865476)))).astype(
            jnp.bfloat16
        )
        active_ref[at] = active
        moves.out(active_ref.at[at], active_far.at[at])
        if at.start == 0:
            down_in.wait()
        part_ref[at] = contract(active, down_weight_ref[...], 1, 0)
        moves.out(part_ref.at[at], part_far)
    moves.finish()


def second_norm_kernel(first_row, last, *refs):
    refs = list(refs)
    if last:
        bits_ref, active_low_far, active_high_far, back_low_far, layer_before_far = refs[:5]
        del refs[:5]
    (
        first_sum_far,
        own_low_far,
        own_high_far,
        *other_refs,
        cotangent_far,
        first_gain_ref,
        first_shift_ref,
        down_bias_ref,
        gain_ref,
        shift_ref,
    ) = refs[:11]
    layer_far, back_second_far, back_down_far, sums_ref = refs[11:15]
    rest = refs[15:]
    if last:
        grads_far, rest = rest[:4], rest[4:]
    first_sum_ref, own_ref, cotangent_ref, layer_ref, back_second_ref, back_down_ref, *rest = rest
    semaphores = rest[-1]
    rows = own_ref.shape[0]
    moves = Moves(semaphores)
    arriving = []
    for at, own_far in zip(row_blocks(rows), (own_low_far, own_high_far), strict=True):
        there = slice(first_row + at.start, first_row + at.stop)
        arriving.append(
            (
                moves.start(own_far, own_ref.at[at]),
                moves.start(first_sum_far.at[at], first_sum_ref.at[at]),
                moves.start(cotangent_far.at[there], cotangent_ref.at[at]),
            )
        )
    if last:
        active_ref, back_before_ref, grads_ref, unused = rest
        early = [
            moves.start(active_low_far, active_ref.at[:rows]),
            moves.start(back_low_far, back_before_ref),
        ]
        late = moves.start(active_high_far, active_ref.at[rows:])
    bias_sum, gain_sum, shift_sum = 0.0, 0.0, 0.0
    gain = gain_ref[...].reshape(1, -1)
    shift = shift_ref[...].reshape(1, -1)
    for at, copies, other_ref in zip(row_blocks(rows), arriving, other_refs, strict=True):
        for copy in copies:
            copy.wait()
        unit, unused = standardize(first_sum_ref[at])
        first = unit * first_gain_ref[...].reshape(1, -1) + first_shift_ref[...].reshape(1, -1)
        second_sum = first + (own_ref[at] + other_ref[...]) + down_bias_ref[...].reshape(1, -1)
        unit, rate = standardize(second_sum)
        layer_ref[at] = (unit * gain + shift).astype(jnp.bfloat16)
        there = slice(first_row + at.start, first_row + at.stop)
        moves.out(layer_ref.at[at], layer_far.at[there])
        upstream = cotangent_ref[at].astype(jnp.float32)
        back_second = norm_back(upstream, unit, rate, gain)
        back_second_ref[at] = back_second
        moves.out(back_second_ref.at[at], back_second_far.at[at])
        back_down_ref[at] = back_second.astype(jnp.bfloat16)
        moves.out(back_down_ref.at[at], back_down_far.at[at])
        bias_sum += column_sum(back_second)
        gain_sum += column_sum(upstream * unit)
        shift_sum += column_sum(upstream)
    put_sums(sums_ref, bias_sum, gain_sum, shift_sum)
    if last:
        for copy in early:
            copy.wait()
        late.wait()
        height = grads_ref.shape[1]
        for slot, (block, same) in enumerate(((0, False), (1, False), (0, True), (1, True))):
            mine = bits_ref[0, block]
            place = mine if same else 1 - mine
            units = pl.ds(pl.multiple_of((2 * block + place) * height, LANES), height)
            grads_ref[slot] = contract(
                active_ref[:rows, units], back_before_ref[...], 0, 0
            ) + contract(active_ref[rows:, units], back_down_ref[...], 0, 0)
            moves.out(grads_ref.at[slot], grads_far[slot])
    moves.finish()


def put_sums(sums_ref, *members):
    sums_ref[...] = jnp.zeros_like(sums_ref)
    for at, member in enumerate(members):
        sums_ref[at : at + 1, :] = member


def feed_back_kernel(last, *refs):
    refs = list(refs)
    if last:
        bits_ref, first_before_far, inner_before_far = refs[:3]
        del refs[:3]
    (
        back_down_far,
        first_low_far,
        up_weight_ref,
        up_bias_ref,
        down_weight_ref,
        part_low_far,
        part_high_far,
        inner_far,
        sums_ref,
        *rest,
    ) = refs
    if last:
        grads_far, rest = rest[:4], rest[4:]
    back_down_ref, first_low_ref, part_ref, inner_ref, *rest = rest
    semaphores = rest[-1]
    rows = back_down_ref.shape[0]
    moves = Moves(semaphores)
    arriving = [
        (
            moves.start(first_low_far.at[at], first_low_ref.at[at]),
            moves.start(back_down_far.at[at], back_down_ref.at[at]),
        )
        for at in row_blocks(rows)
    ]
    if last:
        first_before_ref, inner_before_ref, grads_ref, unused = rest
        late = [
            moves.start(first_before_far, first_before_ref),
            moves.start(inner_before_far, inner_before_ref),
        ]
    total = 0.0
    for at, copies, part_far in zip(
        row_blocks(rows), arriving, (part_low_far, part_high_far), strict=True
    ):
        for copy in copies:
            copy.wait()
        inner = contract(first_low_ref[at], up_weight_ref[...], 1, 0) + up_bias_ref[...].reshape(
            1, -1
        )
        slope = 0.5 * (1.0 + lax.erf(inner * 0.7071067811865476)) + inner * (
            0.3989422804014327 * jnp.exp(-0.5 * inner * inner)
        )
        back_active = contract(back_down_ref[at], down_weight_ref[...], 1, 1)
        back_inner = (back_active * slope).astype(jnp.bfloat16)
        inner_ref[at] = back_inner
        if not last:
            moves.out(inner_ref.at[at], inner_far.at[at])
        part_ref[at] = contract(back_inner, up_weight_ref[...], 1, 1)
        moves.out(part_ref.at[at], part_far)
        total += column_sum(back_inner.astype(jnp.float32))
    put_sums(sums_ref, total)
    if last:
        moves.out(inner_ref.at[:16], inner_far)
        for copy in late:
            copy.wait()
        height, columns = grads_ref.shape[1:]
        for slot, (block, same) in enumerate(((0, False), (1, False), (0, True), (1, True))):
            mine = bits_ref[0, block]
            place = mine if same else 1 - mine
            features = pl.ds(pl.multiple_of(place * height, LANES), height)
            units = slice(block * columns, (block + 1) * columns)
            grads_ref[slot] = contract(
                first_before_ref[:, features], inner_before_ref[:, units], 0, 0
            ) + contract(first_low_ref[:, features], inner_ref[:, units], 0, 0)
            moves.out(grads_ref.at[slot], grads_far[slot])
    moves.finish()


def first_norm_kernel(*refs):
    (
        first_sum_far,
        own_low_far,
        own_high_far,
        *other_refs,
        back_second_far,
        gain_ref,
        back_first_far,
        back_attn_far,
        sums_ref,
        first_sum_ref,
        own_ref,
        back_second_ref,
        back_first_ref,
        back_attn_ref,
        semaphores,
    ) = refs
    rows = own_ref.shape[0]
    moves = Moves(semaphores)
    arriving = [
        (
            moves.start(own_far, own_ref.at[at]),
            moves.start(first_sum_far.at[at], first_sum_ref.at[at]),
            moves.start(back_second_far.at[at], back_second_ref.at[at]),
        )
        for at, own_far in zip(row_blocks(rows), (own_low_far, own_high_far), strict=True)
    ]
    bias_sum, gain_sum, shift_sum = 0.0, 0.0, 0.0
    gain = gain_ref[...].reshape(1, -1)
    for at, copies, other_ref in zip(row_blocks(rows), arriving, other_refs, strict=True):
        for copy in copies:
            copy.wait()
        unit, rate = standardize(first_sum_ref[at])
        upstream = (own_ref[at] + other_ref[...]) + back_second_ref[at]
        back_first_sum = norm_back(upstream, unit, rate, gain)
        back_first_ref[at] = back_first_sum
        moves.out(back_first_ref.at[at], back_first_far.at[at])
        back_attn_ref[at] = back_first_sum.astype(jnp.bfloat16)
        moves.out(back_attn_ref.at[at], back_attn_far.at[at])
        bias_sum += column_sum(back_first_sum)
        gain_sum += column_sum(upstream * unit)
        shift_sum += column_sum(upstream)
    put_sums(sums_ref, bias_sum, gain_sum, shift_sum)
    moves.finish()


def input_kernel(blocks, *refs):
    own_fars, other_refs = refs[:blocks], refs[blocks : 2 * blocks]
    *first_fars, grad_far, own_ref, first_ref, grad_ref, semaphores = refs[2 * blocks :]
    rows = own_ref.shape[0]
    moves = Moves(semaphores)
    arriving = []
    per = blocks // len(first_fars)
    for block, (at, own_far) in enumerate(zip(row_blocks(rows), own_fars, strict=True)):
        inside = slice(block % per * ROW_BLOCK, (block % per + 1) * ROW_BLOCK)
        arriving.append(
            (
                moves.start(own_far, own_ref.at[at]),
                moves.start(first_fars[block // per].at[inside], first_ref.at[at]),
            )
        )
    for at, copies, other_ref in zip(row_blocks(rows), arriving, other_refs, strict=True):
        for copy in copies:
            copy.wait()
        grad_ref[at] = ((own_ref[at] + other_ref[...]) + first_ref[at]).astype(jnp.bfloat16)
        moves.out(grad_ref.at[at], grad_far.at[at])
    moves.finish()


def struct(shape, dtype):
    return jax.ShapeDtypeStruct(shape, dtype)


def in_smem():
    return pl.BlockSpec(memory_space=pltpu.SMEM)


def in_vmem():
    return pl.BlockSpec(memory_space=pltpu.VMEM)


def in_hbm():
    return pl.BlockSpec(memory_space=pltpu.HBM)


def key_widths(rows, steps=(512, 768)):
    return tuple(width for width in steps if width < rows) + (rows,)


def call(body, name, operands, outs, scratch=(), near=(), near_outs=(), scalars=0, room=4, aliases=None):
    bytes_here = sum(
        jnp.dtype(dtype).itemsize * functools.reduce(lambda a, b: a * b, shape) for shape, dtype in scratch
    )
    specs = [
        in_smem() if at < scalars else in_vmem() if at in near else in_hbm()
        for at in range(len(operands))
    ]
    return pl.pallas_call(
        body,
        out_shape=tuple(
            struct(*out) if at in near_outs else pltpu.HBM(*out) for at, out in enumerate(outs)
        ),
        in_specs=specs,
        out_specs=tuple(in_vmem() if at in near_outs else in_hbm() for at in range(len(outs))),
        scratch_shapes=[pltpu.VMEM(*shape) for shape in scratch]
        + [pltpu.SemaphoreType.DMA((48,))],
        input_output_aliases=aliases or {},
        compiler_params=pltpu.CompilerParams(vmem_limit_bytes=bytes_here + room * MIB),
        name=name,
    )(
        *(
            operand
            if at < scalars or at in near
            else pltpu.with_memory_space_constraint(operand, pltpu.HBM)
            for at, operand in enumerate(operands)
        )
    )


low, exact = jnp.bfloat16, jnp.float32


def place_kernel(moves, starts_ref, *refs):
    copies = []
    inputs = 1 + max(source for source, *unused in moves)
    for at, (source, rows, columns, target, row_start, column_start) in enumerate(moves):
        start = row_start(starts_ref) if callable(row_start) else row_start
        size = rows[1] - rows[0]
        copies.append(
            pltpu.make_async_copy(
                refs[source].at[pl.ds(rows[0], size), pl.ds(columns[0], columns[1] - columns[0])],
                refs[inputs + target].at[
                    pl.ds(pl.multiple_of(start, 8), size),
                    pl.ds(column_start, columns[1] - columns[0]),
                ],
                refs[-1].at[at],
            )
        )
    for copy in copies:
        copy.start()
    for copy in copies:
        copy.wait()


def place_blocks(starts, operands, shapes, moves, name):
    anywhere = pl.BlockSpec(memory_space=pl.ANY)
    return pl.pallas_call(
        functools.partial(place_kernel, moves),
        out_shape=tuple(struct(shape, jnp.float32) for shape in shapes),
        in_specs=[in_smem()] + [in_vmem()] * len(operands),
        out_specs=(anywhere,) * len(shapes),
        scratch_shapes=[pltpu.SemaphoreType.DMA((len(moves),))],
        compiler_params=pltpu.CompilerParams(vmem_limit_bytes=4 * MIB),
        name=name,
    )(starts, *operands)


def at_bit(rows, bit, same):
    def first(bits_ref):
        return (bits_ref[0, bit] if same else 1 - bits_ref[0, bit]) * rows

    return first


def swap_cores(value, tensor_count):
    return lax.ppermute(value, "tensor", [(i, i ^ 1) for i in range(tensor_count)])


class Ring:
    def __init__(self, count, place):
        self.count = count
        self.place = place
        top = count.bit_length() - 1
        self.bits = (0, 1, top - 2, top - 1)
        self.between = range(2, top - 2)

    def swap(self, value, bit):
        return lax.ppermute(value, "dp", [(i, i ^ (1 << bit)) for i in range(self.count)])

    def mine(self, name):
        return (self.place >> self.bits[name]) & 1

    def half(self, value, name, same):
        rows = value.shape[0] // 2
        mine = self.mine(name)
        return lax.dynamic_slice_in_dim(value, (mine if same else 1 - mine) * rows, rows, 0)


class Chunk:
    def __init__(self, ring, bits, path, sent, kept):
        self.ring = ring
        self.bits = bits
        *self.path, self.middle = path
        self.held = (kept,)
        self.arriving = None
        self.sent = sent
        self.step = 0

    def inputs(self):
        return self.held + (() if self.arriving is None else (self.arriving,))

    def swap(self, value, name):
        self.arriving = self.ring.swap(value, self.ring.bits[name])

    def join(self, value, arriving, name):
        rows, columns = value.shape
        [joined] = place_blocks(
            self.bits,
            (value, arriving),
            ((2 * rows, columns),),
            (
                (0, (0, rows), (0, columns), 0, at_bit(rows, name, True), 0),
                (1, (0, rows), (0, columns), 0, at_bit(rows, name, False), 0),
            ),
            "join",
        )
        return joined

    def advance(self, inputs):
        ring = self.ring
        step = self.step
        depth = len(self.path)
        self.step += 1
        if step == 0:
            self.swap(self.sent, self.path[0])
            return None
        if step < depth:
            name = self.path[step]
            sent = functools.reduce(jnp.add, [ring.half(member, name, False) for member in inputs])
            self.held = tuple(ring.half(member, name, True) for member in inputs)
            self.swap(sent, name)
            return sent
        if step == depth:
            value = functools.reduce(jnp.add, inputs)
            for bit in ring.between:
                value = value + ring.swap(value, bit)
            self.swap(value, self.middle)
        else:
            value, arrived = inputs
            back = 2 * depth - step
            if back == depth - 1:
                value = value + arrived
            else:
                value = self.join(value, arrived, self.path[back + 1])
            self.swap(value, self.path[back])
        self.held = (value,)
        return value


class Sequence:
    def __init__(self):
        self.last = None

    def after(self, values):
        if self.last is None:
            return tuple(values)
        held = lax.optimization_barrier((*values, self.last))
        return held[:-1]

    def ran(self, result):
        if result is not None:
            self.last = result


paths = {
    "D0": (0, 1, 2, 3),
    "D1": (1, 2, 0, 3),
    "U0": (0, 1, 2, 3),
    "U1": (1, 2, 0, 3),
    "A0": (0, 1, 2, 3),
    "A1": (1, 0, 2, 3),
}

plan = (
    "D0", "FB0", "D1", "FB1", "LN", "U0", "D1", "D0", "LN", "AB", "U1", "D1", "D0", "U0", "GA",
    "A1", "D0", "U1", "A0", "U0", "D0", "D1", "U1", "D1", "U0", "U1", "A0", "D0", "D1", "A1", "U0",
    "A0", "U1", "D0", "A1", "D1", "U0", "U1", "A0", "A1", "U1", "U0", "A1", "PD", "A0", "IP", "A0",
    "A1", "PU", "A0", "A1", "GI", "PA",
)


def local(
    dp_count,
    tensor_count,
    tokens_in,
    cotangent,
    seq_lengths,
    q_weight,
    k_weight,
    v_weight,
    q_bias,
    v_bias,
    out_weight,
    out_bias,
    first_gain,
    first_shift,
    up_weight,
    up_bias,
    down_weight,
    down_bias,
    second_gain,
    second_shift,
):
    place = lax.axis_index("dp")
    ring = Ring(dp_count, place)
    bits = jnp.stack([ring.mine(name) for name in range(4)]).reshape(1, 4)

    def first_bits(name):
        return jnp.stack([ring.mine(paths[name + at][0]) for at in "01"]).reshape(1, 2)

    model = q_weight.shape[0]
    width = q_weight.shape[1]
    hidden = up_weight.shape[1]
    rows = tokens_in.shape[0]
    half_rows = rows // 2
    block = (ROW_BLOCK, model)
    blocks = rows // ROW_BLOCK
    half_blocks = blocks // 2
    half_exact = ((half_rows, model), exact)
    half_low = ((half_rows, model), low)
    half_active = ((half_rows, hidden), low)
    rows_width = ((rows, width), low)
    into = ((model, width), low)
    outof = ((width, model), low)
    seqs = seq_lengths.shape[1]
    widths = key_widths(rows)
    totals_shape = ((rows // QUERY_BLOCK * (width // LANES), 2 * QUERY_BLOCK), exact)
    queries, keys, values, context, totals, *attn_parts = call(
        functools.partial(attend_kernel, widths, seqs),
        "attend",
        (seq_lengths, tokens_in, q_weight, k_weight, v_weight, out_weight, q_bias, v_bias),
        [rows_width] * 4 + [totals_shape] + [(block, exact)] * blocks,
        [((rows, model), low), into, into, into, outof]
        + [rows_width] * 4
        + [totals_shape, ((rows, model), exact)]
        + [((width,), exact)] * 2,
        scalars=1,
        room=8,
    )
    order = Sequence()

    def swapped(parts):
        return tuple(swap_cores(part, tensor_count) for part in parts)

    attn_others = swapped(attn_parts)
    fed = []
    for at in range(2):
        mine = slice(at * half_blocks, (at + 1) * half_blocks)
        fed.append(
            call(
                functools.partial(feed_kernel, at * half_rows),
                "feed",
                (tokens_in, *attn_parts[mine], *attn_others[mine])
                + (out_bias, first_gain, first_shift, up_weight, up_bias, down_weight),
                [half_exact, half_low, half_active] + [(block, exact)] * half_blocks,
                [half_low, half_exact, half_exact, half_low, half_active, half_exact]
                + [((hidden, model), low)],
                near=range(1 + half_blocks, 1 + 2 * half_blocks + 5),
            )
        )
    first_sums, first_lows, actives = zip(*[member[:3] for member in fed], strict=True)
    down_parts = [member[3:] for member in fed]
    down_others = [swapped(parts) for parts in down_parts]
    second_vectors = (first_gain, first_shift, down_bias, second_gain, second_shift)
    sums_shape = ((8, model), exact)

    def second_norm(at, before, scratch, extra_outs):
        lead = len(before)
        return call(
            functools.partial(second_norm_kernel, at * half_rows, at == 1),
            "second_norm",
            (*before, first_sums[at], *down_parts[at], *down_others[at], cotangent)
            + second_vectors,
            [((rows, model), low), half_exact, half_low, sums_shape] + extra_outs,
            [half_exact, half_exact, half_low, half_low, half_exact, half_low] + scratch,
            near=[*range(lead + 1 + half_blocks, lead + 1 + 2 * half_blocks)]
            + [*range(lead + 2 + 2 * half_blocks, lead + 7 + 2 * half_blocks)],
            near_outs=(3,),
            scalars=1 if before else 0,
            room=8,
            aliases={4: 0} if before else None,
        )

    layer_out, back_second, back_down, second_sums = second_norm(0, (), [], [])
    down_piece = (hidden // 4, model)
    layer_out, *rest = second_norm(
        1,
        (first_bits("D"), *actives, back_down, layer_out),
        [((rows, hidden), low), half_low, ((4, *down_piece), exact)],
        [(down_piece, exact)] * 4,
    )
    back_seconds, back_downs = (back_second, rest[0]), (back_down, rest[1])
    second_sums = second_sums + rest[2]
    down_pieces = rest[3:]
    order.ran(down_pieces[0])
    chunks = {}

    def begin(name, pieces):
        chunks[name + "0"] = Chunk(ring, bits, paths[name + "0"], pieces[0], pieces[2])
        chunks[name + "1"] = Chunk(ring, bits, paths[name + "1"], pieces[1], pieces[3])

    def run(*names):
        for name in names:
            chunk = chunks[name]
            inputs = chunk.inputs()
            order.ran(chunk.advance(order.after(inputs) if chunk.step else inputs))

    up_piece = (model // 2, hidden // 2)
    fed_back = []
    normed_back = []
    made = {}

    def feed_back(at, before, inner_rows, scratch, extra_outs):
        [back_down] = order.after((back_downs[at],))
        lead = len(before)
        results = call(
            functools.partial(feed_back_kernel, at == 1),
            "feed_back",
            (*before, back_down, first_lows[at], up_weight, up_bias, down_weight),
            [(block, exact)] * half_blocks
            + [((inner_rows, hidden), low), ((8, hidden), exact)]
            + extra_outs,
            [half_low, half_low, half_exact, half_active] + scratch,
            near=range(lead + 2, lead + 5),
            near_outs=(half_blocks + 1,),
            scalars=1 if before else 0,
            room=6,
        )
        order.ran(results[half_blocks])
        fed_back.append(results)

    def feed_back_first():
        feed_back(0, (), half_rows, [], [])

    def feed_back_last():
        feed_back(
            1,
            (first_bits("U"), first_lows[0], fed_back[0][half_blocks]),
            16,
            [half_low, half_active, ((4, *up_piece), exact)],
            [(up_piece, exact)] * 4,
        )
        begin("U", fed_back[1][half_blocks + 2 :])

    def first_norm_back():
        at = len(normed_back)
        parts = fed_back[at][:half_blocks]
        others = order.after(swapped(parts))
        normed_back.append(
            call(
                first_norm_kernel,
                "first_norm_back",
                (first_sums[at], *parts, *others, back_seconds[at], first_gain),
                [half_exact, half_low, sums_shape],
                [half_exact, half_exact, half_exact, half_exact, half_low],
                near=[*range(1 + half_blocks, 1 + 2 * half_blocks), 2 + 2 * half_blocks],
                near_outs=(2,),
                room=8,
            )
        )
        order.ran(normed_back[-1][1])

    back_all_shape = ((rows, 3 * width), low)

    def attend_back():
        back_attn = order.after([member[1] for member in normed_back])
        made["attns"] = back_attn
        [made["all"]] = call(
            functools.partial(
                attend_back_kernel, key_widths(rows, (384, 512, 640, 768)), seqs
            ),
            "attend_back",
            (seq_lengths, *back_attn, out_weight, queries, keys, values, totals),
            [back_all_shape],
            [((rows, model), low), outof, rows_width, rows_width, rows_width, totals_shape]
            + [rows_width, back_all_shape, ((rows, width), exact), ((rows, width), exact)],
            scalars=1,
            room=12,
        )
        order.ran(made["all"])

    def grad_attn():
        norm_sums = [member[2] for member in normed_back]
        up_sums = fed_back[0][half_blocks + 1] + fed_back[1][half_blocks + 1]
        small = jnp.concatenate(
            [
                jnp.zeros((1, model), jnp.float32),
                up_sums[0].reshape(-1, model),
                (norm_sums[0] + norm_sums[1])[:3],
                second_sums[:3],
            ]
        )
        small = jnp.pad(small, ((0, -small.shape[0] % 64), (0, 0)))
        made["small"] = small.shape[0]
        first_piece = ((model // 2, 2 * width), exact)
        second_rows = (width + model // 2 + small.shape[0]) // 2
        second_piece = ((second_rows, model), exact)
        [back_all] = order.after((made["all"],))
        pieces = call(
            grad_attn_kernel,
            "grad_attn",
            (first_bits("A"), tokens_in, back_all, context, *made["attns"], small),
            [first_piece, first_piece, second_piece, second_piece],
            [((rows, model), low), back_all_shape, rows_width, ((rows, model), low)]
            + [((model, 2 * width), exact), ((2 * second_rows, model), exact)],
            near=(6,),
            scalars=1,
            room=8,
        )
        order.ran(pieces[0])
        begin("A", [pieces[at] for at in (0, 2, 1, 3)])

    def input_part():
        [back_all] = order.after((made["all"],))
        made["parts"] = call(
            input_part_kernel,
            "input_part",
            (back_all, q_weight, k_weight, v_weight),
            [(block, exact)] * blocks,
            [back_all_shape, ((model, 3 * width), low), ((rows, model), exact)],
        )
        order.ran(made["parts"][-1])

    def grad_input():
        parts = made["parts"]
        others = order.after(swapped(parts))
        [result] = call(
            functools.partial(input_kernel, blocks),
            "grad_input",
            (*parts, *others, normed_back[0][0], normed_back[1][0]),
            [((rows, model), low)],
            [((rows, model), exact), ((rows, model), exact), ((rows, model), low)],
            near=range(blocks, 2 * blocks),
        )
        order.ran(result)
        made["input"] = result

    def finish(name, shapes, moves):
        operands = ()
        for chunk in (chunks[name + "0"], chunks[name + "1"]):
            operands += order.after(chunk.inputs())
        results = place_blocks(bits, operands, shapes, moves, "place")
        order.ran(results[0])
        return results

    def halves_at(name, rows, columns, target, row_offset, column, height):
        moves = []
        for at, same in enumerate((True, False)):
            first = at_bit(height, paths[name][0], same)
            moves.append(
                (
                    2 * int(name[1]) + at,
                    rows,
                    columns,
                    target,
                    lambda ref, first=first: row_offset + first(ref),
                    column,
                )
            )
        return moves

    half = hidden // 2
    quarter = half // 2
    columns_here = model // 2
    out_half, value_half = width // 2, model // 4
    tail_start = out_half + value_half
    square = (model, width)

    def place_down():
        [made["down"]] = finish(
            "D",
            ((hidden, model),),
            halves_at("D0", (0, quarter), (0, model), 0, 0, 0, quarter)
            + halves_at("D1", (0, quarter), (0, model), 0, half, 0, quarter),
        )

    def place_up():
        [made["up"]] = finish(
            "U",
            ((model, hidden),),
            halves_at("U0", (0, columns_here), (0, half), 0, 0, 0, columns_here)
            + halves_at("U1", (0, columns_here), (0, half), 0, 0, half, columns_here),
        )

    def place_attn():
        small_half = made["small"] // 2
        made["attn"] = finish(
            "A",
            (square, square, square, (width, model), (2 * small_half, model)),
            halves_at("A0", (0, columns_here), (0, width), 0, 0, 0, columns_here)
            + halves_at("A0", (0, columns_here), (width, 2 * width), 1, 0, 0, columns_here)
            + halves_at("A1", (out_half, tail_start), (0, width), 2, 0, 0, value_half)
            + halves_at(
                "A1", (out_half, tail_start), (width, 2 * width), 2, columns_here, 0, value_half
            )
            + halves_at("A1", (0, out_half), (0, model), 3, 0, 0, out_half)
            + halves_at("A1", (tail_start, tail_start + small_half), (0, model), 4, 0, 0, small_half),
        )

    steps = {
        "FB0": feed_back_first,
        "FB1": feed_back_last,
        "LN": first_norm_back,
        "AB": attend_back,
        "GA": grad_attn,
        "IP": input_part,
        "GI": grad_input,
        "PD": place_down,
        "PU": place_up,
        "PA": place_attn,
    }
    begin("D", down_pieces)
    for name in plan:
        if name in steps:
            steps[name]()
        else:
            run(name)
    grad_q, grad_k, grad_v, grad_out, tail = made["attn"]
    up_rows = hidden // model
    return (
        layer_out,
        made["input"],
        grad_q,
        grad_k,
        grad_v,
        tail[0, :width],
        tail[0, width:],
        grad_out,
        tail[up_rows + 1],
        tail[up_rows + 2],
        tail[up_rows + 3],
        made["up"],
        tail[1 : up_rows + 1].reshape(-1),
        made["down"],
        tail[up_rows + 4],
        tail[up_rows + 5],
        tail[up_rows + 6],
    )


def solution(mesh):
    placed = (
        P("dp", None),
        P("dp", None),
        P("dp", None),
        P(None, "tensor"),
        P(None, "tensor"),
        P(None, "tensor"),
        P("tensor"),
        P("tensor"),
        P("tensor", None),
        P(),
        P(),
        P(),
        P(None, "tensor"),
        P("tensor"),
        P("tensor", None),
        P(),
        P(),
        P(),
    )
    counts = (mesh.shape["dp"], mesh.shape["tensor"])

    def on_device(*args):
        return local(*counts, *args)

    return jax.shard_map(
        on_device,
        mesh=mesh,
        in_specs=placed,
        out_specs=(
            P("dp", None),
            P("dp", None),
            P(None, "tensor"),
            P(None, "tensor"),
            P(None, "tensor"),
            P("tensor"),
            P("tensor"),
            P("tensor", None),
            P(),
            P(),
            P(),
            P(None, "tensor"),
            P("tensor"),
            P("tensor", None),
            P(),
            P(),
            P(),
        ),
        check_vma=False,
    )
```

```python
import functools

import jax
import jax.numpy as jnp
from jax import lax
from jax.experimental import pallas as pl
from jax.experimental.pallas import tpu as pltpu
from jax.sharding import PartitionSpec as P

DH = 64
LANES = 128
QUERY_BLOCK = 256
ROW_BLOCK = 256
MIB = 1 << 20

score_scale = 0.125
norm_eps = 1e-05
far_negative = -1e30
log2_e = 1.4426950408889634


def contract(left_side, right_side, left_dim, right_dim):
    return lax.dot_general(
        left_side,
        right_side,
        (((left_dim,), (right_dim,)), ((), ())),
        preferred_element_type=jnp.float32,
    )


def sequence_ends(lengths_ref, count):
    ends = []
    total = jnp.int32(0)
    for at in range(count):
        total = total + lengths_ref[0, at]
        ends.append(total)
    return ends


def key_window(ends, first_row, rows):
    last_row = first_row + QUERY_BLOCK - 1
    start = jnp.int32(0)
    stop = jnp.int32(rows)
    for end in ends:
        start = jnp.where(end <= first_row, jnp.maximum(start, end), start)
        stop = jnp.where(end > last_row, jnp.minimum(stop, end), stop)
    start = (start // LANES) * LANES
    stop = ((stop + LANES - 1) // LANES) * LANES
    return start, stop


def window_bias(ends, first_row, key_start, width, key_axis):
    line = (1, QUERY_BLOCK) if key_axis == 0 else (QUERY_BLOCK, 1)
    whole = (width, QUERY_BLOCK) if key_axis == 0 else (QUERY_BLOCK, width)
    query_at = lax.broadcasted_iota(jnp.int32, line, 1 - key_axis) + first_row
    seq_start = jnp.zeros(line, jnp.int32)
    seq_stop = jnp.full(line, 1 << 30, jnp.int32)
    for end in ends:
        seq_start = jnp.where(query_at >= end, jnp.maximum(seq_start, end), seq_start)
        seq_stop = jnp.where(query_at < end, jnp.minimum(seq_stop, end), seq_stop)
    key_at = lax.broadcasted_iota(jnp.int32, whole, key_axis) + key_start
    seen = (key_at >= seq_start) & (key_at < seq_stop)
    bias = jnp.where(seen, 0.0, far_negative).astype(jnp.float32)
    return jnp.concatenate([bias, bias], axis=1 - key_axis)


def split_heads(block):
    lane = lax.broadcasted_iota(jnp.int32, block.shape, 1)
    wide = block.astype(jnp.float32)
    return jnp.concatenate(
        [jnp.where(lane < DH, wide, 0.0), jnp.where(lane < DH, 0.0, wide)], axis=0
    ).astype(jnp.bfloat16)


def merge_heads(stacked):
    rows = stacked.shape[0] // 2
    lane = lax.broadcasted_iota(jnp.int32, (rows, LANES), 1)
    return jnp.where(lane < DH, stacked[:rows], stacked[rows:]).astype(jnp.bfloat16)


def put_halves(moves, sent_far, kept_far, sums, mine):
    rows = sent_far.shape[0]
    for far, place in ((sent_far, 1 - mine), (kept_far, mine)):
        moves.out(sums.at[pl.ds(pl.multiple_of(place * rows, 8), rows), :], far)


def over_query_blocks(ends, rows, widths, body):
    @pl.loop(0, rows // QUERY_BLOCK)
    def _(block):
        first_row = pl.multiple_of(block * QUERY_BLOCK, QUERY_BLOCK)
        start, stop = key_window(ends, first_row, rows)
        span = stop - start
        lower = 0
        for width in widths:
            chosen = (span > lower) & (span <= width)
            key_start = pl.multiple_of(jnp.minimum(start, rows - width), LANES)
            pl.when(chosen)(functools.partial(body, block, first_row, key_start, width))
            lower = width


def row_mean(values):
    return jnp.mean(values, axis=-1, keepdims=True)


def standardize(values):
    centre = values - row_mean(values)
    rate = lax.rsqrt(row_mean(centre * centre) + norm_eps)
    return centre * rate, rate


def norm_back(upstream, unit, rate, gain):
    scaled = upstream * gain
    return rate * (scaled - row_mean(scaled) - unit * row_mean(scaled * unit))


def column_sum(member):
    return jnp.sum(member, axis=0, keepdims=True)


def row_blocks(rows):
    return [slice(at, at + ROW_BLOCK) for at in range(0, rows, ROW_BLOCK)]


class Moves:
    def __init__(self, semaphores):
        self.semaphores = semaphores
        self.used = 0
        self.outward = []

    def start(self, source, target):
        copy = pltpu.make_async_copy(source, target, self.semaphores.at[self.used])
        self.used += 1
        copy.start()
        return copy

    def out(self, source, target):
        self.outward.append(self.start(source, target))

    def finish(self):
        for copy in self.outward:
            copy.wait()


def attend_kernel(widths, seqs, *refs):
    (
        lengths_ref,
        tokens_far,
        q_weight_far,
        k_weight_far,
        v_weight_far,
        out_weight_far,
        q_bias_far,
        v_bias_far,
        queries_far,
        keys_far,
        values_far,
        context_far,
        totals_far,
        *parts_far,
        tokens_ref,
        q_weight_ref,
        k_weight_ref,
        v_weight_ref,
        out_weight_ref,
        queries_ref,
        keys_ref,
        values_ref,
        context_ref,
        total_ref,
        part_ref,
        q_bias_ref,
        v_bias_ref,
        semaphores,
    ) = refs
    rows = tokens_ref.shape[0]
    pairs = q_weight_ref.shape[1] // LANES
    moves = Moves(semaphores)
    tokens_in = moves.start(tokens_far, tokens_ref)
    biases_in = [moves.start(q_bias_far, q_bias_ref), moves.start(v_bias_far, v_bias_ref)]
    weights_in = [
        moves.start(far, near)
        for far, near in (
            (q_weight_far, q_weight_ref),
            (k_weight_far, k_weight_ref),
            (v_weight_far, v_weight_ref),
            (out_weight_far, out_weight_ref),
        )
    ]
    tokens_in.wait()
    for copy in biases_in:
        copy.wait()
    tokens = tokens_ref[...]
    for copy, weight_ref, bias, near, far in (
        (weights_in[0], q_weight_ref, q_bias_ref, queries_ref, queries_far),
        (weights_in[1], k_weight_ref, None, keys_ref, keys_far),
        (weights_in[2], v_weight_ref, v_bias_ref, values_ref, values_far),
    ):
        copy.wait()
        product = contract(tokens, weight_ref[...], 1, 0)
        if bias is not None:
            product = product + bias[...].reshape(1, -1)
        near[...] = product.astype(jnp.bfloat16)
        moves.out(near, far)
    ends = sequence_ends(lengths_ref, seqs)

    def body(block, first_row, key_start, width):
        bias = window_bias(ends, first_row, key_start, width, 1)
        for pair in range(pairs):
            lanes = slice(pair * LANES, (pair + 1) * LANES)
            both = split_heads(queries_ref[pl.ds(first_row, QUERY_BLOCK), lanes])
            keys = keys_ref[pl.ds(key_start, width), lanes]
            scores = contract(both, keys, 1, 1) * (score_scale * log2_e) + bias
            peak = jnp.max(scores, axis=1, keepdims=True)
            exponents = jnp.exp2(scores - peak)
            total = jnp.sum(exponents, axis=1, keepdims=True)
            spread = jnp.broadcast_to(peak + jnp.log2(total), (2 * QUERY_BLOCK, LANES))
            total_ref[pl.ds(block * pairs + pair, 1), :] = spread.T[0:1]
            probs = (exponents * (1.0 / total)).astype(jnp.bfloat16)
            context = contract(probs, values_ref[pl.ds(key_start, width), lanes], 1, 0)
            context_ref[pl.ds(first_row, QUERY_BLOCK), lanes] = merge_heads(context)

    over_query_blocks(ends, rows, widths, body)
    moves.out(context_ref, context_far)
    moves.out(total_ref, totals_far)
    weights_in[3].wait()
    for at, far in zip(row_blocks(rows), parts_far, strict=True):
        part_ref[at] = contract(context_ref[at], out_weight_ref[...], 1, 0)
        moves.out(part_ref.at[at], far)
    moves.finish()


def attend_back_kernel(widths, seqs, *refs):
    (
        lengths_ref,
        back_low_far,
        back_high_far,
        out_weight_far,
        queries_far,
        keys_far,
        values_far,
        totals_far,
        back_all_far,
        back_attn_ref,
        out_weight_ref,
        queries_ref,
        keys_ref,
        values_ref,
        total_ref,
        back_context_ref,
        back_all_ref,
        back_keys_ref,
        back_values_ref,
        semaphores,
    ) = refs
    rows, width_here = queries_ref.shape
    pairs = width_here // LANES
    half_rows = rows // 2
    moves = Moves(semaphores)
    early = [
        moves.start(far, near)
        for far, near in (
            (out_weight_far, out_weight_ref),
            (back_low_far, back_attn_ref.at[:half_rows]),
            (back_high_far, back_attn_ref.at[half_rows:]),
        )
    ]
    late = [
        moves.start(far, near)
        for far, near in (
            (queries_far, queries_ref),
            (keys_far, keys_ref),
            (values_far, values_ref),
            (totals_far, total_ref),
        )
    ]
    back_keys_ref[...] = jnp.zeros_like(back_keys_ref)
    back_values_ref[...] = jnp.zeros_like(back_values_ref)
    for copy in early:
        copy.wait()
    back_context_ref[...] = contract(back_attn_ref[...], out_weight_ref[...], 1, 1).astype(
        jnp.bfloat16
    )
    for copy in late:
        copy.wait()
    ends = sequence_ends(lengths_ref, seqs)

    def body(block, first_row, key_start, width):
        bias = window_bias(ends, first_row, key_start, width, 0)
        for pair in range(pairs):
            lanes = slice(pair * LANES, (pair + 1) * LANES)
            both = split_heads(queries_ref[pl.ds(first_row, QUERY_BLOCK), lanes])
            back_both = split_heads(back_context_ref[pl.ds(first_row, QUERY_BLOCK), lanes])
            keys = keys_ref[pl.ds(key_start, width), lanes]
            values = values_ref[pl.ds(key_start, width), lanes]
            scores = contract(keys, both, 1, 1) * (score_scale * log2_e) + bias
            probs = jnp.exp2(scores - total_ref[pl.ds(block * pairs + pair, 1), :])
            back_probs = contract(values, back_both, 1, 1)
            inner = jnp.sum(back_probs * probs, axis=0, keepdims=True)
            back_scores = (probs * (back_probs - inner) * score_scale).astype(jnp.bfloat16)
            back_values_ref[pl.ds(key_start, width), lanes] += contract(
                probs.astype(jnp.bfloat16), back_both, 1, 0
            )
            back_keys_ref[pl.ds(key_start, width), lanes] += contract(back_scores, both, 1, 0)
            back_queries = contract(back_scores, keys, 0, 0)
            back_all_ref[pl.ds(first_row, QUERY_BLOCK), lanes] = merge_heads(back_queries)

    over_query_blocks(ends, rows, widths, body)
    back_all_ref[:, width_here : 2 * width_here] = back_keys_ref[...].astype(jnp.bfloat16)
    back_all_ref[:, 2 * width_here :] = back_values_ref[...].astype(jnp.bfloat16)
    moves.out(back_all_ref, back_all_far)
    moves.finish()


def grad_attn_kernel(*refs):
    (
        bits_ref,
        tokens_far,
        back_all_far,
        context_far,
        back_low_far,
        back_high_far,
        small_ref,
        first_sent_far,
        first_kept_far,
        second_sent_far,
        second_kept_far,
        tokens_ref,
        back_all_ref,
        context_ref,
        back_attn_ref,
        first_pack_ref,
        second_pack_ref,
        semaphores,
    ) = refs
    rows, model = tokens_ref.shape
    width_here = context_ref.shape[1]
    half_rows = rows // 2
    moves = Moves(semaphores)
    arriving = [
        moves.start(far, near)
        for far, near in (
            (tokens_far, tokens_ref),
            (back_all_far, back_all_ref),
            (context_far, context_ref),
            (back_low_far, back_attn_ref.at[:half_rows]),
            (back_high_far, back_attn_ref.at[half_rows:]),
        )
    ]
    for copy in arriving[:2]:
        copy.wait()
    tokens = tokens_ref[...]
    first_pack_ref[...] = contract(tokens, back_all_ref[:, : 2 * width_here], 0, 0)
    put_halves(moves, first_sent_far, first_kept_far, first_pack_ref, bits_ref[0, 0])
    grad_values = contract(tokens, back_all_ref[:, 2 * width_here :], 0, 0)
    for copy in arriving[2:]:
        copy.wait()
    grad_out = contract(context_ref[...], back_attn_ref[...], 0, 0)
    out_half, value_half, small_half = width_here // 2, model // 4, small_ref.shape[0] // 2
    top = 0
    for at in range(2):
        second_pack_ref[top : top + out_half, :] = grad_out[at * out_half : (at + 1) * out_half]
        top += out_half
        for side in range(2):
            start = side * (model // 2) + at * value_half
            second_pack_ref[
                top : top + value_half, side * width_here : (side + 1) * width_here
            ] = grad_values[start : start + value_half]
        top += value_half
        second_pack_ref[top : top + small_half, :] = small_ref[
            at * small_half : (at + 1) * small_half
        ]
        if at == 0:
            for side in range(2):
                member = back_all_ref[:, 2 * side * width_here : (2 * side + 1) * width_here]
                second_pack_ref[top : top + 1, side * width_here : (side + 1) * width_here] = (
                    column_sum(member.astype(jnp.float32))
                )
        top += small_half
    put_halves(moves, second_sent_far, second_kept_far, second_pack_ref, bits_ref[0, 1])
    moves.finish()


def input_part_kernel(*refs):
    (
        back_all_far,
        q_weight_far,
        k_weight_far,
        v_weight_far,
        *parts_far,
        back_all_ref,
        weights_ref,
        part_ref,
        semaphores,
    ) = refs
    width_here = q_weight_far.shape[1]
    moves = Moves(semaphores)
    arriving = [
        moves.start(far, weights_ref.at[:, at * width_here : (at + 1) * width_here])
        for at, far in enumerate((q_weight_far, k_weight_far, v_weight_far))
    ]
    blocks = row_blocks(back_all_ref.shape[0])
    arriving += [moves.start(back_all_far.at[at], back_all_ref.at[at]) for at in blocks]
    for copy in arriving:
        copy.wait()
    for at, far in zip(blocks, parts_far, strict=True):
        part_ref[at] = contract(back_all_ref[at], weights_ref[...], 1, 1)
        moves.out(part_ref.at[at], far)
    moves.finish()


def feed_kernel(first_row, *refs):
    (
        tokens_far,
        *own_fars,
        out_bias_ref,
        gain_ref,
        shift_ref,
        up_weight_ref,
        up_bias_ref,
        down_weight_far,
        first_sum_far,
        first_low_far,
        active_far,
        part_low_far,
        part_high_far,
        tokens_ref,
        own_ref,
        first_sum_ref,
        first_low_ref,
        active_ref,
        part_ref,
        down_weight_ref,
        semaphores,
    ) = refs
    rows = own_ref.shape[0]
    own_fars, other_refs = own_fars[: len(own_fars) // 2], own_fars[len(own_fars) // 2 :]
    moves = Moves(semaphores)
    arriving = []
    for at, own_far in zip(row_blocks(rows), own_fars, strict=True):
        there = slice(first_row + at.start, first_row + at.stop)
        arriving.append(
            (
                moves.start(own_far, own_ref.at[at]),
                moves.start(tokens_far.at[there], tokens_ref.at[at]),
            )
        )
        if at.start == 0:
            down_in = moves.start(down_weight_far, down_weight_ref)
    for at, copies, other_ref, part_far in zip(
        row_blocks(rows), arriving, other_refs, (part_low_far, part_high_far), strict=True
    ):
        for copy in copies:
            copy.wait()
        first_sum = (
            tokens_ref[at].astype(jnp.float32)
            + (own_ref[at] + other_ref[...])
            + out_bias_ref[...].reshape(1, -1)
        )
        first_sum_ref[at] = first_sum
        moves.out(first_sum_ref.at[at], first_sum_far.at[at])
        unit, unused = standardize(first_sum)
        first_low = (
            unit * gain_ref[...].reshape(1, -1) + shift_ref[...].reshape(1, -1)
        ).astype(jnp.bfloat16)
        first_low_ref[at] = first_low
        moves.out(first_low_ref.at[at], first_low_far.at[at])
        inner = contract(first_low, up_weight_ref[...], 1, 0) + up_bias_ref[...].reshape(1, -1)
        active = (inner * (0.5 * (1.0 + lax.erf(inner * 0.7071067811865476)))).astype(
            jnp.bfloat16
        )
        active_ref[at] = active
        moves.out(active_ref.at[at], active_far.at[at])
        if at.start == 0:
            down_in.wait()
        part_ref[at] = contract(active, down_weight_ref[...], 1, 0)
        moves.out(part_ref.at[at], part_far)
    moves.finish()


def second_norm_kernel(first_row, last, *refs):
    refs = list(refs)
    if last:
        bits_ref, active_low_far, active_high_far, back_low_far, layer_before_far = refs[:5]
        del refs[:5]
    (
        first_sum_far,
        own_low_far,
        own_high_far,
        *other_refs,
        cotangent_far,
        first_gain_ref,
        first_shift_ref,
        down_bias_ref,
        gain_ref,
        shift_ref,
    ) = refs[:11]
    layer_far, back_second_far, back_down_far, sums_ref = refs[11:15]
    rest = refs[15:]
    if last:
        grads_far, rest = rest[:4], rest[4:]
    first_sum_ref, own_ref, cotangent_ref, layer_ref, back_second_ref, back_down_ref, *rest = rest
    semaphores = rest[-1]
    rows = own_ref.shape[0]
    moves = Moves(semaphores)
    arriving = []
    for at, own_far in zip(row_blocks(rows), (own_low_far, own_high_far), strict=True):
        there = slice(first_row + at.start, first_row + at.stop)
        arriving.append(
            (
                moves.start(own_far, own_ref.at[at]),
                moves.start(first_sum_far.at[at], first_sum_ref.at[at]),
                moves.start(cotangent_far.at[there], cotangent_ref.at[at]),
            )
        )
    if last:
        active_ref, back_before_ref, grads_ref, unused = rest
        early = [
            moves.start(active_low_far, active_ref.at[:rows]),
            moves.start(back_low_far, back_before_ref),
        ]
        late = moves.start(active_high_far, active_ref.at[rows:])
    bias_sum, gain_sum, shift_sum = 0.0, 0.0, 0.0
    gain = gain_ref[...].reshape(1, -1)
    shift = shift_ref[...].reshape(1, -1)
    for at, copies, other_ref in zip(row_blocks(rows), arriving, other_refs, strict=True):
        for copy in copies:
            copy.wait()
        unit, unused = standardize(first_sum_ref[at])
        first = unit * first_gain_ref[...].reshape(1, -1) + first_shift_ref[...].reshape(1, -1)
        second_sum = first + (own_ref[at] + other_ref[...]) + down_bias_ref[...].reshape(1, -1)
        unit, rate = standardize(second_sum)
        layer_ref[at] = (unit * gain + shift).astype(jnp.bfloat16)
        there = slice(first_row + at.start, first_row + at.stop)
        moves.out(layer_ref.at[at], layer_far.at[there])
        upstream = cotangent_ref[at].astype(jnp.float32)
        back_second = norm_back(upstream, unit, rate, gain)
        back_second_ref[at] = back_second
        moves.out(back_second_ref.at[at], back_second_far.at[at])
        back_down_ref[at] = back_second.astype(jnp.bfloat16)
        moves.out(back_down_ref.at[at], back_down_far.at[at])
        bias_sum += column_sum(back_second)
        gain_sum += column_sum(upstream * unit)
        shift_sum += column_sum(upstream)
    put_sums(sums_ref, bias_sum, gain_sum, shift_sum)
    if last:
        for copy in early:
            copy.wait()
        late.wait()
        height = grads_ref.shape[1]
        for slot, (block, same) in enumerate(((0, False), (1, False), (0, True), (1, True))):
            mine = bits_ref[0, block]
            place = mine if same else 1 - mine
            units = pl.ds(pl.multiple_of((2 * block + place) * height, LANES), height)
            grads_ref[slot] = contract(
                active_ref[:rows, units], back_before_ref[...], 0, 0
            ) + contract(active_ref[rows:, units], back_down_ref[...], 0, 0)
            moves.out(grads_ref.at[slot], grads_far[slot])
    moves.finish()


def put_sums(sums_ref, *members):
    sums_ref[...] = jnp.zeros_like(sums_ref)
    for at, member in enumerate(members):
        sums_ref[at : at + 1, :] = member


def feed_back_kernel(last, *refs):
    refs = list(refs)
    if last:
        bits_ref, first_before_far, inner_before_far = refs[:3]
        del refs[:3]
    (
        back_down_far,
        first_low_far,
        up_weight_ref,
        up_bias_ref,
        down_weight_ref,
        part_low_far,
        part_high_far,
        inner_far,
        sums_ref,
        *rest,
    ) = refs
    if last:
        grads_far, rest = rest[:4], rest[4:]
    back_down_ref, first_low_ref, part_ref, inner_ref, *rest = rest
    semaphores = rest[-1]
    rows = back_down_ref.shape[0]
    moves = Moves(semaphores)
    arriving = [
        (
            moves.start(first_low_far.at[at], first_low_ref.at[at]),
            moves.start(back_down_far.at[at], back_down_ref.at[at]),
        )
        for at in row_blocks(rows)
    ]
    if last:
        first_before_ref, inner_before_ref, grads_ref, unused = rest
        late = [
            moves.start(first_before_far, first_before_ref),
            moves.start(inner_before_far, inner_before_ref),
        ]
    total = 0.0
    for at, copies, part_far in zip(
        row_blocks(rows), arriving, (part_low_far, part_high_far), strict=True
    ):
        for copy in copies:
            copy.wait()
        inner = contract(first_low_ref[at], up_weight_ref[...], 1, 0) + up_bias_ref[...].reshape(
            1, -1
        )
        slope = 0.5 * (1.0 + lax.erf(inner * 0.7071067811865476)) + inner * (
            0.3989422804014327 * jnp.exp(-0.5 * inner * inner)
        )
        back_active = contract(back_down_ref[at], down_weight_ref[...], 1, 1)
        back_inner = (back_active * slope).astype(jnp.bfloat16)
        inner_ref[at] = back_inner
        if not last:
            moves.out(inner_ref.at[at], inner_far.at[at])
        part_ref[at] = contract(back_inner, up_weight_ref[...], 1, 1)
        moves.out(part_ref.at[at], part_far)
        total += column_sum(back_inner.astype(jnp.float32))
    put_sums(sums_ref, total)
    if last:
        moves.out(inner_ref.at[:16], inner_far)
        for copy in late:
            copy.wait()
        height, columns = grads_ref.shape[1:]
        for slot, (block, same) in enumerate(((0, False), (1, False), (0, True), (1, True))):
            mine = bits_ref[0, block]
            place = mine if same else 1 - mine
            features = pl.ds(pl.multiple_of(place * height, LANES), height)
            units = slice(block * columns, (block + 1) * columns)
            grads_ref[slot] = contract(
                first_before_ref[:, features], inner_before_ref[:, units], 0, 0
            ) + contract(first_low_ref[:, features], inner_ref[:, units], 0, 0)
            moves.out(grads_ref.at[slot], grads_far[slot])
    moves.finish()


def first_norm_kernel(*refs):
    (
        first_sum_far,
        own_low_far,
        own_high_far,
        *other_refs,
        back_second_far,
        gain_ref,
        back_first_far,
        back_attn_far,
        sums_ref,
        first_sum_ref,
        own_ref,
        back_second_ref,
        back_first_ref,
        back_attn_ref,
        semaphores,
    ) = refs
    rows = own_ref.shape[0]
    moves = Moves(semaphores)
    arriving = [
        (
            moves.start(own_far, own_ref.at[at]),
            moves.start(first_sum_far.at[at], first_sum_ref.at[at]),
            moves.start(back_second_far.at[at], back_second_ref.at[at]),
        )
        for at, own_far in zip(row_blocks(rows), (own_low_far, own_high_far), strict=True)
    ]
    bias_sum, gain_sum, shift_sum = 0.0, 0.0, 0.0
    gain = gain_ref[...].reshape(1, -1)
    for at, copies, other_ref in zip(row_blocks(rows), arriving, other_refs, strict=True):
        for copy in copies:
            copy.wait()
        unit, rate = standardize(first_sum_ref[at])
        upstream = (own_ref[at] + other_ref[...]) + back_second_ref[at]
        back_first_sum = norm_back(upstream, unit, rate, gain)
        back_first_ref[at] = back_first_sum
        moves.out(back_first_ref.at[at], back_first_far.at[at])
        back_attn_ref[at] = back_first_sum.astype(jnp.bfloat16)
        moves.out(back_attn_ref.at[at], back_attn_far.at[at])
        bias_sum += column_sum(back_first_sum)
        gain_sum += column_sum(upstream * unit)
        shift_sum += column_sum(upstream)
    put_sums(sums_ref, bias_sum, gain_sum, shift_sum)
    moves.finish()


def input_kernel(blocks, *refs):
    own_fars, other_refs = refs[:blocks], refs[blocks : 2 * blocks]
    *first_fars, grad_far, own_ref, first_ref, grad_ref, semaphores = refs[2 * blocks :]
    rows = own_ref.shape[0]
    moves = Moves(semaphores)
    arriving = []
    per = blocks // len(first_fars)
    for block, (at, own_far) in enumerate(zip(row_blocks(rows), own_fars, strict=True)):
        inside = slice(block % per * ROW_BLOCK, (block % per + 1) * ROW_BLOCK)
        arriving.append(
            (
                moves.start(own_far, own_ref.at[at]),
                moves.start(first_fars[block // per].at[inside], first_ref.at[at]),
            )
        )
    for at, copies, other_ref in zip(row_blocks(rows), arriving, other_refs, strict=True):
        for copy in copies:
            copy.wait()
        grad_ref[at] = ((own_ref[at] + other_ref[...]) + first_ref[at]).astype(jnp.bfloat16)
        moves.out(grad_ref.at[at], grad_far.at[at])
    moves.finish()


def struct(shape, dtype):
    return jax.ShapeDtypeStruct(shape, dtype)


def in_smem():
    return pl.BlockSpec(memory_space=pltpu.SMEM)


def in_vmem():
    return pl.BlockSpec(memory_space=pltpu.VMEM)


def in_hbm():
    return pl.BlockSpec(memory_space=pltpu.HBM)


def key_widths(rows, steps=(512, 768)):
    return tuple(width for width in steps if width < rows) + (rows,)


def call(body, name, operands, outs, scratch=(), near=(), near_outs=(), scalars=0, room=4, aliases=None):
    bytes_here = sum(
        jnp.dtype(dtype).itemsize * functools.reduce(lambda a, b: a * b, shape) for shape, dtype in scratch
    )
    specs = [
        in_smem() if at < scalars else in_vmem() if at in near else in_hbm()
        for at in range(len(operands))
    ]
    return pl.pallas_call(
        body,
        out_shape=tuple(
            struct(*out) if at in near_outs else pltpu.HBM(*out) for at, out in enumerate(outs)
        ),
        in_specs=specs,
        out_specs=tuple(in_vmem() if at in near_outs else in_hbm() for at in range(len(outs))),
        scratch_shapes=[pltpu.VMEM(*shape) for shape in scratch]
        + [pltpu.SemaphoreType.DMA((48,))],
        input_output_aliases=aliases or {},
        compiler_params=pltpu.CompilerParams(vmem_limit_bytes=bytes_here + room * MIB),
        name=name,
    )(
        *(
            operand
            if at < scalars or at in near
            else pltpu.with_memory_space_constraint(operand, pltpu.HBM)
            for at, operand in enumerate(operands)
        )
    )


low, exact = jnp.bfloat16, jnp.float32


def place_kernel(moves, starts_ref, *refs):
    copies = []
    inputs = 1 + max(source for source, *unused in moves)
    for at, (source, rows, columns, target, row_start, column_start) in enumerate(moves):
        start = row_start(starts_ref) if callable(row_start) else row_start
        size = rows[1] - rows[0]
        copies.append(
            pltpu.make_async_copy(
                refs[source].at[pl.ds(rows[0], size), pl.ds(columns[0], columns[1] - columns[0])],
                refs[inputs + target].at[
                    pl.ds(pl.multiple_of(start, 8), size),
                    pl.ds(column_start, columns[1] - columns[0]),
                ],
                refs[-1].at[at],
            )
        )
    for copy in copies:
        copy.start()
    for copy in copies:
        copy.wait()


def place_blocks(starts, operands, shapes, moves, name):
    anywhere = pl.BlockSpec(memory_space=pl.ANY)
    return pl.pallas_call(
        functools.partial(place_kernel, moves),
        out_shape=tuple(struct(shape, jnp.float32) for shape in shapes),
        in_specs=[in_smem()] + [in_vmem()] * len(operands),
        out_specs=(anywhere,) * len(shapes),
        scratch_shapes=[pltpu.SemaphoreType.DMA((len(moves),))],
        compiler_params=pltpu.CompilerParams(vmem_limit_bytes=4 * MIB),
        name=name,
    )(starts, *operands)


def at_bit(rows, bit, same):
    def first(bits_ref):
        return (bits_ref[0, bit] if same else 1 - bits_ref[0, bit]) * rows

    return first


def swap_cores(value, tensor_count):
    return lax.ppermute(value, "tensor", [(i, i ^ 1) for i in range(tensor_count)])


class Ring:
    def __init__(self, count, place):
        self.count = count
        self.place = place
        top = count.bit_length() - 1
        self.bits = (0, 1, top - 2, top - 1)
        self.between = range(2, top - 2)

    def swap(self, value, bit):
        return lax.ppermute(value, "dp", [(i, i ^ (1 << bit)) for i in range(self.count)])

    def mine(self, name):
        return (self.place >> self.bits[name]) & 1

    def half(self, value, name, same):
        rows = value.shape[0] // 2
        mine = self.mine(name)
        return lax.dynamic_slice_in_dim(value, (mine if same else 1 - mine) * rows, rows, 0)


class Chunk:
    def __init__(self, ring, bits, path, sent, kept):
        self.ring = ring
        self.bits = bits
        *self.path, self.middle = path
        self.held = (kept,)
        self.arriving = None
        self.sent = sent
        self.step = 0

    def inputs(self):
        return self.held + (() if self.arriving is None else (self.arriving,))

    def swap(self, value, name):
        self.arriving = self.ring.swap(value, self.ring.bits[name])

    def join(self, value, arriving, name):
        rows, columns = value.shape
        [joined] = place_blocks(
            self.bits,
            (value, arriving),
            ((2 * rows, columns),),
            (
                (0, (0, rows), (0, columns), 0, at_bit(rows, name, True), 0),
                (1, (0, rows), (0, columns), 0, at_bit(rows, name, False), 0),
            ),
            "join",
        )
        return joined

    def advance(self, inputs):
        ring = self.ring
        step = self.step
        depth = len(self.path)
        self.step += 1
        if step == 0:
            self.swap(self.sent, self.path[0])
            return None
        if step < depth:
            name = self.path[step]
            sent = functools.reduce(jnp.add, [ring.half(member, name, False) for member in inputs])
            self.held = tuple(ring.half(member, name, True) for member in inputs)
            self.swap(sent, name)
            return sent
        if step == depth:
            value = functools.reduce(jnp.add, inputs)
            for bit in ring.between:
                value = value + ring.swap(value, bit)
            self.swap(value, self.middle)
        else:
            value, arrived = inputs
            back = 2 * depth - step
            if back == depth - 1:
                value = value + arrived
            else:
                value = self.join(value, arrived, self.path[back + 1])
            self.swap(value, self.path[back])
        self.held = (value,)
        return value


class Sequence:
    def __init__(self):
        self.last = None

    def after(self, values):
        if self.last is None:
            return tuple(values)
        held = lax.optimization_barrier((*values, self.last))
        return held[:-1]

    def ran(self, result):
        if result is not None:
            self.last = result


paths = {
    "D0": (0, 1, 2, 3),
    "D1": (1, 2, 0, 3),
    "U0": (0, 1, 2, 3),
    "U1": (1, 2, 0, 3),
    "A0": (0, 1, 2, 3),
    "A1": (1, 0, 2, 3),
}

plan = (
    "D0", "FB0", "D1", "FB1", "LN", "U0", "D1", "D0", "LN", "AB", "U1", "D1", "D0", "U0", "GA",
    "A1", "D0", "U1", "A0", "U0", "D0", "D1", "U1", "D1", "U0", "U1", "A0", "D0", "D1", "A1", "U0",
    "A0", "U1", "D0", "A1", "D1", "U0", "U1", "A0", "A1", "U1", "U0", "A1", "PD", "A0", "IP", "A0",
    "A1", "PU", "A0", "A1", "GI", "PA",
)


def local(
    dp_count,
    tensor_count,
    tokens_in,
    cotangent,
    seq_lengths,
    q_weight,
    k_weight,
    v_weight,
    q_bias,
    v_bias,
    out_weight,
    out_bias,
    first_gain,
    first_shift,
    up_weight,
    up_bias,
    down_weight,
    down_bias,
    second_gain,
    second_shift,
):
    place = lax.axis_index("dp")
    ring = Ring(dp_count, place)
    bits = jnp.stack([ring.mine(name) for name in range(4)]).reshape(1, 4)

    def first_bits(name):
        return jnp.stack([ring.mine(paths[name + at][0]) for at in "01"]).reshape(1, 2)

    model = q_weight.shape[0]
    width = q_weight.shape[1]
    hidden = up_weight.shape[1]
    rows = tokens_in.shape[0]
    half_rows = rows // 2
    block = (ROW_BLOCK, model)
    blocks = rows // ROW_BLOCK
    half_blocks = blocks // 2
    half_exact = ((half_rows, model), exact)
    half_low = ((half_rows, model), low)
    half_active = ((half_rows, hidden), low)
    rows_width = ((rows, width), low)
    into = ((model, width), low)
    outof = ((width, model), low)
    seqs = seq_lengths.shape[1]
    widths = key_widths(rows)
    totals_shape = ((rows // QUERY_BLOCK * (width // LANES), 2 * QUERY_BLOCK), exact)
    queries, keys, values, context, totals, *attn_parts = call(
        functools.partial(attend_kernel, widths, seqs),
        "attend",
        (seq_lengths, tokens_in, q_weight, k_weight, v_weight, out_weight, q_bias, v_bias),
        [rows_width] * 4 + [totals_shape] + [(block, exact)] * blocks,
        [((rows, model), low), into, into, into, outof]
        + [rows_width] * 4
        + [totals_shape, ((rows, model), exact)]
        + [((width,), exact)] * 2,
        scalars=1,
        room=8,
    )
    order = Sequence()

    def swapped(parts):
        return tuple(swap_cores(part, tensor_count) for part in parts)

    attn_others = swapped(attn_parts)
    fed = []
    for at in range(2):
        mine = slice(at * half_blocks, (at + 1) * half_blocks)
        fed.append(
            call(
                functools.partial(feed_kernel, at * half_rows),
                "feed",
                (tokens_in, *attn_parts[mine], *attn_others[mine])
                + (out_bias, first_gain, first_shift, up_weight, up_bias, down_weight),
                [half_exact, half_low, half_active] + [(block, exact)] * half_blocks,
                [half_low, half_exact, half_exact, half_low, half_active, half_exact]
                + [((hidden, model), low)],
                near=range(1 + half_blocks, 1 + 2 * half_blocks + 5),
            )
        )
    first_sums, first_lows, actives = zip(*[member[:3] for member in fed], strict=True)
    down_parts = [member[3:] for member in fed]
    down_others = [swapped(parts) for parts in down_parts]
    second_vectors = (first_gain, first_shift, down_bias, second_gain, second_shift)
    sums_shape = ((8, model), exact)

    def second_norm(at, before, scratch, extra_outs):
        lead = len(before)
        return call(
            functools.partial(second_norm_kernel, at * half_rows, at == 1),
            "second_norm",
            (*before, first_sums[at], *down_parts[at], *down_others[at], cotangent)
            + second_vectors,
            [((rows, model), low), half_exact, half_low, sums_shape] + extra_outs,
            [half_exact, half_exact, half_low, half_low, half_exact, half_low] + scratch,
            near=[*range(lead + 1 + half_blocks, lead + 1 + 2 * half_blocks)]
            + [*range(lead + 2 + 2 * half_blocks, lead + 7 + 2 * half_blocks)],
            near_outs=(3,),
            scalars=1 if before else 0,
            room=8,
            aliases={4: 0} if before else None,
        )

    layer_out, back_second, back_down, second_sums = second_norm(0, (), [], [])
    down_piece = (hidden // 4, model)
    layer_out, *rest = second_norm(
        1,
        (first_bits("D"), *actives, back_down, layer_out),
        [((rows, hidden), low), half_low, ((4, *down_piece), exact)],
        [(down_piece, exact)] * 4,
    )
    back_seconds, back_downs = (back_second, rest[0]), (back_down, rest[1])
    second_sums = second_sums + rest[2]
    down_pieces = rest[3:]
    order.ran(down_pieces[0])
    chunks = {}

    def begin(name, pieces):
        chunks[name + "0"] = Chunk(ring, bits, paths[name + "0"], pieces[0], pieces[2])
        chunks[name + "1"] = Chunk(ring, bits, paths[name + "1"], pieces[1], pieces[3])

    def run(*names):
        for name in names:
            chunk = chunks[name]
            inputs = chunk.inputs()
            order.ran(chunk.advance(order.after(inputs) if chunk.step else inputs))

    up_piece = (model // 2, hidden // 2)
    fed_back = []
    normed_back = []
    made = {}

    def feed_back(at, before, inner_rows, scratch, extra_outs):
        [back_down] = order.after((back_downs[at],))
        lead = len(before)
        results = call(
            functools.partial(feed_back_kernel, at == 1),
            "feed_back",
            (*before, back_down, first_lows[at], up_weight, up_bias, down_weight),
            [(block, exact)] * half_blocks
            + [((inner_rows, hidden), low), ((8, hidden), exact)]
            + extra_outs,
            [half_low, half_low, half_exact, half_active] + scratch,
            near=range(lead + 2, lead + 5),
            near_outs=(half_blocks + 1,),
            scalars=1 if before else 0,
            room=6,
        )
        order.ran(results[half_blocks])
        fed_back.append(results)

    def feed_back_first():
        feed_back(0, (), half_rows, [], [])

    def feed_back_last():
        feed_back(
            1,
            (first_bits("U"), first_lows[0], fed_back[0][half_blocks]),
            16,
            [half_low, half_active, ((4, *up_piece), exact)],
            [(up_piece, exact)] * 4,
        )
        begin("U", fed_back[1][half_blocks + 2 :])

    def first_norm_back():
        at = len(normed_back)
        parts = fed_back[at][:half_blocks]
        others = order.after(swapped(parts))
        normed_back.append(
            call(
                first_norm_kernel,
                "first_norm_back",
                (first_sums[at], *parts, *others, back_seconds[at], first_gain),
                [half_exact, half_low, sums_shape],
                [half_exact, half_exact, half_exact, half_exact, half_low],
                near=[*range(1 + half_blocks, 1 + 2 * half_blocks), 2 + 2 * half_blocks],
                near_outs=(2,),
                room=8,
            )
        )
        order.ran(normed_back[-1][1])

    back_all_shape = ((rows, 3 * width), low)

    def attend_back():
        back_attn = order.after([member[1] for member in normed_back])
        made["attns"] = back_attn
        [made["all"]] = call(
            functools.partial(
                attend_back_kernel, key_widths(rows, (384, 512, 640, 768, 896)), seqs
            ),
            "attend_back",
            (seq_lengths, *back_attn, out_weight, queries, keys, values, totals),
            [back_all_shape],
            [((rows, model), low), outof, rows_width, rows_width, rows_width, totals_shape]
            + [rows_width, back_all_shape, ((rows, width), exact), ((rows, width), exact)],
            scalars=1,
            room=12,
        )
        order.ran(made["all"])

    def grad_attn():
        norm_sums = [member[2] for member in normed_back]
        up_sums = fed_back[0][half_blocks + 1] + fed_back[1][half_blocks + 1]
        small = jnp.concatenate(
            [
                jnp.zeros((1, model), jnp.float32),
                up_sums[0].reshape(-1, model),
                (norm_sums[0] + norm_sums[1])[:3],
                second_sums[:3],
            ]
        )
        small = jnp.pad(small, ((0, -small.shape[0] % 64), (0, 0)))
        made["small"] = small.shape[0]
        first_piece = ((model // 2, 2 * width), exact)
        second_rows = (width + model // 2 + small.shape[0]) // 2
        second_piece = ((second_rows, model), exact)
        [back_all] = order.after((made["all"],))
        pieces = call(
            grad_attn_kernel,
            "grad_attn",
            (first_bits("A"), tokens_in, back_all, context, *made["attns"], small),
            [first_piece, first_piece, second_piece, second_piece],
            [((rows, model), low), back_all_shape, rows_width, ((rows, model), low)]
            + [((model, 2 * width), exact), ((2 * second_rows, model), exact)],
            near=(6,),
            scalars=1,
            room=8,
        )
        order.ran(pieces[0])
        begin("A", [pieces[at] for at in (0, 2, 1, 3)])

    def input_part():
        [back_all] = order.after((made["all"],))
        made["parts"] = call(
            input_part_kernel,
            "input_part",
            (back_all, q_weight, k_weight, v_weight),
            [(block, exact)] * blocks,
            [back_all_shape, ((model, 3 * width), low), ((rows, model), exact)],
        )
        order.ran(made["parts"][-1])

    def grad_input():
        parts = made["parts"]
        others = order.after(swapped(parts))
        [result] = call(
            functools.partial(input_kernel, blocks),
            "grad_input",
            (*parts, *others, normed_back[0][0], normed_back[1][0]),
            [((rows, model), low)],
            [((rows, model), exact), ((rows, model), exact), ((rows, model), low)],
            near=range(blocks, 2 * blocks),
        )
        order.ran(result)
        made["input"] = result

    def finish(name, shapes, moves):
        operands = ()
        for chunk in (chunks[name + "0"], chunks[name + "1"]):
            operands += order.after(chunk.inputs())
        results = place_blocks(bits, operands, shapes, moves, "place")
        order.ran(results[0])
        return results

    def halves_at(name, rows, columns, target, row_offset, column, height):
        moves = []
        for at, same in enumerate((True, False)):
            first = at_bit(height, paths[name][0], same)
            moves.append(
                (
                    2 * int(name[1]) + at,
                    rows,
                    columns,
                    target,
                    lambda ref, first=first: row_offset + first(ref),
                    column,
                )
            )
        return moves

    half = hidden // 2
    quarter = half // 2
    columns_here = model // 2
    out_half, value_half = width // 2, model // 4
    tail_start = out_half + value_half
    square = (model, width)

    def place_down():
        [made["down"]] = finish(
            "D",
            ((hidden, model),),
            halves_at("D0", (0, quarter), (0, model), 0, 0, 0, quarter)
            + halves_at("D1", (0, quarter), (0, model), 0, half, 0, quarter),
        )

    def place_up():
        [made["up"]] = finish(
            "U",
            ((model, hidden),),
            halves_at("U0", (0, columns_here), (0, half), 0, 0, 0, columns_here)
            + halves_at("U1", (0, columns_here), (0, half), 0, 0, half, columns_here),
        )

    def place_attn():
        small_half = made["small"] // 2
        made["attn"] = finish(
            "A",
            (square, square, square, (width, model), (2 * small_half, model)),
            halves_at("A0", (0, columns_here), (0, width), 0, 0, 0, columns_here)
            + halves_at("A0", (0, columns_here), (width, 2 * width), 1, 0, 0, columns_here)
            + halves_at("A1", (out_half, tail_start), (0, width), 2, 0, 0, value_half)
            + halves_at(
                "A1", (out_half, tail_start), (width, 2 * width), 2, columns_here, 0, value_half
            )
            + halves_at("A1", (0, out_half), (0, model), 3, 0, 0, out_half)
            + halves_at("A1", (tail_start, tail_start + small_half), (0, model), 4, 0, 0, small_half),
        )

    steps = {
        "FB0": feed_back_first,
        "FB1": feed_back_last,
        "LN": first_norm_back,
        "AB": attend_back,
        "GA": grad_attn,
        "IP": input_part,
        "GI": grad_input,
        "PD": place_down,
        "PU": place_up,
        "PA": place_attn,
    }
    begin("D", down_pieces)
    for name in plan:
        if name in steps:
            steps[name]()
        else:
            run(name)
    grad_q, grad_k, grad_v, grad_out, tail = made["attn"]
    up_rows = hidden // model
    return (
        layer_out,
        made["input"],
        grad_q,
        grad_k,
        grad_v,
        tail[0, :width],
        tail[0, width:],
        grad_out,
        tail[up_rows + 1],
        tail[up_rows + 2],
        tail[up_rows + 3],
        made["up"],
        tail[1 : up_rows + 1].reshape(-1),
        made["down"],
        tail[up_rows + 4],
        tail[up_rows + 5],
        tail[up_rows + 6],
    )


def solution(mesh):
    placed = (
        P("dp", None),
        P("dp", None),
        P("dp", None),
        P(None, "tensor"),
        P(None, "tensor"),
        P(None, "tensor"),
        P("tensor"),
        P("tensor"),
        P("tensor", None),
        P(),
        P(),
        P(),
        P(None, "tensor"),
        P("tensor"),
        P("tensor", None),
        P(),
        P(),
        P(),
    )
    counts = (mesh.shape["dp"], mesh.shape["tensor"])

    def on_device(*args):
        return local(*counts, *args)

    return jax.shard_map(
        on_device,
        mesh=mesh,
        in_specs=placed,
        out_specs=(
            P("dp", None),
            P("dp", None),
            P(None, "tensor"),
            P(None, "tensor"),
            P(None, "tensor"),
            P("tensor"),
            P("tensor"),
            P("tensor", None),
            P(),
            P(),
            P(),
            P(None, "tensor"),
            P("tensor"),
            P("tensor", None),
            P(),
            P(),
            P(),
        ),
        check_vma=False,
    )
```
